32 devices in a mesh: px: 8 (over y, x, core), py: 4 (over z).
Axes of the slice: x: 2, y: 2, z: 4, core: 2. Of those that a mesh axis runs over, the one named last changes fastest.
Arguments:
- trial_block: float32 [8, 4, 2, 8, 8192], P('px', 'py'), may hold values from -12 to 12
- stiff_coef: float32 [8, 4, 1024], P('px', 'py'), may hold values from 0.3 to 3
- mass_coef: float32 [8, 4, 1024], P('px', 'py'), may hold values from 1 to 12
- elem_count: int32 [8, 4], P('px', 'py'), may hold values from 256 to 1024, as said below
- elem_dofs: int32 [8, 4, 1024, 20], P('px', 'py'), may hold values from 0 to 12287, as said below
- pairing: int32 [2048], replicated, may hold values from 0 to 2047, each once
- bloch_fraction: int32 [2], replicated, may hold values from 1 to 16, as said below
- stiff_ref: float32 [20, 20], replicated, may hold values from -16 to 17, as said below
- mass_ref: float32 [20, 20], replicated, may hold values from -16 to 17, as said below
Outputs:
- curl_image: float32 [8, 4, 2, 8, 8192], P('px', 'py')
- mass_image: float32 [8, 4, 2, 8, 8192], P('px', 'py')
- gram: float32 [2, 2, 8, 8], replicated
The draws below stay inside these ranges and needn't reach their ends.
Inputs may be any that keep to these rules, and one draw needn't show every extreme that they name: `elem_count`: element slots below 128 are the only ones that name indices of 8192 or more; each part's count is at least 256, and each part of a 2-by-2 block of parts has exactly 1024 in every draw. `elem_dofs`: indices into the extended layout; slots at or above 128 name only indices below 8192. bloch_fraction[1] is 16 and 0 < bloch_fraction[0] < bloch_fraction[1]. `stiff_ref`: symmetric positive definite. `mass_ref`: symmetric positive definite.
All inputs are finite; a program needn't handle non-finite values.
Results may differ from the reference program's by a relative error of at most 0.0003.
Values sent between devices are 32-bit elements; how exact they have to be, the bound alone decides.
No kernel may reach another device: no remote copies, remote signals or barrier semaphores. Data moves between devices by JAX's collectives and lax.ppermute only.
A program may use at most 64 MiB of HBM per device.

```python
import math
import jax
import jax.numpy as jnp
from jax import lax

NVEC = 8
NLOC = 20
INTERIOR = 4096
FACE = 2048
ELEM_CAP = 1024
OWNED = 8192
EXTENDED = 12288
N_PX = 8
N_PY = 4


def draw_trial_block(key, part):
    shape = (N_PX, N_PY, 2, NVEC, OWNED)
    row_pos = jnp.arange(N_PX, dtype=jnp.float32).reshape(N_PX, 1, 1, 1, 1) / max(N_PX - 1, 1)
    scale = 1.0 + 2.0 * row_pos
    values = jax.random.truncated_normal(key, -4.0, 4.0, shape, jnp.float32) * scale
    return values


def draw_elem_count(key, part):
    base_key = jax.random.fold_in(key, 21)
    row_key = jax.random.fold_in(key, 22)
    col_key = jax.random.fold_in(key, 23)
    base = jax.random.randint(base_key, (N_PX, N_PY), ELEM_CAP // 4, ELEM_CAP // 2 + 1)
    row_start = jax.random.randint(row_key, (), 0, N_PX)
    col_start = jax.random.randint(col_key, (), 0, N_PY - 1)
    row_ids = jnp.arange(N_PX, dtype=jnp.int32).reshape(N_PX, 1)
    col_ids = jnp.arange(N_PY, dtype=jnp.int32).reshape(1, N_PY)
    in_rows = (row_ids == row_start) | (row_ids == (row_start + 1) % N_PX)
    in_cols = (col_ids == col_start) | (col_ids == col_start + 1)
    return jnp.where(in_rows & in_cols, ELEM_CAP, base).astype(jnp.int32)


def draw_elem_dofs(key, part):
    shape = (N_PX, N_PY, ELEM_CAP, NLOC)
    owned_pick = jax.random.randint(jax.random.fold_in(key, 31), shape, 0, OWNED)
    face_pick = jax.random.randint(jax.random.fold_in(key, 32), shape, OWNED, EXTENDED)
    slot_ids = jnp.arange(ELEM_CAP, dtype=jnp.int32).reshape(1, 1, ELEM_CAP, 1)
    local_ids = jnp.arange(NLOC, dtype=jnp.int32).reshape(1, 1, 1, NLOC)
    use_face = (slot_ids < ELEM_CAP // 8) & (local_ids < 8)
    return jnp.where(use_face, face_pick, owned_pick).astype(jnp.int32)


def draw_bloch_fraction(key, part):
    denominator = jnp.full((), 16, jnp.int32)
    numerator = jax.random.randint(jax.random.fold_in(key, 42), (), 1, 16)
    return jnp.stack([numerator, denominator]).astype(jnp.int32)


def symmetric_matrix(key, diag_shift):
    shape = (NLOC, NLOC)
    factor = jax.random.truncated_normal(key, -4.0, 4.0, shape, jnp.float32)
    product = jnp.dot(factor, factor.T, precision=lax.Precision.HIGHEST) / NLOC
    return product + diag_shift * jnp.eye(NLOC, dtype=jnp.float32)


def draw_stiff_ref(key, part):
    return symmetric_matrix(jax.random.fold_in(key, 51), 0.5)


def draw_mass_ref(key, part):
    return symmetric_matrix(jax.random.fold_in(key, 52), 1.0)


def level_of(key, shape, pieces, low, top_value):
    gain, own = 1.0, jax.random.fold_in(key, 6)
    for axis_at, shards_of in pieces:
        draws = jnp.exp(jax.random.uniform(jax.random.fold_in(own, axis_at), (shards_of,), jnp.float32, low / len(pieces), top_value / len(pieces)))
        gain = gain * jnp.repeat(draws, shape[axis_at] // shards_of).reshape([-1 if axis == axis_at else 1 for axis in range(len(shape))])
    return gain


def setup_inputs(seed: int = 0) -> dict:
    splits = jax.random.split(jax.random.key(seed), 10)
    trial_block = draw_trial_block(jax.random.fold_in(splits[9], 71), 0)
    stiff_coef = jnp.clip(jnp.exp(math.log(3.0) - 2.3025851 * jax.random.uniform(splits[1], (N_PX, N_PY, ELEM_CAP), jnp.float32) ** level_of(splits[1], (N_PX, N_PY, ELEM_CAP), ((0, 8), (1, 4)), -0.2, 0.2)), 0.3, 3.0)
    mass_coef = jnp.clip(jnp.exp(math.log(12.0) - 2.4849066 * jax.random.uniform(splits[2], (N_PX, N_PY, ELEM_CAP), jnp.float32) ** level_of(splits[2], (N_PX, N_PY, ELEM_CAP), ((0, 8), (1, 4)), -0.2, 0.2)), 1.0, 12.0)
    elem_count = draw_elem_count(jax.random.fold_in(splits[9], 71), 0)
    elem_dofs = draw_elem_dofs(jax.random.fold_in(splits[9], 71), 0)
    pairing = jax.random.permutation(splits[5], FACE).astype(jnp.int32)
    bloch_fraction = draw_bloch_fraction(jax.random.fold_in(splits[9], 71), 0)
    stiff_ref = draw_stiff_ref(jax.random.fold_in(splits[9], 71), 0)
    mass_ref = draw_mass_ref(jax.random.fold_in(splits[9], 71), 0)
    return {"trial_block": trial_block, "stiff_coef": stiff_coef, "mass_coef": mass_coef, "elem_count": elem_count, "elem_dofs": elem_dofs, "pairing": pairing, "bloch_fraction": bloch_fraction, "stiff_ref": stiff_ref, "mass_ref": mass_ref}


HIGH = lax.Precision.HIGHEST


def extended_all(trial_block, pairing, cosine, sine_part):
    low_x = trial_block[..., INTERIOR:INTERIOR + FACE]
    low_y = trial_block[..., INTERIOR + FACE:OWNED]
    high_x = jnp.roll(low_x, -1, axis=0)
    wrapped = low_x[0][..., pairing]
    turned = jnp.stack([cosine * wrapped[:, 0] - sine_part * wrapped[:, 1], sine_part * wrapped[:, 0] + cosine * wrapped[:, 1]], axis=1)
    high_x = high_x.at[N_PX - 1].set(turned)
    high_y = jnp.concatenate([low_y[:, 1:], jnp.zeros_like(low_y[:, :1])], axis=1)
    return jnp.concatenate([trial_block, high_x, high_y], axis=-1)


def part_images(ext_part, stiff_part, mass_part, live_total, slot_dofs, stiff_ref, mass_ref):
    flat_rows = ext_part.reshape(2 * NVEC, EXTENDED)
    index_t = slot_dofs.T
    gathered = flat_rows[:, index_t]
    live_mask = (jnp.arange(ELEM_CAP, dtype=jnp.int32) < live_total).astype(jnp.float32)
    curl_terms = jnp.einsum("ji,rie->rje", stiff_ref, gathered, precision=HIGH, preferred_element_type=jnp.float32) * (stiff_part * live_mask)
    mass_terms = jnp.einsum("ji,rie->rje", mass_ref, gathered, precision=HIGH, preferred_element_type=jnp.float32) * (mass_part * live_mask)
    zero_rows = jnp.zeros((2 * NVEC, EXTENDED), jnp.float32)
    curl_ext = zero_rows.at[:, index_t].add(curl_terms)
    mass_ext = zero_rows.at[:, index_t].add(mass_terms)
    return curl_ext.reshape(2, NVEC, EXTENDED), mass_ext.reshape(2, NVEC, EXTENDED)


def assemble(images, pairing, cosine, sine_part):
    owned_part = images[..., :OWNED]
    side_x = images[..., OWNED:OWNED + FACE]
    side_y = images[..., OWNED + FACE:]
    back_x = jnp.roll(side_x, 1, axis=0)
    source = side_x[N_PX - 1]
    turned = jnp.stack([cosine * source[:, 0] + sine_part * source[:, 1], cosine * source[:, 1] - sine_part * source[:, 0]], axis=1)
    placed = jnp.zeros_like(turned).at[..., pairing].set(turned)
    back_x = back_x.at[0].set(placed)
    back_y = jnp.concatenate([jnp.zeros_like(side_y[:, :1]), side_y[:, :-1]], axis=1)
    owned_part = owned_part.at[..., INTERIOR:INTERIOR + FACE].add(back_x)
    owned_part = owned_part.at[..., INTERIOR + FACE:OWNED].add(back_y)
    return owned_part


def gram_of(left_vec, right_vec):
    real_part = jnp.dot(left_vec[0], right_vec[0].T, precision=HIGH, preferred_element_type=jnp.float32) + jnp.dot(left_vec[1], right_vec[1].T, precision=HIGH, preferred_element_type=jnp.float32)
    imag_part = jnp.dot(left_vec[0], right_vec[1].T, precision=HIGH, preferred_element_type=jnp.float32) - jnp.dot(left_vec[1], right_vec[0].T, precision=HIGH, preferred_element_type=jnp.float32)
    return jnp.stack([real_part, imag_part])


def reference(trial_block, stiff_coef, mass_coef, elem_count, elem_dofs, pairing, bloch_fraction, stiff_ref, mass_ref):
    phase_angle = 2.0 * jnp.pi * bloch_fraction[0].astype(jnp.float32) / bloch_fraction[1].astype(jnp.float32)
    cosine = jnp.cos(phase_angle)
    sine_part = jnp.sin(phase_angle)
    parts_all = N_PX * N_PY
    extended = extended_all(trial_block, pairing, cosine, sine_part)

    def one_part(items):
        return part_images(items[0], items[1], items[2], items[3], items[4], stiff_ref, mass_ref)

    curl_ext, mass_ext = lax.map(one_part, (extended.reshape(parts_all, 2, NVEC, EXTENDED), stiff_coef.reshape(parts_all, ELEM_CAP), mass_coef.reshape(parts_all, ELEM_CAP), elem_count.reshape(parts_all), elem_dofs.reshape(parts_all, ELEM_CAP, NLOC)))
    curl_ext = curl_ext.reshape(N_PX, N_PY, 2, NVEC, EXTENDED)
    mass_ext = mass_ext.reshape(N_PX, N_PY, 2, NVEC, EXTENDED)
    curl_image = assemble(curl_ext, pairing, cosine, sine_part)
    mass_image = assemble(mass_ext, pairing, cosine, sine_part)

    def flatten(values):
        return jnp.moveaxis(values.reshape(parts_all, 2, NVEC, OWNED), 0, 2).reshape(2, NVEC, parts_all * OWNED)

    left_vec = flatten(trial_block)
    gram = jnp.stack([gram_of(left_vec, flatten(curl_image)), gram_of(left_vec, flatten(mass_image))]) / (parts_all * OWNED)
    return curl_image, mass_image, gram
```

```python
import functools
import math

import jax
import jax.numpy as jnp
from jax import lax
from jax.experimental import pallas as pl
from jax.experimental.pallas import tpu as pltpu
from jax.sharding import PartitionSpec as P

LANES = 128


def ring_route(axis, steps):
    count = lax.axis_size(axis)
    return [(source, (source + steps) % count) for source in range(count)]


def line_route(axis, distance):
    devices = range(lax.axis_size(axis))
    return [(i - distance, i) for i in devices if i - distance in devices]


def gather_lanes(table_ref, index):
    high = index // LANES
    low = index % LANES
    found = jnp.zeros_like(index)
    for r in range(table_ref.shape[0]):
        line = jnp.broadcast_to(table_ref[r : r + 1, :], index.shape)
        found = jnp.where(high == r, jnp.take_along_axis(line, low, axis=1), found)
    return found


def remap_kernel(owned_len, face_len, flag_ref, dofs_ref, pair_ref, out_ref):
    out_ref[...] = dofs_ref[...]

    @pl.when(flag_ref[0] == 1)
    def _():
        index = dofs_ref[:, :LANES]
        local = index - owned_len
        on_face = (local >= 0) & (local < face_len)
        paired = gather_lanes(pair_ref, jnp.where(on_face, local, 0))
        out_ref[:, :LANES] = jnp.where(on_face, paired + owned_len, index)


def element_kernel(
    dims,
    dofs_ref,
    count_ref,
    turn_ref,
    own_ref,
    high_x_ref,
    high_y_ref,
    pair_coef_ref,
    scale_ref,
    curl_ref,
    mass_ref,
    side_x_ref,
    side_y_ref,
    gram_ref,
    rows_x,
    gath,
    term,
    *accs,
):
    vecs, owned_len, face_len, capacity, nloc, block_rows = dims
    width = 2 * vecs
    groups = LANES // (2 * width)
    copies = LANES // width
    interior = owned_len - 2 * face_len
    extent = owned_len + 2 * face_len
    cos, sin = turn_ref[0], turn_ref[1]
    block_elems = groups * block_rows

    def turn_in(pair):
        return jnp.concatenate(
            [
                cos * pair[:vecs] - sin * pair[vecs:],
                sin * pair[:vecs] + cos * pair[vecs:],
            ],
            axis=0,
        )

    def turn_back(pair):
        return jnp.concatenate(
            [
                cos * pair[:vecs] + sin * pair[vecs:],
                cos * pair[vecs:] - sin * pair[:vecs],
            ],
            axis=0,
        )

    def put_rows(tile, first):
        rows_x[pl.ds(first, LANES), :] = jnp.concatenate([tile] * copies, axis=0).T

    zero_tile = jnp.zeros((LANES, LANES), jnp.float32)

    def build_own(c, carry):
        first = pl.multiple_of(c * LANES, LANES)
        put_rows(own_ref[:, pl.ds(first, LANES)], first)
        for acc in accs:
            acc[pl.ds(first, LANES), :] = zero_tile
        return carry

    lax.fori_loop(0, owned_len // LANES, build_own, 0)

    def build_face(c, carry):
        first = pl.multiple_of(c * LANES, LANES)
        at_x = pl.multiple_of(owned_len + first, LANES)
        at_y = pl.multiple_of(owned_len + face_len + first, LANES)
        put_rows(turn_in(high_x_ref[:, pl.ds(first, LANES)]), at_x)
        put_rows(high_y_ref[:, pl.ds(first, LANES)], at_y)
        for acc in accs:
            acc[pl.ds(at_x, LANES), :] = zero_tile
            acc[pl.ds(at_y, LANES), :] = zero_tile
        return carry

    lax.fori_loop(0, face_len // LANES, build_face, 0)

    lane = lax.broadcasted_iota(jnp.int32, (1, LANES), 1) // (2 * width)
    masks = [lane == k for k in range(groups)]

    def pick(parts):
        out = parts[-1]
        for k in range(groups - 2, -1, -1):
            out = jnp.where(masks[k], parts[k], out)
        return out

    def block(b, carry):
        first_elem = b * block_elems

        def gather_one(g, c):
            elem = first_elem + g * groups
            for i in range(nloc):
                parts = [
                    rows_x[pl.ds(dofs_ref[i * capacity + elem + k], 1), :] for k in range(groups)
                ]
                gath[pl.ds(i * block_rows + g, 1), :] = pick(parts)
            return c

        lax.fori_loop(0, block_rows, gather_one, 0)

        scale = scale_ref[pl.ds(pl.multiple_of(b * block_rows, block_rows), block_rows), :]
        values = [gath[i * block_rows : (i + 1) * block_rows, :] for i in range(nloc)]
        for j in range(nloc):
            total = pair_coef_ref[j * nloc] * values[0]
            for i in range(1, nloc):
                total = total + pair_coef_ref[j * nloc + i] * values[i]
            term[j * block_rows : (j + 1) * block_rows, :] = total * scale

        def scatter_one(g, c):
            elem = first_elem + g * groups
            for j in range(nloc):
                row = term[pl.ds(j * block_rows + g, 1), :]
                for k in range(groups):
                    at = pl.ds(dofs_ref[j * capacity + elem + k], 1)
                    accs[k][at, :] = accs[k][at, :] + row
            return c

        lax.fori_loop(0, block_rows, scatter_one, 0)
        return carry

    live = count_ref[0]
    lax.fori_loop(0, (live + block_elems - 1) // block_elems, block, 0)

    def folded(first):
        at = pl.ds(first, LANES)
        turned = pick([acc[at, :] for acc in accs]).T
        total = turned[: 2 * width]
        for k in range(1, groups):
            total = total + turned[k * 2 * width : (k + 1) * 2 * width]
        return total

    def split(x):
        top = x.astype(jnp.bfloat16)
        return top, (x - top.astype(jnp.float32)).astype(jnp.bfloat16)

    def inner(x, y):
        def one(p, q):
            return lax.dot_general(
                p, q, (((1,), (1,)), ((), ())), preferred_element_type=jnp.float32
            )

        xt, xb = split(x)
        yt, yb = split(y)
        return one(xt, yt) + (one(xt, yb) + one(xb, yt))

    gram_ref[...] = jnp.zeros_like(gram_ref)

    def fold_own(c, carry):
        first = pl.multiple_of(c * LANES, LANES)
        at = pl.ds(first, LANES)
        total = folded(first)
        curl_ref[:, at] = total[:width]
        mass_ref[:, at] = total[width:]
        gram_ref[...] += inner(own_ref[:, at], total)
        return carry

    lax.fori_loop(0, owned_len // LANES, fold_own, 0)

    def fold_face(c, carry):
        first = pl.multiple_of(c * LANES, LANES)
        at = pl.ds(first, LANES)
        total = folded(pl.multiple_of(owned_len + first, LANES))
        gram_ref[...] += inner(turn_in(high_x_ref[:, at]), total)
        side_x_ref[:width, at] = turn_back(total[:width])
        side_x_ref[width:, at] = turn_back(total[width:])
        total = folded(pl.multiple_of(owned_len + face_len + first, LANES))
        gram_ref[...] += inner(high_y_ref[:, at], total)
        side_y_ref[:, at] = total
        return carry

    lax.fori_loop(0, face_len // LANES, fold_face, 0)


def all_sum(value, axis):
    count = lax.axis_size(axis)
    step = 1
    total = value
    while step < count:
        total = total + lax.ppermute(total, axis, [(i, i ^ step) for i in range(count)])
        step *= 2
    return total


def on_device(
    trial_block,
    stiff_coef,
    mass_coef,
    elem_count,
    elem_dofs,
    pairing,
    bloch_fraction,
    stiff_ref,
    mass_ref,
):
    own_block = trial_block[0, 0]
    vecs, owned_len = own_block.shape[1:]
    face_len = pairing.shape[0]
    interior = owned_len - 2 * face_len
    width = 2 * vecs
    groups = LANES // (2 * width)
    capacity, nloc = elem_dofs.shape[2:]
    phase_angle = (
        2.0
        * math.pi
        * bloch_fraction[0].astype(jnp.float32)
        / bloch_fraction[1].astype(jnp.float32)
    )
    at_end = lax.axis_index("px") == lax.axis_size("px") - 1
    turn = jnp.where(
        at_end,
        jnp.stack([jnp.cos(phase_angle), jnp.sin(phase_angle)]),
        jnp.array([1.0, 0.0], jnp.float32),
    )
    own_rows = own_block.reshape(width, owned_len)
    low_x = own_rows[:, interior : interior + face_len]
    low_y = own_rows[:, interior + face_len :]
    high_x = lax.ppermute(low_x, "px", ring_route("px", -1))
    high_y = lax.ppermute(low_y, "py", line_route("py", -1))

    slot_dofs = elem_dofs[0, 0].T
    remapped = pl.pallas_call(
        functools.partial(remap_kernel, owned_len, face_len),
        out_shape=jax.ShapeDtypeStruct(slot_dofs.shape, jnp.int32),
        in_specs=[
            pl.BlockSpec(memory_space=pltpu.SMEM),
            pl.BlockSpec(memory_space=pltpu.VMEM),
            pl.BlockSpec(memory_space=pltpu.VMEM),
        ],
        out_specs=pl.BlockSpec(memory_space=pltpu.VMEM),
        name="remap",
    )(at_end.astype(jnp.int32).reshape(1), slot_dofs, pairing.reshape(-1, LANES))
    flat_dofs = remapped.reshape(-1)

    coefs = jnp.stack([stiff_ref.reshape(-1), mass_ref.reshape(-1)], axis=1)
    block_rows = 8
    pair_coef = jnp.broadcast_to(
        coefs[:, None, None, :, None], (nloc * nloc, block_rows, groups, 2, width)
    ).reshape(nloc * nloc, block_rows, LANES)
    live = elem_count[0]
    slot_live = jnp.arange(capacity, dtype=jnp.int32) < live[0]
    scales = jnp.where(slot_live[None], jnp.stack([stiff_coef[0, 0], mass_coef[0, 0]]), 0.0)
    scale = jnp.broadcast_to(
        scales.reshape(2, capacity // groups, groups).transpose(1, 2, 0)[..., None],
        (capacity // groups, groups, 2, width),
    ).reshape(capacity // groups, LANES)

    extent = owned_len + 2 * face_len
    dims = (vecs, owned_len, face_len, capacity, nloc, block_rows)
    curl, mass, side_x, side_y, gram = pl.pallas_call(
        functools.partial(element_kernel, dims),
        out_shape=(
            jax.ShapeDtypeStruct((width, owned_len), jnp.float32),
            jax.ShapeDtypeStruct((width, owned_len), jnp.float32),
            jax.ShapeDtypeStruct((2 * width, face_len), jnp.float32),
            jax.ShapeDtypeStruct((2 * width, face_len), jnp.float32),
            jax.ShapeDtypeStruct((width, 2 * width), jnp.float32),
        ),
        in_specs=[pl.BlockSpec(memory_space=pltpu.SMEM)] * 3
        + [pl.BlockSpec(memory_space=pltpu.VMEM)] * 5,
        out_specs=[pl.BlockSpec(memory_space=pltpu.VMEM)] * 5,
        scratch_shapes=[
            pltpu.VMEM((extent, LANES), jnp.float32),
            pltpu.VMEM((nloc * block_rows, LANES), jnp.float32),
            pltpu.VMEM((nloc * block_rows, LANES), jnp.float32),
        ]
        + [pltpu.VMEM((extent, LANES), jnp.float32)] * groups,
        compiler_params=pltpu.CompilerParams(vmem_limit_bytes=60 * 1024 * 1024),
        name="elements",
    )(flat_dofs, live, turn, own_rows, high_x, high_y, pair_coef, scale)

    back_x = lax.ppermute(side_x, "px", ring_route("px", 1))
    back_y = lax.ppermute(side_y, "py", line_route("py", 1))

    def finish(image, part):
        add_x = back_x[part * width : (part + 1) * width]
        add_y = back_y[part * width : (part + 1) * width]
        whole = image.at[:, interior:].add(jnp.concatenate([add_x, add_y], axis=1))
        return whole.reshape(1, 1, 2, vecs, owned_len)

    summed = all_sum(all_sum(gram, "px"), "py")
    parts = summed.reshape(2, vecs, 2, 2, vecs)
    real_part = parts[0, :, :, 0] + parts[1, :, :, 1]
    imag_part = parts[0, :, :, 1] - parts[1, :, :, 0]
    divisor = float(lax.axis_size("px") * lax.axis_size("py") * owned_len)
    gram_out = jnp.stack([real_part, imag_part]).transpose(2, 0, 1, 3) / divisor
    return (finish(curl, 0), finish(mass, 1), gram_out)


def solution(mesh):
    return jax.shard_map(
        on_device,
        mesh=mesh,
        in_specs=(
            P("px", "py", None, None, None),
            P("px", "py", None),
            P("px", "py", None),
            P("px", "py"),
            P("px", "py", None, None),
            P(),
            P(),
            P(),
            P(),
        ),
        out_specs=(P("px", "py", None, None, None), P("px", "py", None, None, None), P()),
        check_vma=False,
    )
```

```python
import functools
import math

import jax
import jax.numpy as jnp
from jax import lax
from jax.experimental import pallas as pl
from jax.experimental.pallas import tpu as pltpu
from jax.sharding import PartitionSpec as P

LANES = 128
BLOCK_ROWS = 8
F32 = jnp.float32
BF16 = jnp.bfloat16


def ring_route(axis, steps):
    count = lax.axis_size(axis)
    return [(source, (source + steps) % count) for source in range(count)]


def line_route(axis, distance):
    devices = range(lax.axis_size(axis))
    return [(i - distance, i) for i in devices if i - distance in devices]


def iota(shape, axis):
    return lax.broadcasted_iota(jnp.int32, shape, axis)


def split(x):
    top = x.astype(BF16)
    return top, (x - top.astype(F32)).astype(BF16)


def dot_nt(left, right):
    return lax.dot_general(
        left, right, (((1,), (1,)), ((), ())), preferred_element_type=F32
    )


def gather_lanes(table_ref, index):
    high = index // LANES
    low = index % LANES
    found = jnp.zeros_like(index)
    for r in range(table_ref.shape[0]):
        line = jnp.broadcast_to(table_ref[r : r + 1, :], index.shape)
        found = jnp.where(high == r, jnp.take_along_axis(line, low, axis=1), found)
    return found


def prepare_kernel(
    owned_len, face_len, width, count_ref, bloch_ref, dofs_ref, pair_ref, stiff_ref, mass_ref,
    table_ref, scale_ref, turn_ref,
):
    capacity, nloc = dofs_ref.shape
    rows = table_ref.shape[0]
    groups = LANES // (2 * width)
    at_end = lax.axis_index("px") == lax.axis_size("px") - 1
    per_chunk = LANES // groups
    lane_of = iota((LANES, LANES), 0)
    elem_of = iota((LANES, LANES), 1)
    mine = elem_of % groups == lane_of // (2 * width)
    is_curl = lane_of // width % 2 == 0
    chooser = (iota((per_chunk, LANES), 1) // groups == iota((per_chunk, LANES), 0)).astype(BF16)
    chooser = jnp.concatenate([chooser, chooser], axis=1)
    live = count_ref[0]
    for c in range(capacity // LANES):
        at = slice(c * LANES, (c + 1) * LANES)
        tile = jnp.concatenate(
            [dofs_ref[at, :], jnp.zeros((LANES, LANES - nloc), jnp.int32)], axis=1
        ).T
        index = tile[:rows]
        slot_row = iota((rows, LANES), 0)
        after = jnp.concatenate([index[1:], index[:1]], axis=0)
        clash = (index == after) & (slot_row % 2 == 0) & (slot_row + 1 < nloc)
        flag = jnp.max(clash.astype(jnp.int32), axis=0, keepdims=True)
        flag = jnp.broadcast_to(flag, (8, LANES))
        reach = groups * BLOCK_ROWS // 2
        while reach:
            flag = jnp.maximum(flag, pltpu.roll(flag, reach, 1))
            reach //= 2
        index = jnp.where(slot_row == nloc, flag[:1], index)
        table_ref[:, at] = index
        scales = jnp.where(is_curl, stiff_ref[:, at], mass_ref[:, at])
        scales = jnp.where(mine & (c * LANES + elem_of < live), scales, 0.0)
        scale_ref[c * per_chunk : (c + 1) * per_chunk, :] = dot_nt(
            chooser, jnp.concatenate(split(scales), axis=1)
        )

    @pl.when(at_end)
    def _():
        index = table_ref[:, :LANES]
        local = index - owned_len
        on_face = (local >= 0) & (local < face_len) & (iota((rows, LANES), 0) < nloc)
        paired = gather_lanes(pair_ref, jnp.where(on_face, local, 0))
        table_ref[:, :LANES] = jnp.where(on_face, paired + owned_len, index)

    ratio = jnp.full((8, LANES), bloch_ref[0].astype(F32), F32) / bloch_ref[1].astype(F32)
    angle = (2.0 * math.pi) * jnp.where(at_end, ratio, 0.0)
    turn_ref[:8] = jnp.cos(angle)
    turn_ref[8:] = jnp.sin(angle)


def element_kernel(
    width,
    count_ref,
    stiff_ref,
    mass_ref,
    table_hbm,
    turn_ref,
    own_ref,
    high_x_ref,
    high_y_ref,
    scale_ref,
    curl_ref,
    mass_out_ref,
    side_x_ref,
    side_y_ref,
    gram_ref,
    dofs_ref,
    pair_coef,
    rows_x,
    gath,
    term,
    sems,
    *accs,
):
    owned_len = own_ref.shape[1]
    face_len = high_x_ref.shape[1]
    vecs = width // 2
    nloc = stiff_ref.shape[0]
    capacity = table_hbm.shape[1]
    block_rows = BLOCK_ROWS
    groups = LANES // (2 * width)
    copies = LANES // width
    block_elems = groups * block_rows

    loads = [
        pltpu.make_async_copy(
            table_hbm.at[i], dofs_ref.at[pl.ds(i * capacity, capacity)], sems.at[i]
        )
        for i in range(nloc + 1)
    ]
    for load in loads:
        load.start()

    cos, sin = turn_ref[:vecs], turn_ref[8 : 8 + vecs]

    def turn_in(pair):
        n = pair.shape[1] // LANES
        c, s = jnp.concatenate([cos] * n, axis=1), jnp.concatenate([sin] * n, axis=1)
        a, b = pair[:vecs], pair[vecs:]
        return jnp.concatenate([c * a - s * b, s * a + c * b], axis=0)

    def turn_back(pair):
        n = pair.shape[1] // LANES
        c, s = jnp.concatenate([cos] * n, axis=1), jnp.concatenate([sin] * n, axis=1)
        a, b = pair[:vecs], pair[vecs:]
        return jnp.concatenate([c * a + s * b, c * b - s * a], axis=0)

    unit = (iota((LANES, LANES), 0) == iota((LANES, LANES), 1)).astype(BF16)
    unit = jnp.concatenate([unit, unit], axis=1)
    zero_tile = jnp.zeros((LANES, LANES), F32)

    def put_rows(tile, first):
        top, low = split(tile)
        tiled = jnp.concatenate(
            [jnp.concatenate([top] * copies, axis=0), jnp.concatenate([low] * copies, axis=0)],
            axis=1,
        )
        rows_x[pl.ds(first, LANES), :] = dot_nt(unit, tiled)
        for acc in accs:
            acc[pl.ds(first, LANES), :] = zero_tile

    span = 4 * LANES

    def build_own(c, carry):
        for u in range(span // LANES):
            first = pl.multiple_of(c * span + u * LANES, LANES)
            put_rows(own_ref[:, pl.ds(first, LANES)], first)
        return carry

    lax.fori_loop(0, owned_len // span, build_own, 0)

    def build_face(c, carry):
        for u in range(2):
            first = pl.multiple_of(c * 2 * LANES + u * LANES, LANES)
            put_rows(
                turn_in(high_x_ref[:, pl.ds(first, LANES)]),
                pl.multiple_of(owned_len + first, LANES),
            )
            put_rows(
                high_y_ref[:, pl.ds(first, LANES)],
                pl.multiple_of(owned_len + face_len + first, LANES),
            )
        return carry

    lax.fori_loop(0, face_len // (2 * LANES), build_face, 0)

    curl_lane = iota((8, LANES), 1) // width % 2 == 0

    def build_coef(j, carry):
        for i in range(nloc):
            pair_coef[j * nloc + i] = jnp.where(curl_lane, stiff_ref[j, i], mass_ref[j, i])
        return carry

    lax.fori_loop(0, nloc, build_coef, 0)

    for load in loads:
        load.wait()

    lane = iota((1, LANES), 1) // (2 * width)
    masks = [lane == k for k in range(groups)]

    def pick(parts):
        out = parts[-1]
        for k in range(groups - 2, -1, -1):
            out = jnp.where(masks[k], parts[k], out)
        return out

    def index_of(i, elem):
        return dofs_ref.at[pl.ds(i * capacity, capacity)][elem]

    unroll = 2

    def block(b, carry):
        first_elem = b * block_elems

        def gather_some(t, c):
            for u in range(unroll):
                g = t * unroll + u
                elem = first_elem + g * groups
                for i in range(nloc):
                    parts = [
                        rows_x[pl.ds(index_of(i, elem + k), 1), :] for k in range(groups)
                    ]
                    gath[pl.ds(i * block_rows + g, 1), :] = pick(parts)
            return c

        lax.fori_loop(0, block_rows // unroll, gather_some, 0)

        scale = scale_ref[pl.ds(pl.multiple_of(b * block_rows, block_rows), block_rows), :]
        values = [gath[i * block_rows : (i + 1) * block_rows, :] for i in range(nloc)]
        for j in range(nloc):
            total = pair_coef[j * nloc] * values[0]
            for i in range(1, nloc):
                total = total + pair_coef[j * nloc + i] * values[i]
            term[j * block_rows : (j + 1) * block_rows, :] = total * scale

        def scatter_some(step):
            def some(t, c):
                for u in range(unroll):
                    g = t * unroll + u
                    elem = first_elem + g * groups
                    for j in range(0, nloc, step):
                        slots = range(j, min(j + step, nloc))
                        new = [term[pl.ds(s * block_rows + g, 1), :] for s in slots]
                        places = [
                            [pl.ds(index_of(s, elem + k), 1) for k in range(groups)]
                            for s in slots
                        ]
                        sums = [
                            [accs[k][at[k], :] + row for k in range(groups)]
                            for at, row in zip(places, new)
                        ]
                        for at, row in zip(places, sums):
                            for k in range(groups):
                                accs[k][at[k], :] = row[k]
                return c

            lax.fori_loop(0, block_rows // unroll, some, 0)

        clash = index_of(nloc, first_elem + block_elems - 1)

        @pl.when(clash == 0)
        def _():
            scatter_some(2)

        @pl.when(clash != 0)
        def _():
            scatter_some(1)

        return carry

    live = count_ref[0]
    lax.fori_loop(0, (live + block_elems - 1) // block_elems, block, 0)

    folder = (iota((2 * width, LANES), 1) % (2 * width) == iota((2 * width, LANES), 0)).astype(BF16)
    folder = jnp.concatenate([folder, folder], axis=1)
    wide = 2 * LANES

    def folded(first):
        at = pl.ds(first, wide)
        total = pick([acc[at, :] for acc in accs])
        return dot_nt(folder, jnp.concatenate(split(total), axis=1))

    def inner(x, y):
        xt, xb = split(x)
        yt, yb = split(y)
        return dot_nt(
            jnp.concatenate([xt, xt, xb], axis=1), jnp.concatenate([yt, yb, yt], axis=1)
        )

    def fold_own(c, gram):
        for u in range(2):
            first = pl.multiple_of(c * 2 * wide + u * wide, wide)
            at = pl.ds(first, wide)
            total = folded(first)
            curl_ref[:, at] = total[:width]
            mass_out_ref[:, at] = total[width:]
            gram = gram + inner(own_ref[:, at], total)
        return gram

    gram = lax.fori_loop(
        0, owned_len // (2 * wide), fold_own, jnp.zeros((width, 2 * width), F32)
    )

    def fold_face(c, gram):
        first = pl.multiple_of(c * wide, wide)
        at = pl.ds(first, wide)
        total = folded(pl.multiple_of(owned_len + first, wide))
        gram = gram + inner(turn_in(high_x_ref[:, at]), total)
        side_x_ref[:width, at] = turn_back(total[:width])
        side_x_ref[width:, at] = turn_back(total[width:])
        total = folded(pl.multiple_of(owned_len + face_len + first, wide))
        gram = gram + inner(high_y_ref[:, at], total)
        side_y_ref[:, at] = total
        return gram

    gram_ref[...] = lax.fori_loop(0, face_len // wide, fold_face, gram)


def all_sum(value, axis):
    count = lax.axis_size(axis)
    step = 1
    total = value
    while step < count:
        total = total + lax.ppermute(total, axis, [(i, i ^ step) for i in range(count)])
        step *= 2
    return total


def on_device(
    trial_block,
    stiff_coef,
    mass_coef,
    elem_count,
    elem_dofs,
    pairing,
    bloch_fraction,
    stiff_ref,
    mass_ref,
):
    own_block = trial_block[0, 0]
    vecs, owned_len = own_block.shape[1:]
    face_len = pairing.shape[0]
    interior = owned_len - 2 * face_len
    width = 2 * vecs
    groups = LANES // (2 * width)
    capacity, nloc = elem_dofs.shape[2:]
    own_rows = own_block.reshape(width, owned_len)
    low_x = own_rows[:, interior : interior + face_len]
    low_y = own_rows[:, interior + face_len :]
    high_x = lax.ppermute(low_x, "px", ring_route("px", -1))
    high_y = lax.ppermute(low_y, "py", line_route("py", -1))
    live = elem_count[0]
    table_rows = -(-(nloc + 1) // 8) * 8
    smem = pl.BlockSpec(memory_space=pltpu.SMEM)
    vmem = pl.BlockSpec(memory_space=pltpu.VMEM)

    table, scale, turn = pl.pallas_call(
        functools.partial(prepare_kernel, owned_len, face_len, width),
        out_shape=(
            jax.ShapeDtypeStruct((table_rows, capacity), jnp.int32),
            jax.ShapeDtypeStruct((capacity // groups, LANES), F32),
            jax.ShapeDtypeStruct((16, LANES), F32),
        ),
        in_specs=[smem] * 2 + [vmem] * 4,
        out_specs=[vmem] * 3,
        name="prepare",
    )(
        live,
        bloch_fraction,
        elem_dofs[0, 0],
        pairing.reshape(-1, LANES),
        stiff_coef[0],
        mass_coef[0],
    )

    extent = owned_len + 2 * face_len
    curl, mass, side_x, side_y, gram = pl.pallas_call(
        functools.partial(element_kernel, width),
        out_shape=(
            jax.ShapeDtypeStruct((width, owned_len), F32),
            jax.ShapeDtypeStruct((width, owned_len), F32),
            jax.ShapeDtypeStruct((2 * width, face_len), F32),
            jax.ShapeDtypeStruct((2 * width, face_len), F32),
            jax.ShapeDtypeStruct((width, 2 * width), F32),
        ),
        in_specs=[smem] * 3 + [pl.BlockSpec(memory_space=pl.ANY)] + [vmem] * 5,
        out_specs=[vmem] * 5,
        scratch_shapes=[
            pltpu.SMEM(((nloc + 1) * capacity,), jnp.int32),
            pltpu.VMEM((nloc * nloc, BLOCK_ROWS, LANES), F32),
            pltpu.VMEM((extent, LANES), F32),
            pltpu.VMEM((nloc * BLOCK_ROWS, LANES), F32),
            pltpu.VMEM((nloc * BLOCK_ROWS, LANES), F32),
            pltpu.SemaphoreType.DMA((nloc + 1,)),
        ]
        + [pltpu.VMEM((extent, LANES), F32)] * groups,
        compiler_params=pltpu.CompilerParams(vmem_limit_bytes=60 * 1024 * 1024),
        name="elements",
    )(live, stiff_ref, mass_ref, table, turn, own_rows, high_x, high_y, scale)

    back_x = lax.ppermute(side_x, "px", ring_route("px", 1))
    back_y = lax.ppermute(side_y, "py", line_route("py", 1))

    def finish(image, part):
        add_x = back_x[part * width : (part + 1) * width]
        add_y = back_y[part * width : (part + 1) * width]
        whole = image.at[:, interior:].add(jnp.concatenate([add_x, add_y], axis=1))
        return whole.reshape(1, 1, 2, vecs, owned_len)

    summed = all_sum(all_sum(gram, "px"), "py")
    parts = summed.reshape(2, vecs, 2, 2, vecs)
    real_part = parts[0, :, :, 0] + parts[1, :, :, 1]
    imag_part = parts[0, :, :, 1] - parts[1, :, :, 0]
    divisor = float(lax.axis_size("px") * lax.axis_size("py") * owned_len)
    gram_out = jnp.stack([real_part, imag_part]).transpose(2, 0, 1, 3) / divisor
    return (finish(curl, 0), finish(mass, 1), gram_out)


def solution(mesh):
    return jax.shard_map(
        on_device,
        mesh=mesh,
        in_specs=(
            P("px", "py", None, None, None),
            P("px", "py", None),
            P("px", "py", None),
            P("px", "py"),
            P("px", "py", None, None),
            P(),
            P(),
            P(),
            P(),
        ),
        out_specs=(P("px", "py", None, None, None), P("px", "py", None, None, None), P()),
        check_vma=False,
    )
```

```python
import functools
import math

import jax
import jax.numpy as jnp
from jax import lax
from jax.experimental import pallas as pl
from jax.experimental.pallas import tpu as pltpu
from jax.sharding import PartitionSpec as P

LANES = 128
BLOCK_ROWS = 8
STEP = 4
N_ACC = 4
F32 = jnp.float32
BF16 = jnp.bfloat16


def ring_route(axis, steps):
    count = lax.axis_size(axis)
    return [(source, (source + steps) % count) for source in range(count)]


def line_route(axis, distance):
    devices = range(lax.axis_size(axis))
    return [(i - distance, i) for i in devices if i - distance in devices]


def iota(shape, axis):
    return lax.broadcasted_iota(jnp.int32, shape, axis)


def split(x):
    top = x.astype(BF16)
    return top, (x - top.astype(F32)).astype(BF16)


def dot_nt(left, right):
    return lax.dot_general(
        left, right, (((1,), (1,)), ((), ())), preferred_element_type=F32
    )


def gather_lanes(table_ref, index):
    high = index // LANES
    low = index % LANES
    found = jnp.zeros_like(index)
    for r in range(table_ref.shape[0]):
        line = jnp.broadcast_to(table_ref[r : r + 1, :], index.shape)
        found = jnp.where(high == r, jnp.take_along_axis(line, low, axis=1), found)
    return found


def prepare_kernel(
    owned_len, face_len, width, count_ref, bloch_ref, dofs_ref, pair_ref, stiff_ref, mass_ref,
    table_ref, own_table_ref, face_table_ref, scale_ref, turn_ref,
):
    capacity, nloc = dofs_ref.shape
    rows = table_ref.shape[0]
    face_slots = face_table_ref.shape[1]
    groups = LANES // (2 * width)
    at_end = lax.axis_index("px") == lax.axis_size("px") - 1
    per_chunk = LANES // groups
    lane_of = iota((LANES, LANES), 0)
    elem_of = iota((LANES, LANES), 1)
    mine = elem_of % groups == lane_of // (2 * width)
    is_curl = lane_of // width % 2 == 0
    chooser = (iota((per_chunk, LANES), 1) // groups == iota((per_chunk, LANES), 0)).astype(BF16)
    chooser = jnp.concatenate([chooser, chooser], axis=1)
    live = count_ref[0]
    slot_row = iota((rows, LANES), 0)
    for c in range(capacity // LANES):
        at = slice(c * LANES, (c + 1) * LANES)
        tile = jnp.concatenate(
            [dofs_ref[at, :], jnp.zeros((LANES, LANES - nloc), jnp.int32)], axis=1
        ).T
        index = tile[:rows]
        clash = jnp.zeros((rows, LANES), jnp.int32)
        for d in range(1, STEP):
            after = jnp.concatenate([index[d:], index[:d]], axis=0)
            same = (index == after) & (slot_row % STEP + d < STEP) & (slot_row + d < nloc)
            clash = jnp.maximum(clash, same.astype(jnp.int32))
        flag = jnp.broadcast_to(jnp.max(clash, axis=0, keepdims=True), (8, LANES))
        reach = groups * BLOCK_ROWS // 2
        while reach:
            flag = jnp.maximum(flag, pltpu.roll(flag, reach, 1))
            reach //= 2
        if c * LANES < face_slots:
            local = index - owned_len
            on_face = at_end & (local >= 0) & (local < face_len)
            paired = gather_lanes(pair_ref, jnp.where(on_face, local, 0))
            index = jnp.where(on_face, paired + owned_len, index)
            face_table_ref[:, at] = jnp.where(
                index >= owned_len, index - owned_len, 2 * face_len
            )
        flags = jnp.broadcast_to(flag[:1], (rows, LANES))
        table_ref[:, at] = jnp.where(slot_row == nloc, flags, index)
        own_table_ref[:, at] = jnp.where(slot_row == nloc, flags, jnp.minimum(index, owned_len))
        scales = jnp.where(is_curl, stiff_ref[:, at], mass_ref[:, at])
        scales = jnp.where(mine & (c * LANES + elem_of < live), scales, 0.0)
        scale_ref[c * per_chunk : (c + 1) * per_chunk, :] = dot_nt(
            chooser, jnp.concatenate(split(scales), axis=1)
        )

    ratio = jnp.full((8, LANES), bloch_ref[0].astype(F32), F32) / bloch_ref[1].astype(F32)
    angle = (2.0 * math.pi) * jnp.where(at_end, ratio, 0.0)
    turn_ref[:8] = jnp.cos(angle)
    turn_ref[8:] = jnp.sin(angle)


def load_table(source, target, sems, count):
    columns = source.shape[1]
    loads = [
        pltpu.make_async_copy(source.at[i], target.at[pl.ds(i * columns, columns)], sems.at[i])
        for i in range(count)
    ]
    for load in loads:
        load.start()
    return loads


def lane_masks(width, groups):
    lane = iota((1, LANES), 1) // (2 * width)
    return [lane == k for k in range(groups)]


def pick(masks, parts):
    out = parts[-1]
    for mask, part in zip(masks[-2::-1], parts[-2::-1]):
        out = jnp.where(mask, part, out)
    return out


def folder_of(width):
    rows = 2 * width
    folder = (iota((rows, LANES), 1) % rows == iota((rows, LANES), 0)).astype(BF16)
    return jnp.concatenate([folder, folder], axis=1)


def add_rows(term_ref, accs, index_of, first_row, first_elem, nloc, groups, clash):
    unroll = 2

    def run(step):
        def some(t, c):
            for u in range(unroll):
                g = t * unroll + u
                elem = first_elem + g * groups
                for j in range(0, nloc, step):
                    slots = range(j, min(j + step, nloc))
                    new = [term_ref[pl.ds(first_row + s * BLOCK_ROWS + g, 1), :] for s in slots]
                    for k in range(groups):
                        places = [pl.ds(index_of(s, elem + k), 1) for s in slots]
                        sums = [accs[k][at, :] + row for at, row in zip(places, new)]
                        for at, row in zip(places, sums):
                            accs[k][at, :] = row
            return c

        lax.fori_loop(0, BLOCK_ROWS // unroll, some, 0)

    @pl.when(clash == 0)
    def _():
        run(STEP)

    @pl.when(clash != 0)
    def _():
        run(1)


def term_kernel(
    width,
    count_ref,
    stiff_ref,
    mass_ref,
    table_hbm,
    face_table_hbm,
    turn_ref,
    own_ref,
    high_x_ref,
    high_y_ref,
    scale_ref,
    term_ref,
    side_x_ref,
    side_y_ref,
    gram_ref,
    dofs_ref,
    face_dofs_ref,
    pair_coef,
    rows_x,
    gath,
    gram_acc,
    sems,
    face_sems,
    *accs,
):
    owned_len = own_ref.shape[1]
    face_len = high_x_ref.shape[1]
    vecs = width // 2
    nloc = stiff_ref.shape[0]
    capacity = table_hbm.shape[1]
    face_slots = face_table_hbm.shape[1]
    groups = LANES // (2 * width)
    copies = LANES // width
    block_elems = groups * BLOCK_ROWS
    block_terms = nloc * BLOCK_ROWS

    loads = load_table(table_hbm, dofs_ref, sems, nloc + 1)
    loads += load_table(face_table_hbm, face_dofs_ref, face_sems, nloc)

    cos, sin = turn_ref[:vecs], turn_ref[8 : 8 + vecs]

    def turned(pair, sign):
        n = pair.shape[1] // LANES
        c = jnp.concatenate([cos] * n, axis=1)
        s = jnp.concatenate([sin] * n, axis=1) * sign
        a, b = pair[:vecs], pair[vecs:]
        return jnp.concatenate([c * a - s * b, s * a + c * b], axis=0)

    unit = (iota((LANES, LANES), 0) == iota((LANES, LANES), 1)).astype(BF16)
    unit = jnp.concatenate([unit, unit], axis=1)
    zero_tile = jnp.zeros((LANES, LANES), F32)

    def put_rows(tile, first):
        top, low = split(tile)
        tiled = jnp.concatenate(
            [jnp.concatenate([top] * copies, axis=0), jnp.concatenate([low] * copies, axis=0)],
            axis=1,
        )
        rows_x[pl.ds(first, LANES), :] = dot_nt(unit, tiled)

    many = 8

    def build_own(c, carry):
        for u in range(many):
            first = pl.multiple_of((c * many + u) * LANES, LANES)
            put_rows(own_ref[:, pl.ds(first, LANES)], first)
        return carry

    lax.fori_loop(0, owned_len // (many * LANES), build_own, 0)

    def build_face(c, carry):
        for u in range(many // 2):
            first = pl.multiple_of((c * (many // 2) + u) * LANES, LANES)
            put_rows(
                turned(high_x_ref[:, pl.ds(first, LANES)], 1.0),
                pl.multiple_of(owned_len + first, LANES),
            )
            put_rows(
                high_y_ref[:, pl.ds(first, LANES)],
                pl.multiple_of(owned_len + face_len + first, LANES),
            )
            for acc in accs:
                acc[pl.ds(pl.multiple_of(2 * first, 2 * LANES), LANES), :] = zero_tile
                acc[pl.ds(pl.multiple_of(2 * first + LANES, LANES), LANES), :] = zero_tile
        return carry

    lax.fori_loop(0, face_len // (many // 2 * LANES), build_face, 0)

    curl_lane = iota((8, LANES), 1) // width % 2 == 0

    def build_coef(j, carry):
        for i in range(nloc):
            pair_coef[j * nloc + i] = jnp.where(curl_lane, stiff_ref[j, i], mass_ref[j, i])
        return carry

    lax.fori_loop(0, nloc, build_coef, 0)
    gram_acc[...] = jnp.zeros_like(gram_acc)

    for load in loads:
        load.wait()

    masks = lane_masks(width, groups)

    def index_of(i, elem):
        return dofs_ref.at[pl.ds(i * capacity, capacity)][elem]

    def face_index_of(i, elem):
        return face_dofs_ref.at[pl.ds(i * face_slots, face_slots)][elem]

    unroll = 2

    def block(b, carry):
        first_elem = b * block_elems

        def gather_some(t, c):
            for u in range(unroll):
                g = t * unroll + u
                elem = first_elem + g * groups
                for i in range(nloc):
                    parts = [
                        rows_x[pl.ds(index_of(i, elem + k), 1), :] for k in range(groups)
                    ]
                    gath[pl.ds(i * BLOCK_ROWS + g, 1), :] = pick(masks, parts)
            return c

        lax.fori_loop(0, BLOCK_ROWS // unroll, gather_some, 0)

        scale = scale_ref[pl.ds(pl.multiple_of(b * BLOCK_ROWS, BLOCK_ROWS), BLOCK_ROWS), :]
        values = [gath[i * BLOCK_ROWS : (i + 1) * BLOCK_ROWS, :] for i in range(nloc)]
        first_row = pl.multiple_of(b * block_terms, BLOCK_ROWS)
        for j in range(nloc):
            total = pair_coef[j * nloc] * values[0]
            for i in range(1, nloc):
                total = total + pair_coef[j * nloc + i] * values[i]
            at = pl.ds(pl.multiple_of(first_row + j * BLOCK_ROWS, BLOCK_ROWS), BLOCK_ROWS)
            term_ref[at, :] = total * scale
        left, left_low = split(gath[...])
        right, right_low = split(term_ref[pl.ds(first_row, block_terms), :])
        gram_acc[...] += lax.dot_general(
            jnp.concatenate([left, left, left_low], axis=0),
            jnp.concatenate([right, right_low, right], axis=0),
            (((0,), (0,)), ((), ())),
            preferred_element_type=F32,
        )
        return carry

    def face_block(b, carry):
        first_elem = b * block_elems
        clash = index_of(nloc, first_elem + block_elems - 1)
        add_rows(
            term_ref, accs, face_index_of, b * block_terms, first_elem, nloc, groups, clash
        )
        return carry

    live = count_ref[0]
    blocks = (live + block_elems - 1) // block_elems
    face_blocks = jnp.minimum(blocks, face_slots // block_elems)
    lax.fori_loop(0, blocks, block, 0)
    lax.fori_loop(0, face_blocks, face_block, 0)

    folder = folder_of(width)
    wide = 2 * LANES

    def folded(first):
        at = pl.ds(first, wide)
        total = pick(masks, [acc[at, :] for acc in accs])
        return dot_nt(folder, jnp.concatenate(split(total), axis=1))

    def fold_face(c, carry):
        for u in range(2):
            first = pl.multiple_of((2 * c + u) * wide, wide)
            at = pl.ds(first, wide)
            total = folded(first)
            side_x_ref[:width, at] = turned(total[:width], -1.0)
            side_x_ref[width:, at] = turned(total[width:], -1.0)
            side_y_ref[:, at] = folded(pl.multiple_of(face_len + first, wide))
        return carry

    lax.fori_loop(0, face_len // (2 * wide), fold_face, 0)

    whole = gram_acc[...]
    total = whole[:width]
    for k in range(1, groups):
        part = whole[2 * width * k : 2 * width * k + width]
        total = total + pltpu.roll(part, LANES - 2 * width * k, 1)
    re_left, im_left = total[:vecs], total[vecs:]
    lane = iota((vecs, LANES), 1)
    real_here = lane // vecs % 2 == 0
    swapped = jnp.where(
        real_here, pltpu.roll(im_left, LANES - vecs, 1), -pltpu.roll(im_left, vecs, 1)
    )
    joined = re_left + swapped
    for n in range(gram_ref.shape[0]):
        gram_ref[n] = joined


def add_kernel(width, count_ref, table_hbm, term_ref, curl_ref, mass_ref, dofs_ref, sems, *accs):
    owned_len = curl_ref.shape[1]
    capacity = table_hbm.shape[1]
    groups = LANES // (2 * width)
    block_elems = groups * BLOCK_ROWS
    nloc = term_ref.shape[0] // (capacity // groups)
    block_terms = nloc * BLOCK_ROWS
    loads = load_table(table_hbm, dofs_ref, sems, nloc + 1)
    many = 4
    zero_tile = jnp.zeros((many * LANES, LANES), F32)

    def clear(c, carry):
        at = pl.ds(pl.multiple_of(c * many * LANES, LANES), many * LANES)
        for acc in accs:
            acc[at, :] = zero_tile
        return carry

    lax.fori_loop(0, owned_len // (many * LANES), clear, 0)
    for load in loads:
        load.wait()

    def index_of(i, elem):
        return dofs_ref.at[pl.ds(i * capacity, capacity)][elem]

    def block(b, carry):
        first_elem = b * block_elems
        clash = index_of(nloc, first_elem + block_elems - 1)
        add_rows(term_ref, accs, index_of, b * block_terms, first_elem, nloc, groups, clash)
        return carry

    live = count_ref[0]
    lax.fori_loop(0, (live + block_elems - 1) // block_elems, block, 0)

    masks = lane_masks(width, groups)
    folder = folder_of(width)
    wide = 2 * LANES
    many = 4

    def fold_own(c, carry):
        for u in range(many):
            at = pl.ds(pl.multiple_of((c * many + u) * wide, wide), wide)
            total = pick(masks, [acc[at, :] for acc in accs])
            total = dot_nt(folder, jnp.concatenate(split(total), axis=1))
            curl_ref[:, at] = total[:width]
            mass_ref[:, at] = total[width:]
        return carry

    lax.fori_loop(0, owned_len // (many * wide), fold_own, 0)


def on_device(
    trial_block,
    stiff_coef,
    mass_coef,
    elem_count,
    elem_dofs,
    pairing,
    bloch_fraction,
    stiff_ref,
    mass_ref,
):
    own_block = trial_block[0, 0]
    vecs, owned_len = own_block.shape[1:]
    face_len = pairing.shape[0]
    interior = owned_len - 2 * face_len
    width = 2 * vecs
    groups = LANES // (2 * width)
    capacity, nloc = elem_dofs.shape[2:]
    face_slots = capacity // 8
    devices = lax.axis_size("px") * lax.axis_size("py")
    own_rows = own_block.reshape(width, owned_len)
    low_x = own_rows[:, interior : interior + face_len]
    low_y = own_rows[:, interior + face_len :]
    high_x = lax.ppermute(low_x, "px", ring_route("px", -1))
    high_y = lax.ppermute(low_y, "py", line_route("py", -1))
    live = elem_count[0]
    table_rows = -(-(nloc + 1) // 8) * 8
    smem = pl.BlockSpec(memory_space=pltpu.SMEM)
    vmem = pl.BlockSpec(memory_space=pltpu.VMEM)
    left = pl.BlockSpec(memory_space=pl.ANY)

    table, own_table, face_table, scale, turn = pl.pallas_call(
        functools.partial(prepare_kernel, owned_len, face_len, width),
        out_shape=(
            jax.ShapeDtypeStruct((table_rows, capacity), jnp.int32),
            jax.ShapeDtypeStruct((table_rows, capacity), jnp.int32),
            jax.ShapeDtypeStruct((table_rows, face_slots), jnp.int32),
            jax.ShapeDtypeStruct((capacity // groups, LANES), F32),
            jax.ShapeDtypeStruct((16, LANES), F32),
        ),
        in_specs=[smem] * 2 + [vmem] * 4,
        out_specs=[vmem] * 5,
        name="prepare",
    )(
        live,
        bloch_fraction,
        elem_dofs[0, 0],
        pairing.reshape(-1, LANES),
        stiff_coef[0],
        mass_coef[0],
    )

    extent = owned_len + 2 * face_len
    limit = 32 * 1024 * 1024
    terms, side_x, side_y, gram = pl.pallas_call(
        functools.partial(term_kernel, width),
        out_shape=(
            jax.ShapeDtypeStruct((nloc * capacity // groups, LANES), F32),
            jax.ShapeDtypeStruct((2 * width, face_len), F32),
            jax.ShapeDtypeStruct((2 * width, face_len), F32),
            jax.ShapeDtypeStruct((devices, vecs, LANES), F32),
        ),
        in_specs=[smem] * 3 + [left] * 2 + [vmem] * 5,
        out_specs=[vmem] * 4,
        scratch_shapes=[
            pltpu.SMEM(((nloc + 1) * capacity,), jnp.int32),
            pltpu.SMEM((nloc * face_slots,), jnp.int32),
            pltpu.VMEM((nloc * nloc, BLOCK_ROWS, LANES), F32),
            pltpu.VMEM((extent, LANES), F32),
            pltpu.VMEM((nloc * BLOCK_ROWS, LANES), F32),
            pltpu.VMEM((LANES, LANES), F32),
            pltpu.SemaphoreType.DMA((nloc + 1,)),
            pltpu.SemaphoreType.DMA((nloc,)),
        ]
        + [pltpu.VMEM((2 * face_len + 8, LANES), F32)] * N_ACC,
        compiler_params=pltpu.CompilerParams(vmem_limit_bytes=limit),
        name="terms",
    )(
        live, stiff_ref, mass_ref, table, face_table, turn, own_rows, high_x, high_y, scale
    )

    gathered = lax.all_to_all(gram, ("px", "py"), 0, 0)
    back_x = lax.ppermute(side_x, "px", ring_route("px", 1))
    back_y = lax.ppermute(side_y, "py", line_route("py", 1))

    curl, mass = pl.pallas_call(
        functools.partial(add_kernel, width),
        out_shape=(
            jax.ShapeDtypeStruct((width, owned_len), F32),
            jax.ShapeDtypeStruct((width, owned_len), F32),
        ),
        in_specs=[smem, left, vmem],
        out_specs=[vmem] * 2,
        scratch_shapes=[
            pltpu.SMEM(((nloc + 1) * capacity,), jnp.int32),
            pltpu.SemaphoreType.DMA((nloc + 1,)),
        ]
        + [pltpu.VMEM((owned_len + 8, LANES), F32)] * N_ACC,
        compiler_params=pltpu.CompilerParams(vmem_limit_bytes=limit),
        cost_estimate=pl.CostEstimate(
            flops=40 * 1024 * 1024 * 1024, bytes_accessed=40 * 1024 * 1024, transcendentals=0
        ),
        name="adds",
    )(live, own_table, terms)

    def finish(image, part):
        add_x = back_x[part * width : (part + 1) * width]
        add_y = back_y[part * width : (part + 1) * width]
        whole = image.at[:, interior:].add(jnp.concatenate([add_x, add_y], axis=1))
        return whole.reshape(1, 1, 2, vecs, owned_len)

    total = jnp.sum(gathered, axis=0)[:, : 2 * width] / float(devices * owned_len)
    gram_out = total.reshape(vecs, 2, 2, vecs).transpose(1, 2, 0, 3)
    return (finish(curl, 0), finish(mass, 1), gram_out)


def solution(mesh):
    return jax.shard_map(
        on_device,
        mesh=mesh,
        in_specs=(
            P("px", "py", None, None, None),
            P("px", "py", None),
            P("px", "py", None),
            P("px", "py"),
            P("px", "py", None, None),
            P(),
            P(),
            P(),
            P(),
        ),
        out_specs=(P("px", "py", None, None, None), P("px", "py", None, None, None), P()),
        check_vma=False,
    )
```

```python
import functools
import math

import jax
import jax.numpy as jnp
from jax import lax
from jax.experimental import pallas as pl
from jax.experimental.pallas import tpu as pltpu
from jax.sharding import PartitionSpec as P

LANES = 128
BLOCK_ROWS = 8
STEP = 4
N_ACC = 4
F32 = jnp.float32
BF16 = jnp.bfloat16


def ring_route(axis, steps):
    count = lax.axis_size(axis)
    return [(source, (source + steps) % count) for source in range(count)]


def line_route(axis, distance):
    devices = range(lax.axis_size(axis))
    return [(i - distance, i) for i in devices if i - distance in devices]


def iota(shape, axis):
    return lax.broadcasted_iota(jnp.int32, shape, axis)


def split(x):
    top = x.astype(BF16)
    return top, (x - top.astype(F32)).astype(BF16)


def dot_nt(left, right):
    return lax.dot_general(
        left, right, (((1,), (1,)), ((), ())), preferred_element_type=F32
    )


def gather_lanes(table_ref, index):
    high = index // LANES
    low = index % LANES
    found = jnp.zeros_like(index)
    for r in range(table_ref.shape[0]):
        line = jnp.broadcast_to(table_ref[r : r + 1, :], index.shape)
        found = jnp.where(high == r, jnp.take_along_axis(line, low, axis=1), found)
    return found


def prepare_kernel(
    owned_len, face_len, width, count_ref, bloch_ref,
    dofs_ref, pair_ref, stiff_ref, mass_ref,
    table_ref, own_table_ref, face_table_ref, scale_ref, turn_ref,
):
    nloc, _, capacity = dofs_ref.shape
    face_slots = face_table_ref.shape[1]
    groups = LANES // (2 * width)
    at_end = lax.axis_index("px") == lax.axis_size("px") - 1
    live = count_ref[0]

    index = [dofs_ref[i] for i in range(nloc)]
    flag = jnp.zeros((1, capacity), jnp.int32)
    for i in range(nloc):
        for k in range(i + 1, min(i // STEP * STEP + STEP, nloc)):
            flag = jnp.where(index[i] == index[k], 1, flag)
    reach = groups * BLOCK_ROWS // 2
    while reach:
        flag = jnp.maximum(flag, pltpu.roll(flag, reach, 1))
        reach //= 2
    table_ref[nloc] = flag
    own_table_ref[nloc] = flag
    for i in range(nloc):
        table_ref[i] = index[i]
        own_table_ref[i] = jnp.minimum(index[i], owned_len)

    pad = face_table_ref.shape[0] - nloc
    for c in range(0, face_slots, LANES):
        at = slice(c, c + LANES)
        first = jnp.concatenate(
            [row[:, at] for row in index] + [jnp.zeros((pad, LANES), jnp.int32)], axis=0
        )
        local = first - owned_len
        on_face = at_end & (local >= 0) & (local < face_len)
        paired = gather_lanes(pair_ref, jnp.where(on_face, local, 0))
        first = jnp.where(on_face, paired + owned_len, first)
        face_table_ref[:, at] = jnp.where(first >= owned_len, first - owned_len, 2 * face_len)
        for i in range(nloc):
            table_ref[i, :, at] = first[i : i + 1]

    per_chunk = LANES // groups
    lane_of = iota((LANES, LANES), 0)
    elem_of = iota((LANES, LANES), 1)
    mine = elem_of % groups == lane_of // (2 * width)
    is_curl = lane_of // width % 2 == 0
    chooser = (iota((per_chunk, LANES), 1) // groups == iota((per_chunk, LANES), 0)).astype(BF16)
    chooser = jnp.concatenate([chooser, chooser], axis=1)
    for c in range(capacity // LANES):
        at = slice(c * LANES, (c + 1) * LANES)
        scales = jnp.where(is_curl, stiff_ref[:, at], mass_ref[:, at])
        scales = jnp.where(mine & (c * LANES + elem_of < live), scales, 0.0)
        scale_ref[c * per_chunk : (c + 1) * per_chunk, :] = dot_nt(
            chooser, jnp.concatenate(split(scales), axis=1)
        )

    ratio = jnp.full((8, LANES), bloch_ref[0].astype(F32), F32) / bloch_ref[1].astype(F32)
    angle = (2.0 * math.pi) * jnp.where(at_end, ratio, 0.0)
    turn_ref[:8] = jnp.cos(angle)
    turn_ref[8:] = jnp.sin(angle)


def lane_masks(width, groups):
    lane = iota((1, LANES), 1) // (2 * width)
    return [lane == k for k in range(groups)]


def pick(masks, parts):
    out = parts[-1]
    for mask, part in zip(masks[-2::-1], parts[-2::-1]):
        out = jnp.where(mask, part, out)
    return out


def folder_of(width):
    rows = 2 * width
    folder = (iota((rows, LANES), 1) % rows == iota((rows, LANES), 0)).astype(BF16)
    return jnp.concatenate([folder, folder], axis=1)


def add_rows(term_ref, accs, index_of, first_row, first_elem, nloc, groups, clash):
    unroll = 2

    def run(step):
        def some(t, c):
            for u in range(unroll):
                g = t * unroll + u
                elem = first_elem + g * groups
                for j in range(0, nloc, step):
                    slots = range(j, min(j + step, nloc))
                    new = [term_ref[pl.ds(first_row + s * BLOCK_ROWS + g, 1), :] for s in slots]
                    for k in range(groups):
                        places = [pl.ds(index_of(s, elem + k), 1) for s in slots]
                        sums = [accs[k][at, :] + row for at, row in zip(places, new)]
                        for at, row in zip(places, sums):
                            accs[k][at, :] = row
            return c

        lax.fori_loop(0, BLOCK_ROWS // unroll, some, 0)

    @pl.when(clash == 0)
    def _():
        run(STEP)

    @pl.when(clash != 0)
    def _():
        run(1)


def term_kernel(
    width,
    count_ref,
    stiff_ref,
    mass_ref,
    table_hbm,
    face_table_hbm,
    turn_ref,
    own_ref,
    high_x_ref,
    high_y_ref,
    scale_ref,
    term_hbm,
    side_x_ref,
    side_y_ref,
    gram_ref,
    dofs_ref,
    face_dofs_ref,
    term_ref,
    coef_ref,
    rows_x,
    gath,
    gram_acc,
    sems,
    term_sems,
    *accs,
):
    owned_len = own_ref.shape[1]
    face_len = high_x_ref.shape[1]
    vecs = width // 2
    groups = LANES // (2 * width)
    capacity = scale_ref.shape[0] * groups
    nloc = stiff_ref.shape[0]
    face_slots = capacity // 8
    copies = LANES // width
    block_elems = groups * BLOCK_ROWS
    block_terms = nloc * BLOCK_ROWS

    loads = [
        pltpu.make_async_copy(table_hbm, dofs_ref, sems.at[0]),
        pltpu.make_async_copy(face_table_hbm, face_dofs_ref, sems.at[1]),
    ]
    for load in loads:
        load.start()

    cos, sin = turn_ref[:vecs], turn_ref[8 : 8 + vecs]

    def turned(pair, sign):
        n = pair.shape[1] // LANES
        c = jnp.concatenate([cos] * n, axis=1)
        s = jnp.concatenate([sin] * n, axis=1) * sign
        a, b = pair[:vecs], pair[vecs:]
        return jnp.concatenate([c * a - s * b, s * a + c * b], axis=0)

    unit = (iota((LANES, LANES), 0) == iota((LANES, LANES), 1)).astype(BF16)
    unit = jnp.concatenate([unit, unit], axis=1)
    zero_tile = jnp.zeros((LANES, LANES), F32)

    def put_rows(tile, first):
        top, low = split(tile)
        tiled = jnp.concatenate(
            [jnp.concatenate([top] * copies, axis=0), jnp.concatenate([low] * copies, axis=0)],
            axis=1,
        )
        rows_x[pl.ds(first, LANES), :] = dot_nt(unit, tiled)

    many = 8

    def build_own(c, carry):
        for u in range(many):
            first = pl.multiple_of((c * many + u) * LANES, LANES)
            put_rows(own_ref[:, pl.ds(first, LANES)], first)
        return carry

    lax.fori_loop(0, owned_len // (many * LANES), build_own, 0)

    def build_face(c, carry):
        for u in range(many // 2):
            first = pl.multiple_of((c * (many // 2) + u) * LANES, LANES)
            put_rows(
                turned(high_x_ref[:, pl.ds(first, LANES)], 1.0),
                pl.multiple_of(owned_len + first, LANES),
            )
            put_rows(
                high_y_ref[:, pl.ds(first, LANES)],
                pl.multiple_of(owned_len + face_len + first, LANES),
            )
            for acc in accs:
                acc[pl.ds(pl.multiple_of(2 * first, 2 * LANES), LANES), :] = zero_tile
                acc[pl.ds(pl.multiple_of(2 * first + LANES, LANES), LANES), :] = zero_tile
        return carry

    lax.fori_loop(0, face_len // (many // 2 * LANES), build_face, 0)

    curl_lane = iota((BLOCK_ROWS, LANES), 1) // width % 2 == 0

    def build_coef(j, carry):
        for i in range(nloc):
            coef_ref[j * nloc + i] = jnp.where(curl_lane, stiff_ref[j, i], mass_ref[j, i])
        return carry

    lax.fori_loop(0, nloc, build_coef, 0)
    gath[...] = jnp.zeros_like(gath)
    gram_acc[...] = jnp.zeros_like(gram_acc)

    for load in loads:
        load.wait()

    masks = lane_masks(width, groups)

    def index_of(i, elem):
        return dofs_ref.at[pl.ds(i * capacity, capacity)][elem]

    def face_index_of(i, elem):
        return face_dofs_ref.at[pl.ds(i * face_slots, face_slots)][elem]

    unroll = 2
    steps = BLOCK_ROWS // unroll
    part = nloc // steps

    def block(b, gather):
        here = pl.multiple_of(lax.rem(b, 2) * block_terms, BLOCK_ROWS)
        there = pl.multiple_of(block_terms - here, BLOCK_ROWS)
        behind = jnp.maximum(b - 1, 0)
        scale_at = pl.ds(pl.multiple_of(behind * BLOCK_ROWS, BLOCK_ROWS), BLOCK_ROWS)
        first_term = pl.multiple_of(behind * block_terms, BLOCK_ROWS)
        first_elem = b * block_elems

        def step(t, c):
            first_row = pl.multiple_of(there + t * part * BLOCK_ROWS, BLOCK_ROWS)
            left, left_low = split(gath[pl.ds(first_row, part * BLOCK_ROWS), :])
            scale = scale_ref[scale_at, :]
            values = [
                gath[pl.ds(pl.multiple_of(there + i * BLOCK_ROWS, BLOCK_ROWS), BLOCK_ROWS), :]
                for i in range(nloc)
            ]
            made = []
            for q in range(part):
                j = t * part + q
                total = coef_ref[j * nloc] * values[0]
                for i in range(1, nloc):
                    total = total + coef_ref[j * nloc + i] * values[i]
                total = total * scale
                at = pl.multiple_of(first_term + j * BLOCK_ROWS, BLOCK_ROWS)
                term_ref[pl.ds(at, BLOCK_ROWS), :] = total
                made.append(total)
            right, right_low = split(jnp.concatenate(made, axis=0))
            gram_acc[...] += lax.dot_general(
                jnp.concatenate([left, left, left_low], axis=0),
                jnp.concatenate([right, right_low, right], axis=0),
                (((0,), (0,)), ((), ())),
                preferred_element_type=F32,
            )
            if gather:
                for u in range(unroll):
                    g = t * unroll + u
                    elem = first_elem + g * groups
                    for i in range(nloc):
                        rows = [
                            rows_x[pl.ds(index_of(i, elem + k), 1), :] for k in range(groups)
                        ]
                        gath[pl.ds(here + i * BLOCK_ROWS + g, 1), :] = pick(masks, rows)
            return c

        lax.fori_loop(0, steps, step, 0)

    def send(b):
        at = pl.ds(pl.multiple_of(b * block_terms, BLOCK_ROWS), block_terms)
        return pltpu.make_async_copy(term_ref.at[at], term_hbm.at[at], term_sems.at[b])

    def face_block(b, carry):
        first_elem = b * block_elems
        clash = index_of(nloc, first_elem + block_elems - 1)
        add_rows(
            term_ref, accs, face_index_of, b * block_terms, first_elem, nloc, groups, clash
        )
        return carry

    live = count_ref[0]
    blocks = (live + block_elems - 1) // block_elems
    face_blocks = jnp.minimum(blocks, face_slots // block_elems)
    def full_block(b, carry):
        block(b, True)

        @pl.when(b > 0)
        def _():
            send(b - 1).start()

        return carry

    lax.fori_loop(0, blocks, full_block, 0)
    block(blocks, False)
    send(blocks - 1).start()
    lax.fori_loop(0, face_blocks, face_block, 0)

    folder = folder_of(width)
    wide = 2 * LANES

    def folded(first):
        at = pl.ds(first, wide)
        total = pick(masks, [acc[at, :] for acc in accs])
        return dot_nt(folder, jnp.concatenate(split(total), axis=1))

    def fold_face(c, carry):
        for u in range(2):
            first = pl.multiple_of((2 * c + u) * wide, wide)
            at = pl.ds(first, wide)
            total = folded(first)
            side_x_ref[:width, at] = turned(total[:width], -1.0)
            side_x_ref[width:, at] = turned(total[width:], -1.0)
            side_y_ref[:, at] = folded(pl.multiple_of(face_len + first, wide))
        return carry

    lax.fori_loop(0, face_len // (2 * wide), fold_face, 0)

    whole = gram_acc[...]
    total = whole[:width]
    for k in range(1, groups):
        part = whole[2 * width * k : 2 * width * k + width]
        total = total + pltpu.roll(part, LANES - 2 * width * k, 1)
    re_left, im_left = total[:vecs], total[vecs:]
    lane = iota((vecs, LANES), 1)
    real_here = lane // vecs % 2 == 0
    swapped = jnp.where(
        real_here, pltpu.roll(im_left, LANES - vecs, 1), -pltpu.roll(im_left, vecs, 1)
    )
    joined = re_left + swapped
    for n in range(gram_ref.shape[0]):
        gram_ref[n] = joined

    def sent(b, carry):
        send(b).wait()
        return carry

    lax.fori_loop(0, blocks, sent, 0)


def add_kernel(
    width, nloc, interior, count_ref, table_hbm, term_hbm, curl_hbm, mass_hbm, face_ref,
    dofs_ref, term_ref, images, sem, term_sems, out_sems, *accs
):
    owned_len = curl_hbm.shape[1]
    groups = LANES // (2 * width)
    capacity = term_ref.shape[0] // nloc * groups
    block_elems = groups * BLOCK_ROWS
    block_terms = nloc * BLOCK_ROWS
    load = pltpu.make_async_copy(table_hbm, dofs_ref, sem)
    load.start()
    live = count_ref[0]
    blocks = (live + block_elems - 1) // block_elems

    def fetch(b):
        at = pl.ds(pl.multiple_of(b * block_terms, BLOCK_ROWS), block_terms)
        return pltpu.make_async_copy(term_hbm.at[at], term_ref.at[at], term_sems.at[b])

    def fetch_all(b, carry):
        fetch(b).start()
        return carry

    lax.fori_loop(0, blocks, fetch_all, 0)
    many = 4
    zero_tile = jnp.zeros((many * LANES, LANES), F32)

    def clear(c, carry):
        at = pl.ds(pl.multiple_of(c * many * LANES, LANES), many * LANES)
        for acc in accs:
            acc[at, :] = zero_tile
        return carry

    lax.fori_loop(0, owned_len // (many * LANES), clear, 0)
    load.wait()

    def index_of(i, elem):
        return dofs_ref.at[pl.ds(i * capacity, capacity)][elem]

    def block(b, carry):
        first_elem = b * block_elems
        clash = index_of(nloc, first_elem + block_elems - 1)
        fetch(b).wait()
        add_rows(term_ref, accs, index_of, b * block_terms, first_elem, nloc, groups, clash)
        return carry

    lax.fori_loop(0, blocks, block, 0)

    masks = lane_masks(width, groups)
    folder = folder_of(width)
    wide = 2 * LANES
    many = 4
    span = many * wide

    def fold_some(first, curl, mass):
        for u in range(many):
            at = pl.ds(pl.multiple_of(first + u * wide, wide), wide)
            total = pick(masks, [acc[at, :] for acc in accs])
            total = dot_nt(folder, jnp.concatenate(split(total), axis=1))
            to = slice(u * wide, (u + 1) * wide)
            curl[:, to] = total[:width]
            mass[:, to] = total[width:]

    moves = []
    for c in range(owned_len // span):
        at = pl.ds(c * span, span)
        if c * span < interior:
            fold_some(c * span, images.at[0, :, at], images.at[1, :, at])
            for n, image in enumerate((curl_hbm, mass_hbm)):
                moves.append(
                    pltpu.make_async_copy(
                        images.at[n, :, at], image.at[:, at], out_sems.at[2 * c + n]
                    )
                )
                moves[-1].start()
        else:
            at = pl.ds(c * span - interior, span)
            fold_some(c * span, face_ref.at[0, :, at], face_ref.at[1, :, at])
    for move in moves:
        move.wait()


def finish_kernel(
    width, scale, curl_in, mass_in, face_ref, back_x_ref, back_y_ref, gram_ref,
    curl_out, mass_out, gram_out, faces, sems,
):
    del curl_in, mass_in
    face_len = back_x_ref.shape[1]
    outer = pl.ds(curl_out.shape[1] - 2 * face_len, 2 * face_len)
    moves = []
    for n, image in enumerate((curl_out, mass_out)):
        rows = slice(n * width, (n + 1) * width)
        faces[n, :, :face_len] = face_ref[n, :, :face_len] + back_x_ref[rows, :]
        faces[n, :, face_len:] = face_ref[n, :, face_len:] + back_y_ref[rows, :]
        moves.append(pltpu.make_async_copy(faces.at[n], image.at[:, outer], sems.at[n]))
        moves[-1].start()
    total = gram_ref[0]
    for d in range(1, gram_ref.shape[0]):
        total = total + gram_ref[d]
    total = total * scale
    vecs = total.shape[0]
    for q in range(4):
        shifted = total if q == 0 else pltpu.roll(total, LANES - q * vecs, 1)
        gram_out[q * vecs : (q + 1) * vecs, :] = shifted[:, :vecs]
    for move in moves:
        move.wait()


def on_device(
    trial_block,
    stiff_coef,
    mass_coef,
    elem_count,
    elem_dofs,
    pairing,
    bloch_fraction,
    stiff_ref,
    mass_ref,
):
    own_block = trial_block[0, 0]
    vecs, owned_len = own_block.shape[1:]
    face_len = pairing.shape[0]
    interior = owned_len - 2 * face_len
    width = 2 * vecs
    groups = LANES // (2 * width)
    capacity, nloc = elem_dofs.shape[2:]
    face_slots = capacity // 8
    devices = lax.axis_size("px") * lax.axis_size("py")
    own_rows = own_block.reshape(width, owned_len)
    low_x = own_rows[:, interior : interior + face_len]
    low_y = own_rows[:, interior + face_len :]
    high_x = lax.ppermute(low_x, "px", ring_route("px", -1))
    high_y = lax.ppermute(low_y, "py", line_route("py", -1))
    live = elem_count[0]
    smem = pl.BlockSpec(memory_space=pltpu.SMEM)
    vmem = pl.BlockSpec(memory_space=pltpu.VMEM)
    left = pl.BlockSpec(memory_space=pl.ANY)

    limit = 62 * 1024 * 1024
    params = pltpu.CompilerParams(vmem_limit_bytes=limit)
    table, own_table, face_table, scale, turn = pl.pallas_call(
        functools.partial(prepare_kernel, owned_len, face_len, width),
        out_shape=(
            jax.ShapeDtypeStruct((nloc + 1, 1, capacity), jnp.int32),
            jax.ShapeDtypeStruct((nloc + 1, 1, capacity), jnp.int32),
            jax.ShapeDtypeStruct((-(-nloc // 8) * 8, face_slots), jnp.int32),
            jax.ShapeDtypeStruct((capacity // groups, LANES), F32),
            jax.ShapeDtypeStruct((16, LANES), F32),
        ),
        in_specs=[smem] * 2 + [vmem] * 4,
        out_specs=[vmem] * 5,
        compiler_params=params,
        name="prepare",
    )(
        live,
        bloch_fraction,
        elem_dofs.transpose(0, 3, 1, 2).reshape(nloc, 1, capacity),
        pairing.reshape(-1, LANES),
        stiff_coef[0],
        mass_coef[0],
    )
    table = table.reshape(-1)
    own_table = own_table.reshape(-1)
    face_table = face_table.reshape(-1)

    extent = owned_len + 2 * face_len
    blocks = capacity // (groups * BLOCK_ROWS)
    term_rows = nloc * capacity // groups
    terms, side_x, side_y, gram = pl.pallas_call(
        functools.partial(term_kernel, width),
        out_shape=(
            jax.ShapeDtypeStruct((term_rows, LANES), F32),
            jax.ShapeDtypeStruct((2 * width, face_len), F32),
            jax.ShapeDtypeStruct((2 * width, face_len), F32),
            jax.ShapeDtypeStruct((devices, vecs, LANES), F32),
        ),
        in_specs=[smem] * 3 + [left] * 2 + [vmem] * 5,
        out_specs=[left] + [vmem] * 3,
        scratch_shapes=[
            pltpu.SMEM(table.shape, jnp.int32),
            pltpu.SMEM(face_table.shape, jnp.int32),
            pltpu.VMEM((term_rows, LANES), F32),
            pltpu.VMEM((nloc * nloc, BLOCK_ROWS, LANES), F32),
            pltpu.VMEM((extent, LANES), F32),
            pltpu.VMEM((2 * nloc * BLOCK_ROWS, LANES), F32),
            pltpu.VMEM((LANES, LANES), F32),
            pltpu.SemaphoreType.DMA((2,)),
            pltpu.SemaphoreType.DMA((blocks,)),
        ]
        + [pltpu.VMEM((2 * face_len + 8, LANES), F32)] * N_ACC,
        compiler_params=pltpu.CompilerParams(vmem_limit_bytes=60 * 1024 * 1024),
        name="terms",
    )(
        live, stiff_ref, mass_ref, table, face_table, turn, own_rows, high_x, high_y, scale
    )

    gathered = lax.all_to_all(gram, ("px", "py"), 0, 0)
    back_x = lax.ppermute(side_x, "px", ring_route("px", 1))
    back_y = lax.ppermute(side_y, "py", line_route("py", 1))

    curl, mass, faces = pl.pallas_call(
        functools.partial(add_kernel, width, nloc, interior),
        out_shape=(
            jax.ShapeDtypeStruct((width, owned_len), F32),
            jax.ShapeDtypeStruct((width, owned_len), F32),
            jax.ShapeDtypeStruct((2, width, 2 * face_len), F32),
        ),
        in_specs=[smem, left, left],
        out_specs=[left, left, vmem],
        scratch_shapes=[
            pltpu.SMEM(own_table.shape, jnp.int32),
            pltpu.VMEM((term_rows, LANES), F32),
            pltpu.VMEM((2, width, interior), F32),
            pltpu.SemaphoreType.DMA,
            pltpu.SemaphoreType.DMA((blocks,)),
            pltpu.SemaphoreType.DMA((2 * owned_len // (8 * LANES),)),
        ]
        + [pltpu.VMEM((owned_len + 8, LANES), F32)] * N_ACC,
        compiler_params=params,
        cost_estimate=pl.CostEstimate(
            flops=40 * 1024 * 1024 * 1024, bytes_accessed=40 * 1024 * 1024, transcendentals=0
        ),
        name="adds",
    )(live, own_table, terms)

    curl, mass, gram = pl.pallas_call(
        functools.partial(finish_kernel, width, 1.0 / float(devices * owned_len)),
        out_shape=(
            jax.ShapeDtypeStruct((width, owned_len), F32),
            jax.ShapeDtypeStruct((width, owned_len), F32),
            jax.ShapeDtypeStruct((4 * vecs, vecs), F32),
        ),
        in_specs=[left] * 2 + [vmem] * 4,
        out_specs=[left, left, vmem],
        scratch_shapes=[
            pltpu.VMEM((2, width, 2 * face_len), F32),
            pltpu.SemaphoreType.DMA((2,)),
        ],
        input_output_aliases={0: 0, 1: 1},
        compiler_params=pltpu.CompilerParams(vmem_limit_bytes=8 * 1024 * 1024),
        name="finish",
    )(curl, mass, faces, back_x, back_y, gathered)
    shape = (1, 1, 2, vecs, owned_len)
    return curl.reshape(shape), mass.reshape(shape), gram.reshape(2, 2, vecs, vecs)


def solution(mesh):
    return jax.shard_map(
        on_device,
        mesh=mesh,
        in_specs=(
            P("px", "py", None, None, None),
            P("px", "py", None),
            P("px", "py", None),
            P("px", "py"),
            P("px", "py", None, None),
            P(),
            P(),
            P(),
            P(),
        ),
        out_specs=(P("px", "py", None, None, None), P("px", "py", None, None, None), P()),
        check_vma=False,
    )
```

```python
import functools
import math

import jax
import jax.numpy as jnp
from jax import lax
from jax.experimental import pallas as pl
from jax.experimental.pallas import tpu as pltpu
from jax.sharding import PartitionSpec as P

LANES = 128
BLOCK_ROWS = 16
SUB_ROWS = 8
STEP = 4
DEEP = 4
N_ACC = 4
F32 = jnp.float32
BF16 = jnp.bfloat16


def ring_route(axis, steps):
    count = lax.axis_size(axis)
    return [(source, (source + steps) % count) for source in range(count)]


def line_route(axis, distance):
    devices = range(lax.axis_size(axis))
    return [(i - distance, i) for i in devices if i - distance in devices]


def iota(shape, axis):
    return lax.broadcasted_iota(jnp.int32, shape, axis)


def split(x):
    top = x.astype(BF16)
    return top, (x - top.astype(F32)).astype(BF16)


def dot_nt(left, right):
    return lax.dot_general(
        left, right, (((1,), (1,)), ((), ())), preferred_element_type=F32
    )


def gather_lanes(table_ref, index):
    high = index // LANES
    low = index % LANES
    found = jnp.zeros_like(index)
    for r in range(table_ref.shape[0]):
        line = jnp.broadcast_to(table_ref[r : r + 1, :], index.shape)
        found = jnp.where(high == r, jnp.take_along_axis(line, low, axis=1), found)
    return found


def prepare_kernel(
    owned_len, face_len, width, count_ref, bloch_ref,
    dofs_ref, pair_ref, stiff_ref, mass_ref,
    table_ref, own_table_ref, face_table_ref, scale_ref, turn_ref,
):
    nloc, _, capacity = dofs_ref.shape
    face_slots = face_table_ref.shape[1]
    groups = LANES // (2 * width)
    at_end = lax.axis_index("px") == lax.axis_size("px") - 1
    live = count_ref[0]

    index = [dofs_ref[i] for i in range(nloc)]
    flag = jnp.zeros((1, capacity), jnp.int32)
    for i in range(nloc):
        for k in range(i + 1, min(i // STEP * STEP + STEP, nloc)):
            flag = jnp.where(index[i] == index[k], 1, flag)
    reach = groups * SUB_ROWS // 2
    while reach:
        flag = jnp.maximum(flag, pltpu.roll(flag, reach, 1))
        reach //= 2
    table_ref[nloc] = flag
    own_table_ref[nloc] = flag
    for i in range(nloc):
        table_ref[i] = index[i]
        own_table_ref[i] = jnp.minimum(index[i], owned_len)

    pad = face_table_ref.shape[0] - nloc
    for c in range(0, face_slots, LANES):
        at = slice(c, c + LANES)
        first = jnp.concatenate(
            [row[:, at] for row in index] + [jnp.zeros((pad, LANES), jnp.int32)], axis=0
        )
        local = first - owned_len
        on_face = at_end & (local >= 0) & (local < face_len)
        paired = gather_lanes(pair_ref, jnp.where(on_face, local, 0))
        first = jnp.where(on_face, paired + owned_len, first)
        face_table_ref[:, at] = jnp.where(first >= owned_len, first - owned_len, 2 * face_len)
        for i in range(nloc):
            table_ref[i, :, at] = first[i : i + 1]

    per_chunk = LANES // groups
    lane_of = iota((LANES, LANES), 0)
    elem_of = iota((LANES, LANES), 1)
    mine = elem_of % groups == lane_of // (2 * width)
    is_curl = lane_of // width % 2 == 0
    chooser = (iota((per_chunk, LANES), 1) // groups == iota((per_chunk, LANES), 0)).astype(BF16)
    chooser = jnp.concatenate([chooser, chooser], axis=1)
    for c in range(capacity // LANES):
        at = slice(c * LANES, (c + 1) * LANES)
        scales = jnp.where(is_curl, stiff_ref[:, at], mass_ref[:, at])
        scales = jnp.where(mine & (c * LANES + elem_of < live), scales, 0.0)
        scale_ref[c * per_chunk : (c + 1) * per_chunk, :] = dot_nt(
            chooser, jnp.concatenate(split(scales), axis=1)
        )

    ratio = jnp.full((8, LANES), bloch_ref[0].astype(F32), F32) / bloch_ref[1].astype(F32)
    angle = (2.0 * math.pi) * jnp.where(at_end, ratio, 0.0)
    turn_ref[:8] = jnp.cos(angle)
    turn_ref[8:] = jnp.sin(angle)


def lane_masks(width, groups):
    lane = iota((1, LANES), 1) // (2 * width)
    return [lane == k for k in range(groups)]


def pick(masks, parts):
    out = parts[-1]
    for mask, part in zip(masks[-2::-1], parts[-2::-1]):
        out = jnp.where(mask, part, out)
    return out


def folder_of(width):
    rows = 2 * width
    folder = (iota((rows, LANES), 1) % rows == iota((rows, LANES), 0)).astype(BF16)
    return jnp.concatenate([folder, folder], axis=1)


def add_block(term_ref, accs, index_of, b, nloc, groups):
    unroll = 2

    def run(step, first_row, first_elem):
        def some(t, c):
            for u in range(unroll):
                g = t * unroll + u
                elem = first_elem + g * groups
                for j in range(0, nloc, step):
                    slots = range(j, min(j + step, nloc))
                    new = [term_ref[pl.ds(first_row + s * BLOCK_ROWS + g, 1), :] for s in slots]
                    for k in range(groups):
                        places = [pl.ds(index_of[0](s, elem + k), 1) for s in slots]
                        sums = [accs[k][at, :] + row for at, row in zip(places, new)]
                        for at, row in zip(places, sums):
                            accs[k][at, :] = row
            return c

        lax.fori_loop(0, SUB_ROWS // unroll, some, 0)

    def part(h, carry):
        first_row = b * nloc * BLOCK_ROWS + h * SUB_ROWS
        first_elem = (b * (BLOCK_ROWS // SUB_ROWS) + h) * SUB_ROWS * groups
        clash = index_of[1](nloc, first_elem + SUB_ROWS * groups - 1)

        @pl.when(clash == 0)
        def _():
            run(STEP, first_row, first_elem)

        @pl.when(clash != 0)
        def _():
            run(1, first_row, first_elem)

        return carry

    index_of = index_of if isinstance(index_of, tuple) else (index_of, index_of)
    lax.fori_loop(0, BLOCK_ROWS // SUB_ROWS, part, 0)


def term_kernel(
    width,
    count_ref,
    stiff_ref,
    mass_ref,
    table_hbm,
    face_table_hbm,
    turn_ref,
    own_ref,
    high_x_ref,
    high_y_ref,
    scale_ref,
    term_hbm,
    side_x_ref,
    side_y_ref,
    gram_ref,
    dofs_ref,
    face_dofs_ref,
    term_ref,
    coef_ref,
    rows_x,
    gath,
    gram_acc,
    sems,
    term_sems,
    *accs,
):
    owned_len = own_ref.shape[1]
    face_len = high_x_ref.shape[1]
    vecs = width // 2
    groups = LANES // (2 * width)
    capacity = scale_ref.shape[0] * groups
    nloc = stiff_ref.shape[0]
    face_slots = capacity // 8
    copies = LANES // width
    block_elems = groups * BLOCK_ROWS
    block_terms = nloc * BLOCK_ROWS

    loads = [
        pltpu.make_async_copy(table_hbm, dofs_ref, sems.at[0]),
        pltpu.make_async_copy(face_table_hbm, face_dofs_ref, sems.at[1]),
    ]
    for load in loads:
        load.start()

    cos, sin = turn_ref[:vecs], turn_ref[8 : 8 + vecs]

    def turned(pair, sign):
        n = pair.shape[1] // LANES
        c = jnp.concatenate([cos] * n, axis=1)
        s = jnp.concatenate([sin] * n, axis=1) * sign
        a, b = pair[:vecs], pair[vecs:]
        return jnp.concatenate([c * a - s * b, s * a + c * b], axis=0)

    unit = (iota((LANES, LANES), 0) == iota((LANES, LANES), 1)).astype(BF16)
    unit = jnp.concatenate([unit, unit], axis=1)
    zero_tile = jnp.zeros((LANES, LANES), F32)

    def put_rows(tile, first):
        top, low = split(tile)
        tiled = jnp.concatenate(
            [jnp.concatenate([top] * copies, axis=0), jnp.concatenate([low] * copies, axis=0)],
            axis=1,
        )
        rows_x[pl.ds(first, LANES), :] = dot_nt(unit, tiled)

    many = 8

    def build_own(c, carry):
        for u in range(many):
            first = pl.multiple_of((c * many + u) * LANES, LANES)
            put_rows(own_ref[:, pl.ds(first, LANES)], first)
        return carry

    lax.fori_loop(0, owned_len // (many * LANES), build_own, 0)

    def build_face(c, carry):
        for u in range(many // 2):
            first = pl.multiple_of((c * (many // 2) + u) * LANES, LANES)
            put_rows(
                turned(high_x_ref[:, pl.ds(first, LANES)], 1.0),
                pl.multiple_of(owned_len + first, LANES),
            )
            put_rows(
                high_y_ref[:, pl.ds(first, LANES)],
                pl.multiple_of(owned_len + face_len + first, LANES),
            )
            for acc in accs:
                acc[pl.ds(pl.multiple_of(2 * first, 2 * LANES), LANES), :] = zero_tile
                acc[pl.ds(pl.multiple_of(2 * first + LANES, LANES), LANES), :] = zero_tile
        return carry

    lax.fori_loop(0, face_len // (many // 2 * LANES), build_face, 0)

    curl_lane = iota((8, LANES), 1) // width % 2 == 0

    def build_coef(j, carry):
        for i in range(nloc):
            coef_ref[j * nloc + i] = jnp.where(curl_lane, stiff_ref[j, i], mass_ref[j, i])
        return carry

    lax.fori_loop(0, nloc, build_coef, 0)
    gram_acc[...] = jnp.zeros_like(gram_acc)

    for load in loads:
        load.wait()

    masks = lane_masks(width, groups)

    def index_of(i, elem):
        return dofs_ref.at[pl.ds(i * capacity, capacity)][elem]

    def face_index_of(i, elem):
        return face_dofs_ref.at[pl.ds(i * face_slots, face_slots)][elem]

    unroll = 4
    steps = BLOCK_ROWS // unroll
    halves = range(0, BLOCK_ROWS, 8)
    part = nloc // steps

    def block(b, gather):
        behind = jnp.maximum(b - 1, 0)
        here = pl.multiple_of(b * block_terms, BLOCK_ROWS)
        there = pl.multiple_of(behind * block_terms, BLOCK_ROWS)
        first_term = pl.multiple_of(behind * block_terms, BLOCK_ROWS)
        first_elem = b * block_elems

        def step(t, c):
            totals = [[None] * len(halves) for _ in range(part)]
            for i in range(nloc):
                if gather:
                    for u in range(unroll):
                        g = t * unroll + u
                        elem = first_elem + g * groups
                        rows = [
                            rows_x[pl.ds(index_of(i, elem + k), 1), :] for k in range(groups)
                        ]
                        gath[pl.ds(here + i * BLOCK_ROWS + g, 1), :] = pick(masks, rows)
                values = [
                    gath[pl.ds(pl.multiple_of(there + i * BLOCK_ROWS + h, 8), 8), :] for h in halves
                ]
                for q in range(part):
                    coef = coef_ref[(t * part + q) * nloc + i]
                    for n, value in enumerate(values):
                        product = coef * value
                        totals[q][n] = product if i == 0 else totals[q][n] + product
            for n, h in enumerate(halves):
                scale = scale_ref[pl.ds(pl.multiple_of(behind * BLOCK_ROWS + h, 8), 8), :]
                for q in range(part):
                    at = first_term + (t * part + q) * BLOCK_ROWS + h
                    term_ref[pl.ds(pl.multiple_of(at, 8), 8), :] = totals[q][n] * scale
            return c

        lax.fori_loop(0, steps, step, 0)

    def send(b):
        at = pl.ds(pl.multiple_of(b * block_terms, BLOCK_ROWS), block_terms)
        return pltpu.make_async_copy(term_ref.at[at], term_hbm.at[at], term_sems.at[b])

    def face_block(b, carry):
        add_block(term_ref, accs, (face_index_of, index_of), b, nloc, groups)
        return carry

    live = count_ref[0]
    blocks = (live + block_elems - 1) // block_elems
    face_blocks = jnp.minimum(blocks, face_slots // block_elems)
    def full_block(b, carry):
        block(b, True)

        @pl.when(b > 0)
        def _():
            send(b - 1).start()

        return carry

    lax.fori_loop(0, blocks, full_block, 0)
    block(blocks, False)
    send(blocks - 1).start()
    lax.fori_loop(0, face_blocks, face_block, 0)

    deep = DEEP * block_terms
    zero_block = jnp.zeros((block_terms, LANES), F32)
    chunks = (blocks + DEEP - 1) // DEEP

    def blank(b, carry):
        at = pl.ds(pl.multiple_of(b * block_terms, BLOCK_ROWS), block_terms)
        gath[at, :] = zero_block
        term_ref[at, :] = zero_block
        return carry

    lax.fori_loop(blocks, chunks * DEEP, blank, 0)

    def products(c, carry):
        at = pl.ds(pl.multiple_of(c * deep, BLOCK_ROWS), deep)
        left, left_low = split(gath[at, :])
        right, right_low = split(term_ref[at, :])
        gram_acc[...] += lax.dot_general(
            jnp.concatenate([left, left, left_low], axis=0),
            jnp.concatenate([right, right_low, right], axis=0),
            (((0,), (0,)), ((), ())),
            preferred_element_type=F32,
        )
        return carry

    lax.fori_loop(0, chunks, products, 0)
    folder = folder_of(width)
    wide = 2 * LANES

    def folded(first):
        at = pl.ds(first, wide)
        total = pick(masks, [acc[at, :] for acc in accs])
        return dot_nt(folder, jnp.concatenate(split(total), axis=1))

    def fold_face(c, carry):
        for u in range(2):
            first = pl.multiple_of((2 * c + u) * wide, wide)
            at = pl.ds(first, wide)
            total = folded(first)
            side_x_ref[:width, at] = turned(total[:width], -1.0)
            side_x_ref[width:, at] = turned(total[width:], -1.0)
            side_y_ref[:, at] = folded(pl.multiple_of(face_len + first, wide))
        return carry

    lax.fori_loop(0, face_len // (2 * wide), fold_face, 0)

    whole = gram_acc[...]
    total = whole[:width]
    for k in range(1, groups):
        part = whole[2 * width * k : 2 * width * k + width]
        total = total + pltpu.roll(part, LANES - 2 * width * k, 1)
    re_left, im_left = total[:vecs], total[vecs:]
    lane = iota((vecs, LANES), 1)
    real_here = lane // vecs % 2 == 0
    swapped = jnp.where(
        real_here, pltpu.roll(im_left, LANES - vecs, 1), -pltpu.roll(im_left, vecs, 1)
    )
    joined = re_left + swapped
    for n in range(gram_ref.shape[0]):
        gram_ref[n] = joined

    def sent(b, carry):
        send(b).wait()
        return carry

    lax.fori_loop(0, blocks, sent, 0)


def add_kernel(
    width, nloc, interior, count_ref, table_hbm, term_hbm, curl_hbm, mass_hbm, face_ref,
    dofs_ref, term_ref, images, sem, term_sems, out_sems, *accs
):
    owned_len = curl_hbm.shape[1]
    groups = LANES // (2 * width)
    capacity = term_ref.shape[0] // nloc * groups
    block_elems = groups * BLOCK_ROWS
    block_terms = nloc * BLOCK_ROWS
    load = pltpu.make_async_copy(table_hbm, dofs_ref, sem)
    load.start()
    live = count_ref[0]
    blocks = (live + block_elems - 1) // block_elems

    def fetch(b):
        at = pl.ds(pl.multiple_of(b * block_terms, BLOCK_ROWS), block_terms)
        return pltpu.make_async_copy(term_hbm.at[at], term_ref.at[at], term_sems.at[b])

    def fetch_all(b, carry):
        fetch(b).start()
        return carry

    lax.fori_loop(0, blocks, fetch_all, 0)
    many = 4
    zero_tile = jnp.zeros((many * LANES, LANES), F32)

    def clear(c, carry):
        at = pl.ds(pl.multiple_of(c * many * LANES, LANES), many * LANES)
        for acc in accs:
            acc[at, :] = zero_tile
        return carry

    lax.fori_loop(0, owned_len // (many * LANES), clear, 0)
    load.wait()

    def index_of(i, elem):
        return dofs_ref.at[pl.ds(i * capacity, capacity)][elem]

    def block(b, carry):
        fetch(b).wait()
        add_block(term_ref, accs, index_of, b, nloc, groups)
        return carry

    lax.fori_loop(0, blocks, block, 0)

    masks = lane_masks(width, groups)
    folder = folder_of(width)
    wide = 2 * LANES
    many = 4
    span = many * wide

    def fold_some(first, curl, mass):
        for u in range(many):
            at = pl.ds(pl.multiple_of(first + u * wide, wide), wide)
            total = pick(masks, [acc[at, :] for acc in accs])
            total = dot_nt(folder, jnp.concatenate(split(total), axis=1))
            to = slice(u * wide, (u + 1) * wide)
            curl[:, to] = total[:width]
            mass[:, to] = total[width:]

    moves = []
    for c in range(owned_len // span):
        at = pl.ds(c * span, span)
        if c * span < interior:
            fold_some(c * span, images.at[0, :, at], images.at[1, :, at])
            for n, image in enumerate((curl_hbm, mass_hbm)):
                moves.append(
                    pltpu.make_async_copy(
                        images.at[n, :, at], image.at[:, at], out_sems.at[2 * c + n]
                    )
                )
                moves[-1].start()
        else:
            at = pl.ds(c * span - interior, span)
            fold_some(c * span, face_ref.at[0, :, at], face_ref.at[1, :, at])
    for move in moves:
        move.wait()


def finish_kernel(
    width, scale, curl_in, mass_in, face_ref, back_x_ref, back_y_ref, gram_ref,
    curl_out, mass_out, gram_out, faces, sems,
):
    del curl_in, mass_in
    face_len = back_x_ref.shape[1]
    outer = pl.ds(curl_out.shape[1] - 2 * face_len, 2 * face_len)
    moves = []
    for n, image in enumerate((curl_out, mass_out)):
        rows = slice(n * width, (n + 1) * width)
        faces[n, :, :face_len] = face_ref[n, :, :face_len] + back_x_ref[rows, :]
        faces[n, :, face_len:] = face_ref[n, :, face_len:] + back_y_ref[rows, :]
        moves.append(pltpu.make_async_copy(faces.at[n], image.at[:, outer], sems.at[n]))
        moves[-1].start()
    total = gram_ref[0]
    for d in range(1, gram_ref.shape[0]):
        total = total + gram_ref[d]
    total = total * scale
    vecs = total.shape[0]
    for q in range(4):
        shifted = total if q == 0 else pltpu.roll(total, LANES - q * vecs, 1)
        gram_out[q * vecs : (q + 1) * vecs, :] = shifted[:, :vecs]
    for move in moves:
        move.wait()


def on_device(
    trial_block,
    stiff_coef,
    mass_coef,
    elem_count,
    elem_dofs,
    pairing,
    bloch_fraction,
    stiff_ref,
    mass_ref,
):
    own_block = trial_block[0, 0]
    vecs, owned_len = own_block.shape[1:]
    face_len = pairing.shape[0]
    interior = owned_len - 2 * face_len
    width = 2 * vecs
    groups = LANES // (2 * width)
    capacity, nloc = elem_dofs.shape[2:]
    face_slots = capacity // 8
    devices = lax.axis_size("px") * lax.axis_size("py")
    own_rows = own_block.reshape(width, owned_len)
    low_x = own_rows[:, interior : interior + face_len]
    low_y = own_rows[:, interior + face_len :]
    high_x = lax.ppermute(low_x, "px", ring_route("px", -1))
    high_y = lax.ppermute(low_y, "py", line_route("py", -1))
    live = elem_count[0]
    smem = pl.BlockSpec(memory_space=pltpu.SMEM)
    vmem = pl.BlockSpec(memory_space=pltpu.VMEM)
    left = pl.BlockSpec(memory_space=pl.ANY)

    limit = 62 * 1024 * 1024
    params = pltpu.CompilerParams(vmem_limit_bytes=limit)
    table, own_table, face_table, scale, turn = pl.pallas_call(
        functools.partial(prepare_kernel, owned_len, face_len, width),
        out_shape=(
            jax.ShapeDtypeStruct((nloc + 1, 1, capacity), jnp.int32),
            jax.ShapeDtypeStruct((nloc + 1, 1, capacity), jnp.int32),
            jax.ShapeDtypeStruct((-(-nloc // 8) * 8, face_slots), jnp.int32),
            jax.ShapeDtypeStruct((capacity // groups, LANES), F32),
            jax.ShapeDtypeStruct((16, LANES), F32),
        ),
        in_specs=[smem] * 2 + [vmem] * 4,
        out_specs=[vmem] * 5,
        compiler_params=params,
        name="prepare",
    )(
        live,
        bloch_fraction,
        elem_dofs.transpose(0, 3, 1, 2).reshape(nloc, 1, capacity),
        pairing.reshape(-1, LANES),
        stiff_coef[0],
        mass_coef[0],
    )
    table = table.reshape(-1)
    own_table = own_table.reshape(-1)
    face_table = face_table.reshape(-1)

    extent = owned_len + 2 * face_len
    blocks = capacity // (groups * BLOCK_ROWS)
    term_rows = nloc * capacity // groups
    terms, side_x, side_y, gram = pl.pallas_call(
        functools.partial(term_kernel, width),
        out_shape=(
            jax.ShapeDtypeStruct((term_rows, LANES), F32),
            jax.ShapeDtypeStruct((2 * width, face_len), F32),
            jax.ShapeDtypeStruct((2 * width, face_len), F32),
            jax.ShapeDtypeStruct((devices, vecs, LANES), F32),
        ),
        in_specs=[smem] * 3 + [left] * 2 + [vmem] * 5,
        out_specs=[left] + [vmem] * 3,
        scratch_shapes=[
            pltpu.SMEM(table.shape, jnp.int32),
            pltpu.SMEM(face_table.shape, jnp.int32),
            pltpu.VMEM((term_rows, LANES), F32),
            pltpu.VMEM((nloc * nloc, 8, LANES), F32),
            pltpu.VMEM((extent, LANES), F32),
            pltpu.VMEM((term_rows, LANES), F32),
            pltpu.VMEM((LANES, LANES), F32),
            pltpu.SemaphoreType.DMA((2,)),
            pltpu.SemaphoreType.DMA((blocks,)),
        ]
        + [pltpu.VMEM((2 * face_len + 8, LANES), F32)] * N_ACC,
        compiler_params=pltpu.CompilerParams(vmem_limit_bytes=60 * 1024 * 1024),
        name="terms",
    )(
        live, stiff_ref, mass_ref, table, face_table, turn, own_rows, high_x, high_y, scale
    )

    gathered = lax.all_to_all(gram, ("px", "py"), 0, 0)
    back_x = lax.ppermute(side_x, "px", ring_route("px", 1))
    back_y = lax.ppermute(side_y, "py", line_route("py", 1))

    curl, mass, faces = pl.pallas_call(
        functools.partial(add_kernel, width, nloc, interior),
        out_shape=(
            jax.ShapeDtypeStruct((width, owned_len), F32),
            jax.ShapeDtypeStruct((width, owned_len), F32),
            jax.ShapeDtypeStruct((2, width, 2 * face_len), F32),
        ),
        in_specs=[smem, left, left],
        out_specs=[left, left, vmem],
        scratch_shapes=[
            pltpu.SMEM(own_table.shape, jnp.int32),
            pltpu.VMEM((term_rows, LANES), F32),
            pltpu.VMEM((2, width, interior), F32),
            pltpu.SemaphoreType.DMA,
            pltpu.SemaphoreType.DMA((blocks,)),
            pltpu.SemaphoreType.DMA((2 * owned_len // (8 * LANES),)),
        ]
        + [pltpu.VMEM((owned_len + 8, LANES), F32)] * N_ACC,
        compiler_params=params,
        cost_estimate=pl.CostEstimate(
            flops=40 * 1024 * 1024 * 1024, bytes_accessed=40 * 1024 * 1024, transcendentals=0
        ),
        name="adds",
    )(live, own_table, terms)

    curl, mass, gram = pl.pallas_call(
        functools.partial(finish_kernel, width, 1.0 / float(devices * owned_len)),
        out_shape=(
            jax.ShapeDtypeStruct((width, owned_len), F32),
            jax.ShapeDtypeStruct((width, owned_len), F32),
            jax.ShapeDtypeStruct((4 * vecs, vecs), F32),
        ),
        in_specs=[left] * 2 + [vmem] * 4,
        out_specs=[left, left, vmem],
        scratch_shapes=[
            pltpu.VMEM((2, width, 2 * face_len), F32),
            pltpu.SemaphoreType.DMA((2,)),
        ],
        input_output_aliases={0: 0, 1: 1},
        compiler_params=pltpu.CompilerParams(vmem_limit_bytes=8 * 1024 * 1024),
        name="finish",
    )(curl, mass, faces, back_x, back_y, gathered)
    shape = (1, 1, 2, vecs, owned_len)
    return curl.reshape(shape), mass.reshape(shape), gram.reshape(2, 2, vecs, vecs)


def solution(mesh):
    return jax.shard_map(
        on_device,
        mesh=mesh,
        in_specs=(
            P("px", "py", None, None, None),
            P("px", "py", None),
            P("px", "py", None),
            P("px", "py"),
            P("px", "py", None, None),
            P(),
            P(),
            P(),
            P(),
        ),
        out_specs=(P("px", "py", None, None, None), P("px", "py", None, None, None), P()),
        check_vma=False,
    )
```

```python
import functools
import math

import jax
import jax.numpy as jnp
from jax import lax
from jax.experimental import pallas as pl
from jax.experimental.pallas import tpu as pltpu
from jax.sharding import PartitionSpec as P

LANES = 128
BLOCK_ROWS = 16
SUB_ROWS = 8
TERM_MIB = 32
ADD_MIB = 26
STEP = 4
DEEP = 4
N_ACC = 4
F32 = jnp.float32
BF16 = jnp.bfloat16


def ring_route(axis, steps):
    count = lax.axis_size(axis)
    return [(source, (source + steps) % count) for source in range(count)]


def line_route(axis, distance):
    devices = range(lax.axis_size(axis))
    return [(i - distance, i) for i in devices if i - distance in devices]


def iota(shape, axis):
    return lax.broadcasted_iota(jnp.int32, shape, axis)


def split(x):
    top = x.astype(BF16)
    return top, (x - top.astype(F32)).astype(BF16)


def dot_nt(left, right):
    return lax.dot_general(
        left, right, (((1,), (1,)), ((), ())), preferred_element_type=F32
    )


def gather_lanes(table_ref, index):
    high = index // LANES
    low = index % LANES
    found = jnp.zeros_like(index)
    for r in range(table_ref.shape[0]):
        line = jnp.broadcast_to(table_ref[r : r + 1, :], index.shape)
        found = jnp.where(high == r, jnp.take_along_axis(line, low, axis=1), found)
    return found


def prepare_kernel(
    owned_len, face_len, width, count_ref, bloch_ref, stiff_elem_ref, mass_elem_ref,
    dofs_ref, pair_ref, stiff_ref, mass_ref,
    table_ref, own_table_ref, face_table_ref, scale_ref, turn_ref, coef_ref,
):
    nloc, _, capacity = dofs_ref.shape
    face_slots = face_table_ref.shape[1]
    groups = LANES // (2 * width)
    at_end = lax.axis_index("px") == lax.axis_size("px") - 1
    live = count_ref[0]

    index = [dofs_ref[i] for i in range(nloc)]
    flag = jnp.zeros((1, capacity), jnp.int32)
    for i in range(nloc):
        for k in range(i + 1, min(i // STEP * STEP + STEP, nloc)):
            flag = jnp.where(index[i] == index[k], 1, flag)
    reach = groups * SUB_ROWS // 2
    while reach:
        flag = jnp.maximum(flag, pltpu.roll(flag, reach, 1))
        reach //= 2
    table_ref[nloc] = flag
    own_table_ref[nloc] = flag
    for i in range(nloc):
        table_ref[i] = index[i]
        own_table_ref[i] = jnp.minimum(index[i], owned_len)

    pad = face_table_ref.shape[0] - nloc
    for c in range(0, face_slots, LANES):
        at = slice(c, c + LANES)
        first = jnp.concatenate(
            [row[:, at] for row in index] + [jnp.zeros((pad, LANES), jnp.int32)], axis=0
        )
        local = first - owned_len
        on_face = at_end & (local >= 0) & (local < face_len)
        paired = gather_lanes(pair_ref, jnp.where(on_face, local, 0))
        first = jnp.where(on_face, paired + owned_len, first)
        face_table_ref[:, at] = jnp.where(first >= owned_len, first - owned_len, 2 * face_len)
        for i in range(nloc):
            table_ref[i, :, at] = first[i : i + 1]

    per_chunk = LANES // groups
    lane_of = iota((LANES, LANES), 0)
    elem_of = iota((LANES, LANES), 1)
    mine = elem_of % groups == lane_of // (2 * width)
    is_curl = lane_of // width % 2 == 0
    chooser = (iota((per_chunk, LANES), 1) // groups == iota((per_chunk, LANES), 0)).astype(BF16)
    chooser = jnp.concatenate([chooser, chooser], axis=1)
    for c in range(capacity // LANES):
        at = slice(c * LANES, (c + 1) * LANES)
        scales = jnp.where(is_curl, stiff_ref[:, at], mass_ref[:, at])
        scales = jnp.where(mine & (c * LANES + elem_of < live), scales, 0.0)
        scale_ref[c * per_chunk : (c + 1) * per_chunk, :] = dot_nt(
            chooser, jnp.concatenate(split(scales), axis=1)
        )

    curl_lane = iota((8, LANES), 1) // width % 2 == 0

    def build_coef(j, carry):
        for i in range(nloc):
            coef_ref[j * nloc + i] = jnp.where(curl_lane, stiff_elem_ref[j, i], mass_elem_ref[j, i])
        return carry

    lax.fori_loop(0, nloc, build_coef, 0)

    ratio = jnp.full((8, LANES), bloch_ref[0].astype(F32), F32) / bloch_ref[1].astype(F32)
    angle = (2.0 * math.pi) * jnp.where(at_end, ratio, 0.0)
    turn_ref[:8] = jnp.cos(angle)
    turn_ref[8:] = jnp.sin(angle)


def lane_masks(width, groups):
    lane = iota((1, LANES), 1) // (2 * width)
    return [lane == k for k in range(groups)]


def pick(masks, parts):
    out = parts[-1]
    for mask, part in zip(masks[-2::-1], parts[-2::-1]):
        out = jnp.where(mask, part, out)
    return out


def folder_of(width):
    rows = 2 * width
    folder = (iota((rows, LANES), 1) % rows == iota((rows, LANES), 0)).astype(BF16)
    return jnp.concatenate([folder, folder], axis=1)


def add_block(term_ref, accs, index_of, b, nloc, groups):
    unroll = 2

    def run(step, first_row, first_elem):
        def some(t, c):
            for u in range(unroll):
                g = t * unroll + u
                elem = first_elem + g * groups
                for j in range(0, nloc, step):
                    slots = range(j, min(j + step, nloc))
                    new = [term_ref[pl.ds(first_row + s * BLOCK_ROWS + g, 1), :] for s in slots]
                    for k in range(groups):
                        places = [pl.ds(index_of[0](s, elem + k), 1) for s in slots]
                        sums = [accs[k][at, :] + row for at, row in zip(places, new)]
                        for at, row in zip(places, sums):
                            accs[k][at, :] = row
            return c

        lax.fori_loop(0, SUB_ROWS // unroll, some, 0)

    def part(h, carry):
        first_row = b * nloc * BLOCK_ROWS + h * SUB_ROWS
        first_elem = (b * (BLOCK_ROWS // SUB_ROWS) + h) * SUB_ROWS * groups
        clash = index_of[1](nloc, first_elem + SUB_ROWS * groups - 1)

        @pl.when(clash == 0)
        def _():
            run(STEP, first_row, first_elem)

        @pl.when(clash != 0)
        def _():
            run(1, first_row, first_elem)

        return carry

    index_of = index_of if isinstance(index_of, tuple) else (index_of, index_of)
    lax.fori_loop(0, BLOCK_ROWS // SUB_ROWS, part, 0)


def term_kernel(
    width,
    nloc,
    count_ref,
    table_hbm,
    face_table_hbm,
    turn_hbm,
    own_hbm,
    scale_hbm,
    coef_hbm,
    high_x_ref,
    high_y_ref,
    term_hbm,
    side_x_ref,
    side_y_ref,
    gram_ref,
    dofs_ref,
    face_dofs_ref,
    turn_ref,
    own_ref,
    scale_ref,
    coef_ref,
    term_ref,
    rows_x,
    gath,
    gram_acc,
    sems,
    term_sems,
    *accs,
):
    owned_len = own_ref.shape[1]
    face_len = high_x_ref.shape[1]
    vecs = width // 2
    groups = LANES // (2 * width)
    capacity = scale_ref.shape[0] * groups
    face_slots = capacity // 8
    copies = LANES // width
    block_elems = groups * BLOCK_ROWS
    block_terms = nloc * BLOCK_ROWS

    own_load, turn_load, *loads = [
        pltpu.make_async_copy(source, target, sems.at[n])
        for n, (source, target) in enumerate(
            (
                (own_hbm, own_ref),
                (turn_hbm, turn_ref),
                (table_hbm, dofs_ref),
                (face_table_hbm, face_dofs_ref),
                (coef_hbm, coef_ref),
                (scale_hbm, scale_ref),
            )
        )
    ]
    for load in (own_load, turn_load, *loads):
        load.start()

    def clear(c, carry):
        at = pl.ds(pl.multiple_of(c * 4 * LANES, LANES), 4 * LANES)
        for acc in accs:
            acc[at, :] = jnp.zeros((4 * LANES, LANES), F32)
        return carry

    lax.fori_loop(0, face_len // (2 * LANES), clear, 0)
    gram_acc[...] = jnp.zeros_like(gram_acc)
    turn_load.wait()
    cos, sin = turn_ref[:vecs], turn_ref[8 : 8 + vecs]

    def turned(pair, sign):
        n = pair.shape[1] // LANES
        c = jnp.concatenate([cos] * n, axis=1)
        s = jnp.concatenate([sin] * n, axis=1) * sign
        a, b = pair[:vecs], pair[vecs:]
        return jnp.concatenate([c * a - s * b, s * a + c * b], axis=0)

    unit = (iota((LANES, LANES), 0) == iota((LANES, LANES), 1)).astype(BF16)
    unit = jnp.concatenate([unit, unit], axis=1)
    def put_rows(tile, first):
        top, low = split(tile)
        tiled = jnp.concatenate(
            [jnp.concatenate([top] * copies, axis=0), jnp.concatenate([low] * copies, axis=0)],
            axis=1,
        )
        rows_x[pl.ds(first, LANES), :] = dot_nt(unit, tiled)

    many = 8

    def build_own(c, carry):
        for u in range(many):
            first = pl.multiple_of((c * many + u) * LANES, LANES)
            put_rows(own_ref[:, pl.ds(first, LANES)], first)
        return carry


    def build_face(c, carry):
        for u in range(many // 2):
            first = pl.multiple_of((c * (many // 2) + u) * LANES, LANES)
            put_rows(
                turned(high_x_ref[:, pl.ds(first, LANES)], 1.0),
                pl.multiple_of(owned_len + first, LANES),
            )
            put_rows(
                high_y_ref[:, pl.ds(first, LANES)],
                pl.multiple_of(owned_len + face_len + first, LANES),
            )
        return carry

    lax.fori_loop(0, face_len // (many // 2 * LANES), build_face, 0)
    own_load.wait()
    lax.fori_loop(0, owned_len // (many * LANES), build_own, 0)

    for load in loads:
        load.wait()

    masks = lane_masks(width, groups)

    def index_of(i, elem):
        return dofs_ref.at[pl.ds(i * capacity, capacity)][elem]

    def face_index_of(i, elem):
        return face_dofs_ref.at[pl.ds(i * face_slots, face_slots)][elem]

    unroll = 4
    steps = BLOCK_ROWS // unroll
    halves = range(0, BLOCK_ROWS, 8)
    part = nloc // steps

    def block(b, gather):
        behind = jnp.maximum(b - 1, 0)
        here = pl.multiple_of(b * block_terms, BLOCK_ROWS)
        there = pl.multiple_of(behind * block_terms, BLOCK_ROWS)
        first_term = pl.multiple_of(behind * block_terms, BLOCK_ROWS)
        first_elem = b * block_elems

        def step(t, c):
            totals = [[None] * len(halves) for _ in range(part)]
            for i in range(nloc):
                if gather:
                    for u in range(unroll):
                        g = t * unroll + u
                        elem = first_elem + g * groups
                        rows = [
                            rows_x[pl.ds(index_of(i, elem + k), 1), :] for k in range(groups)
                        ]
                        gath[pl.ds(here + i * BLOCK_ROWS + g, 1), :] = pick(masks, rows)
                values = [
                    gath[pl.ds(pl.multiple_of(there + i * BLOCK_ROWS + h, 8), 8), :] for h in halves
                ]
                for q in range(part):
                    coef = coef_ref[(t * part + q) * nloc + i]
                    for n, value in enumerate(values):
                        product = coef * value
                        totals[q][n] = product if i == 0 else totals[q][n] + product
            for n, h in enumerate(halves):
                scale = scale_ref[pl.ds(pl.multiple_of(behind * BLOCK_ROWS + h, 8), 8), :]
                for q in range(part):
                    at = first_term + (t * part + q) * BLOCK_ROWS + h
                    term_ref[pl.ds(pl.multiple_of(at, 8), 8), :] = totals[q][n] * scale
            return c

        lax.fori_loop(0, steps, step, 0)

    def send(b):
        at = pl.ds(pl.multiple_of(b * block_terms, BLOCK_ROWS), block_terms)
        return pltpu.make_async_copy(term_ref.at[at], term_hbm.at[at], term_sems.at[b])

    def face_block(b, carry):
        add_block(term_ref, accs, (face_index_of, index_of), b, nloc, groups)
        return carry

    live = count_ref[0]
    blocks = (live + block_elems - 1) // block_elems
    face_blocks = jnp.minimum(blocks, face_slots // block_elems)
    def full_block(b, carry):
        block(b, True)

        @pl.when(b > 0)
        def _():
            send(b - 1).start()

        return carry

    lax.fori_loop(0, blocks, full_block, 0)
    block(blocks, False)
    send(blocks - 1).start()
    lax.fori_loop(0, face_blocks, face_block, 0)

    deep = DEEP * block_terms
    zero_block = jnp.zeros((block_terms, LANES), F32)
    chunks = (blocks + DEEP - 1) // DEEP

    def blank(b, carry):
        at = pl.ds(pl.multiple_of(b * block_terms, BLOCK_ROWS), block_terms)
        gath[at, :] = zero_block
        term_ref[at, :] = zero_block
        return carry

    lax.fori_loop(blocks, chunks * DEEP, blank, 0)

    def products(c, carry):
        at = pl.ds(pl.multiple_of(c * deep, BLOCK_ROWS), deep)
        left, left_low = split(gath[at, :])
        right, right_low = split(term_ref[at, :])
        gram_acc[...] += lax.dot_general(
            jnp.concatenate([left, left, left_low], axis=0),
            jnp.concatenate([right, right_low, right], axis=0),
            (((0,), (0,)), ((), ())),
            preferred_element_type=F32,
        )
        return carry

    lax.fori_loop(0, chunks, products, 0)
    folder = folder_of(width)
    wide = 2 * LANES

    def folded(first):
        at = pl.ds(first, wide)
        total = pick(masks, [acc[at, :] for acc in accs])
        return dot_nt(folder, jnp.concatenate(split(total), axis=1))

    def fold_face(c, carry):
        for u in range(2):
            first = pl.multiple_of((2 * c + u) * wide, wide)
            at = pl.ds(first, wide)
            total = folded(first)
            side_x_ref[:width, at] = turned(total[:width], -1.0)
            side_x_ref[width:, at] = turned(total[width:], -1.0)
            side_y_ref[:, at] = folded(pl.multiple_of(face_len + first, wide))
        return carry

    lax.fori_loop(0, face_len // (2 * wide), fold_face, 0)

    whole = gram_acc[...]
    total = whole[:width]
    for k in range(1, groups):
        part = whole[2 * width * k : 2 * width * k + width]
        total = total + pltpu.roll(part, LANES - 2 * width * k, 1)
    re_left, im_left = total[:vecs], total[vecs:]
    lane = iota((vecs, LANES), 1)
    real_here = lane // vecs % 2 == 0
    swapped = jnp.where(
        real_here, pltpu.roll(im_left, LANES - vecs, 1), -pltpu.roll(im_left, vecs, 1)
    )
    joined = re_left + swapped
    for n in range(gram_ref.shape[0]):
        gram_ref[n] = joined

    def sent(b, carry):
        send(b).wait()
        return carry

    lax.fori_loop(0, blocks, sent, 0)


def add_kernel(
    width, nloc, interior, count_ref, table_hbm, term_hbm, curl_hbm, mass_hbm, face_ref,
    dofs_ref, term_ref, images, sem, term_sems, out_sems, *accs
):
    owned_len = curl_hbm.shape[1]
    groups = LANES // (2 * width)
    capacity = term_ref.shape[0] // nloc * groups
    block_elems = groups * BLOCK_ROWS
    block_terms = nloc * BLOCK_ROWS
    load = pltpu.make_async_copy(table_hbm, dofs_ref, sem)
    load.start()
    live = count_ref[0]
    blocks = (live + block_elems - 1) // block_elems

    def fetch(b):
        at = pl.ds(pl.multiple_of(b * block_terms, BLOCK_ROWS), block_terms)
        return pltpu.make_async_copy(term_hbm.at[at], term_ref.at[at], term_sems.at[b])

    def fetch_all(b, carry):
        fetch(b).start()
        return carry

    lax.fori_loop(0, blocks, fetch_all, 0)
    many = 4
    zero_tile = jnp.zeros((many * LANES, LANES), F32)

    def clear(c, carry):
        at = pl.ds(pl.multiple_of(c * many * LANES, LANES), many * LANES)
        for acc in accs:
            acc[at, :] = zero_tile
        return carry

    lax.fori_loop(0, owned_len // (many * LANES), clear, 0)
    load.wait()

    def index_of(i, elem):
        return dofs_ref.at[pl.ds(i * capacity, capacity)][elem]

    def block(b, carry):
        fetch(b).wait()
        add_block(term_ref, accs, index_of, b, nloc, groups)
        return carry

    lax.fori_loop(0, blocks, block, 0)

    masks = lane_masks(width, groups)
    folder = folder_of(width)
    wide = 2 * LANES
    many = 4
    span = many * wide

    def fold_some(first, curl, mass):
        for u in range(many):
            at = pl.ds(pl.multiple_of(first + u * wide, wide), wide)
            total = pick(masks, [acc[at, :] for acc in accs])
            total = dot_nt(folder, jnp.concatenate(split(total), axis=1))
            to = slice(u * wide, (u + 1) * wide)
            curl[:, to] = total[:width]
            mass[:, to] = total[width:]

    moves = []
    for c in range(owned_len // span):
        at = pl.ds(c * span, span)
        if c * span < interior:
            fold_some(c * span, images.at[0, :, at], images.at[1, :, at])
            for n, image in enumerate((curl_hbm, mass_hbm)):
                moves.append(
                    pltpu.make_async_copy(
                        images.at[n, :, at], image.at[:, at], out_sems.at[2 * c + n]
                    )
                )
                moves[-1].start()
        else:
            at = pl.ds(c * span - interior, span)
            fold_some(c * span, face_ref.at[0, :, at], face_ref.at[1, :, at])
    for move in moves:
        move.wait()


def finish_kernel(
    width, scale, curl_in, mass_in, face_ref, back_x_ref, back_y_ref, gram_ref,
    curl_out, mass_out, gram_out, faces, sems,
):
    del curl_in, mass_in
    face_len = back_x_ref.shape[1]
    outer = pl.ds(curl_out.shape[1] - 2 * face_len, 2 * face_len)
    moves = []
    for n, image in enumerate((curl_out, mass_out)):
        rows = slice(n * width, (n + 1) * width)
        faces[n, :, :face_len] = face_ref[n, :, :face_len] + back_x_ref[rows, :]
        faces[n, :, face_len:] = face_ref[n, :, face_len:] + back_y_ref[rows, :]
        moves.append(pltpu.make_async_copy(faces.at[n], image.at[:, outer], sems.at[n]))
        moves[-1].start()
    total = gram_ref[0]
    for d in range(1, gram_ref.shape[0]):
        total = total + gram_ref[d]
    total = total * scale
    vecs = total.shape[0]
    for q in range(4):
        shifted = total if q == 0 else pltpu.roll(total, LANES - q * vecs, 1)
        gram_out[q * vecs : (q + 1) * vecs, :] = shifted[:, :vecs]
    for move in moves:
        move.wait()


def on_device(
    trial_block,
    stiff_coef,
    mass_coef,
    elem_count,
    elem_dofs,
    pairing,
    bloch_fraction,
    stiff_ref,
    mass_ref,
):
    own_block = trial_block[0, 0]
    vecs, owned_len = own_block.shape[1:]
    face_len = pairing.shape[0]
    interior = owned_len - 2 * face_len
    width = 2 * vecs
    groups = LANES // (2 * width)
    capacity, nloc = elem_dofs.shape[2:]
    face_slots = capacity // 8
    devices = lax.axis_size("px") * lax.axis_size("py")
    own_rows = own_block.reshape(width, owned_len)
    low_x = own_rows[:, interior : interior + face_len]
    low_y = own_rows[:, interior + face_len :]
    high_x = lax.ppermute(low_x, "px", ring_route("px", -1))
    high_y = lax.ppermute(low_y, "py", line_route("py", -1))
    live = elem_count[0]
    smem = pl.BlockSpec(memory_space=pltpu.SMEM)
    vmem = pl.BlockSpec(memory_space=pltpu.VMEM)
    left = pl.BlockSpec(memory_space=pl.ANY)

    limit = 62 * 1024 * 1024
    params = pltpu.CompilerParams(vmem_limit_bytes=limit)

    def in_hbm(*values):
        return [pltpu.with_memory_space_constraint(value, pltpu.HBM) for value in values]

    table, own_table, face_table, scale, turn, coef = pl.pallas_call(
        functools.partial(prepare_kernel, owned_len, face_len, width),
        out_shape=(
            jax.ShapeDtypeStruct((nloc + 1, 1, capacity), jnp.int32),
            jax.ShapeDtypeStruct((nloc + 1, 1, capacity), jnp.int32),
            jax.ShapeDtypeStruct((-(-nloc // 8) * 8, face_slots), jnp.int32),
            jax.ShapeDtypeStruct((capacity // groups, LANES), F32),
            jax.ShapeDtypeStruct((16, LANES), F32),
            jax.ShapeDtypeStruct((nloc * nloc, 8, LANES), F32),
        ),
        in_specs=[smem] * 4 + [vmem] * 4,
        out_specs=[vmem] * 6,
        compiler_params=params,
        name="prepare",
    )(
        live,
        bloch_fraction,
        stiff_ref,
        mass_ref,
        elem_dofs.transpose(0, 3, 1, 2).reshape(nloc, 1, capacity),
        pairing.reshape(-1, LANES),
        stiff_coef[0],
        mass_coef[0],
    )
    table = table.reshape(-1)
    own_table = own_table.reshape(-1)
    face_table = face_table.reshape(-1)

    extent = owned_len + 2 * face_len
    blocks = capacity // (groups * BLOCK_ROWS)
    term_rows = nloc * capacity // groups
    terms, side_x, side_y, gram = pl.pallas_call(
        functools.partial(term_kernel, width, nloc),
        out_shape=(
            pltpu.HBM((term_rows, LANES), F32),
            jax.ShapeDtypeStruct((2 * width, face_len), F32),
            jax.ShapeDtypeStruct((2 * width, face_len), F32),
            jax.ShapeDtypeStruct((devices, vecs, LANES), F32),
        ),
        in_specs=[smem] + [left] * 6 + [vmem] * 2,
        out_specs=[left] + [vmem] * 3,
        scratch_shapes=[
            pltpu.SMEM(table.shape, jnp.int32),
            pltpu.SMEM(face_table.shape, jnp.int32),
            pltpu.VMEM(turn.shape, F32),
            pltpu.VMEM(own_rows.shape, F32),
            pltpu.VMEM(scale.shape, F32),
            pltpu.VMEM(coef.shape, F32),
            pltpu.VMEM((term_rows, LANES), F32),
            pltpu.VMEM((extent, LANES), F32),
            pltpu.VMEM((term_rows, LANES), F32),
            pltpu.VMEM((LANES, LANES), F32),
            pltpu.SemaphoreType.DMA((6,)),
            pltpu.SemaphoreType.DMA((blocks,)),
        ]
        + [pltpu.VMEM((2 * face_len + 8, LANES), F32)] * N_ACC,
        compiler_params=pltpu.CompilerParams(vmem_limit_bytes=TERM_MIB * 1024 * 1024),
        name="terms",
    )(live, *in_hbm(table, face_table, turn, own_rows, scale, coef), high_x, high_y)

    gathered = lax.all_to_all(gram, ("px", "py"), 0, 0)
    back_x = lax.ppermute(side_x, "px", ring_route("px", 1))
    back_y = lax.ppermute(side_y, "py", line_route("py", 1))

    curl, mass, faces = pl.pallas_call(
        functools.partial(add_kernel, width, nloc, interior),
        out_shape=(
            jax.ShapeDtypeStruct((width, owned_len), F32),
            jax.ShapeDtypeStruct((width, owned_len), F32),
            jax.ShapeDtypeStruct((2, width, 2 * face_len), F32),
        ),
        in_specs=[smem, left, left],
        out_specs=[left, left, vmem],
        scratch_shapes=[
            pltpu.SMEM(own_table.shape, jnp.int32),
            pltpu.VMEM((term_rows, LANES), F32),
            pltpu.VMEM((2, width, interior), F32),
            pltpu.SemaphoreType.DMA,
            pltpu.SemaphoreType.DMA((blocks,)),
            pltpu.SemaphoreType.DMA((2 * owned_len // (8 * LANES),)),
        ]
        + [pltpu.VMEM((owned_len + 8, LANES), F32)] * N_ACC,
        compiler_params=pltpu.CompilerParams(vmem_limit_bytes=ADD_MIB * 1024 * 1024),
        cost_estimate=pl.CostEstimate(
            flops=40 * 1024 * 1024 * 1024, bytes_accessed=40 * 1024 * 1024, transcendentals=0
        ),
        name="adds",
    )(live, *in_hbm(own_table, terms))

    curl, mass, gram = pl.pallas_call(
        functools.partial(finish_kernel, width, 1.0 / float(devices * owned_len)),
        out_shape=(
            jax.ShapeDtypeStruct((width, owned_len), F32),
            jax.ShapeDtypeStruct((width, owned_len), F32),
            jax.ShapeDtypeStruct((4 * vecs, vecs), F32),
        ),
        in_specs=[left] * 2 + [vmem] * 4,
        out_specs=[left, left, vmem],
        scratch_shapes=[
            pltpu.VMEM((2, width, 2 * face_len), F32),
            pltpu.SemaphoreType.DMA((2,)),
        ],
        input_output_aliases={0: 0, 1: 1},
        compiler_params=pltpu.CompilerParams(vmem_limit_bytes=8 * 1024 * 1024),
        name="finish",
    )(curl, mass, faces, back_x, back_y, gathered)
    shape = (1, 1, 2, vecs, owned_len)
    return curl.reshape(shape), mass.reshape(shape), gram.reshape(2, 2, vecs, vecs)


def solution(mesh):
    return jax.shard_map(
        on_device,
        mesh=mesh,
        in_specs=(
            P("px", "py", None, None, None),
            P("px", "py", None),
            P("px", "py", None),
            P("px", "py"),
            P("px", "py", None, None),
            P(),
            P(),
            P(),
            P(),
        ),
        out_specs=(P("px", "py", None, None, None), P("px", "py", None, None, None), P()),
        check_vma=False,
    )
```

```python
import functools
import math

import jax
import jax.numpy as jnp
from jax import lax
from jax.experimental import pallas as pl
from jax.experimental.pallas import tpu as pltpu
from jax.sharding import PartitionSpec as P


LANES = 128
BLOCK_ROWS = 16
SUB_ROWS = 8
PAIR = 2
TERM_MIB = 32
ADD_MIB = 26
STEP = 4
DEEP = 4
N_ACC = 4
F32 = jnp.float32
BF16 = jnp.bfloat16


def ring_route(axis, steps):
    count = lax.axis_size(axis)
    return [(source, (source + steps) % count) for source in range(count)]


def line_route(axis, distance):
    devices = range(lax.axis_size(axis))
    return [(i - distance, i) for i in devices if i - distance in devices]


def iota(shape, axis):
    return lax.broadcasted_iota(jnp.int32, shape, axis)


def split(x):
    top = x.astype(BF16)
    return top, (x - top.astype(F32)).astype(BF16)


def dot_nt(left, right):
    return lax.dot_general(
        left, right, (((1,), (1,)), ((), ())), preferred_element_type=F32
    )


def gather_lanes(table_ref, index):
    high = index // LANES
    low = index % LANES
    found = jnp.zeros_like(index)
    for r in range(table_ref.shape[0]):
        line = jnp.broadcast_to(table_ref[r : r + 1, :], index.shape)
        found = jnp.where(high == r, jnp.take_along_axis(line, low, axis=1), found)
    return found


def prepare_kernel(
    owned_len, face_len, width, count_ref, bloch_ref, stiff_elem_ref, mass_elem_ref,
    dofs_ref, pair_ref, stiff_ref, mass_ref,
    table_ref, own_table_ref, face_table_ref, scale_ref, turn_ref, coef_hbm, coef_ref, coef_sem,
):
    nloc, _, capacity = dofs_ref.shape
    face_slots = face_table_ref.shape[1]
    groups = LANES // (2 * width)
    at_end = lax.axis_index("px") == lax.axis_size("px") - 1
    live = count_ref[0]

    curl_lane = iota((8, LANES), 1) // width % 2 == 0

    def build_coef(j, carry):
        for i in range(nloc):
            coef_ref[j * nloc + i] = jnp.where(curl_lane, stiff_elem_ref[j, i], mass_elem_ref[j, i])
        return carry

    lax.fori_loop(0, nloc, build_coef, 0)
    coef_move = pltpu.make_async_copy(coef_ref, coef_hbm, coef_sem)
    coef_move.start()

    index = [dofs_ref[i] for i in range(nloc)]
    flag = jnp.zeros((1, capacity), jnp.int32)
    for i in range(nloc):
        for k in range(i + 1, min(i // STEP * STEP + STEP, nloc)):
            flag = jnp.where(index[i] == index[k], 1, flag)
    reach = 1
    for row, rows in ((1, PAIR), (0, SUB_ROWS)):
        while reach < groups * rows:
            flag = jnp.maximum(flag, pltpu.roll(flag, reach, 1))
            reach *= 2
        table_ref[nloc + row] = flag
        own_table_ref[nloc + row] = flag
    for i in range(nloc):
        table_ref[i] = index[i]
        own_table_ref[i] = jnp.minimum(index[i], owned_len)

    pad = face_table_ref.shape[0] - nloc
    for c in range(0, face_slots, LANES):
        at = slice(c, c + LANES)
        first = jnp.concatenate(
            [row[:, at] for row in index] + [jnp.zeros((pad, LANES), jnp.int32)], axis=0
        )
        local = first - owned_len
        on_face = at_end & (local >= 0) & (local < face_len)
        paired = gather_lanes(pair_ref, jnp.where(on_face, local, 0))
        first = jnp.where(on_face, paired + owned_len, first)
        face_table_ref[:, at] = jnp.where(first >= owned_len, first - owned_len, 2 * face_len)
        for i in range(nloc):
            table_ref[i, :, at] = first[i : i + 1]

    per_chunk = LANES // groups
    lane_of = iota((LANES, LANES), 0)
    elem_of = iota((LANES, LANES), 1)
    mine = elem_of % groups == lane_of // (2 * width)
    is_curl = lane_of // width % 2 == 0
    chooser = (iota((per_chunk, LANES), 1) // groups == iota((per_chunk, LANES), 0)).astype(BF16)
    chooser = jnp.concatenate([chooser, chooser], axis=1)
    for c in range(capacity // LANES):
        at = slice(c * LANES, (c + 1) * LANES)
        scales = jnp.where(is_curl, stiff_ref[:, at], mass_ref[:, at])
        scales = jnp.where(mine & (c * LANES + elem_of < live), scales, 0.0)
        scale_ref[c * per_chunk : (c + 1) * per_chunk, :] = dot_nt(
            chooser, jnp.concatenate(split(scales), axis=1)
        )

    ratio = jnp.full((8, LANES), bloch_ref[0].astype(F32), F32) / bloch_ref[1].astype(F32)
    angle = (2.0 * math.pi) * jnp.where(at_end, ratio, 0.0)
    turn_ref[:8] = jnp.cos(angle)
    turn_ref[8:] = jnp.sin(angle)
    coef_move.wait()


def lane_masks(width, groups):
    lane = iota((1, LANES), 1) // (2 * width)
    return [lane == k for k in range(groups)]


def pick(masks, parts):
    out = parts[-1]
    for mask, part in zip(masks[-2::-1], parts[-2::-1]):
        out = jnp.where(mask, part, out)
    return out


def folder_of(width):
    rows = 2 * width
    folder = (iota((rows, LANES), 1) % rows == iota((rows, LANES), 0)).astype(BF16)
    return jnp.concatenate([folder, folder], axis=1)


def add_block(term_ref, accs, index_of, flag_of, b, nloc, groups):
    def part(h, carry):
        first_row = b * nloc * BLOCK_ROWS + h * SUB_ROWS
        first_elem = (b * (BLOCK_ROWS // SUB_ROWS) + h) * SUB_ROWS * groups

        def add_pair(t, step):
            for u in range(PAIR):
                g = t * PAIR + u
                elem = first_elem + g * groups
                for j in range(0, nloc, step):
                    slots = range(j, min(j + step, nloc))
                    new = [term_ref[pl.ds(first_row + s * BLOCK_ROWS + g, 1), :] for s in slots]
                    for k in range(groups):
                        places = [pl.ds(index_of(s, elem + k), 1) for s in slots]
                        sums = [accs[k][at, :] + row for at, row in zip(places, new)]
                        for at, row in zip(places, sums):
                            accs[k][at, :] = row

        def plain(t, c):
            add_pair(t, STEP)
            return c

        def careful(t, c):
            repeated = flag_of(nloc + 1, first_elem + (t + 1) * PAIR * groups - 1)

            @pl.when(repeated == 0)
            def _():
                add_pair(t, STEP)

            @pl.when(repeated != 0)
            def _():
                add_pair(t, 1)

            return c

        clash = flag_of(nloc, first_elem + SUB_ROWS * groups - 1)

        @pl.when(clash == 0)
        def _():
            lax.fori_loop(0, SUB_ROWS // PAIR, plain, 0)

        @pl.when(clash != 0)
        def _():
            lax.fori_loop(0, SUB_ROWS // PAIR, careful, 0)

        return carry

    lax.fori_loop(0, BLOCK_ROWS // SUB_ROWS, part, 0)


def term_kernel(
    width,
    nloc,
    count_ref,
    table_hbm,
    face_table_hbm,
    turn_hbm,
    own_hbm,
    scale_hbm,
    coef_hbm,
    high_x_ref,
    high_y_ref,
    term_hbm,
    side_x_ref,
    side_y_ref,
    gram_ref,
    dofs_ref,
    face_dofs_ref,
    turn_ref,
    own_ref,
    scale_ref,
    coef_ref,
    term_ref,
    rows_x,
    gath,
    gram_acc,
    sems,
    term_sems,
    *accs,
):
    owned_len = own_ref.shape[1]
    face_len = high_x_ref.shape[1]
    vecs = width // 2
    groups = LANES // (2 * width)
    capacity = scale_ref.shape[0] * groups
    face_slots = capacity // 8
    copies = LANES // width
    block_elems = groups * BLOCK_ROWS
    block_terms = nloc * BLOCK_ROWS

    own_load, turn_load, *loads = [
        pltpu.make_async_copy(source, target, sems.at[n])
        for n, (source, target) in enumerate(
            (
                (own_hbm, own_ref),
                (turn_hbm, turn_ref),
                (table_hbm, dofs_ref),
                (face_table_hbm, face_dofs_ref),
                (coef_hbm, coef_ref),
                (scale_hbm, scale_ref),
            )
        )
    ]
    for load in (own_load, turn_load, *loads):
        load.start()

    def clear(c, carry):
        at = pl.ds(pl.multiple_of(c * 4 * LANES, LANES), 4 * LANES)
        for acc in accs:
            acc[at, :] = jnp.zeros((4 * LANES, LANES), F32)
        return carry

    lax.fori_loop(0, face_len // (2 * LANES), clear, 0)
    gram_acc[...] = jnp.zeros_like(gram_acc)
    turn_load.wait()
    cos, sin = turn_ref[:vecs], turn_ref[8 : 8 + vecs]

    def turned(pair, sign):
        n = pair.shape[1] // LANES
        c = jnp.concatenate([cos] * n, axis=1)
        s = jnp.concatenate([sin] * n, axis=1) * sign
        a, b = pair[:vecs], pair[vecs:]
        return jnp.concatenate([c * a - s * b, s * a + c * b], axis=0)

    unit = (iota((LANES, LANES), 0) == iota((LANES, LANES), 1)).astype(BF16)
    unit = jnp.concatenate([unit, unit], axis=1)

    def put_rows(tile, first):
        top, low = split(tile)
        tiled = jnp.concatenate(
            [jnp.concatenate([top] * copies, axis=0), jnp.concatenate([low] * copies, axis=0)],
            axis=1,
        )
        rows_x[pl.ds(first, LANES), :] = dot_nt(unit, tiled)

    many = 8

    def build_own(c, carry):
        for u in range(many):
            first = pl.multiple_of((c * many + u) * LANES, LANES)
            put_rows(own_ref[:, pl.ds(first, LANES)], first)
        return carry


    def build_face(c, carry):
        for u in range(many // 2):
            first = pl.multiple_of((c * (many // 2) + u) * LANES, LANES)
            put_rows(
                turned(high_x_ref[:, pl.ds(first, LANES)], 1.0),
                pl.multiple_of(owned_len + first, LANES),
            )
            put_rows(
                high_y_ref[:, pl.ds(first, LANES)],
                pl.multiple_of(owned_len + face_len + first, LANES),
            )
        return carry

    lax.fori_loop(0, face_len // (many // 2 * LANES), build_face, 0)
    own_load.wait()
    lax.fori_loop(0, owned_len // (many * LANES), build_own, 0)

    for load in loads:
        load.wait()

    masks = lane_masks(width, groups)

    def index_of(i, elem):
        return dofs_ref.at[pl.ds(i * capacity, capacity)][elem]

    def face_index_of(i, elem):
        return face_dofs_ref.at[pl.ds(i * face_slots, face_slots)][elem]

    unroll = 4
    steps = BLOCK_ROWS // unroll
    halves = range(0, BLOCK_ROWS, 8)
    part = nloc // steps

    def block(b, gather):
        behind = jnp.maximum(b - 1, 0)
        here = pl.multiple_of(b * block_terms, BLOCK_ROWS)
        there = pl.multiple_of(behind * block_terms, BLOCK_ROWS)
        first_term = pl.multiple_of(behind * block_terms, BLOCK_ROWS)
        first_elem = b * block_elems

        def step(t, c):
            totals = [[None] * len(halves) for _ in range(part)]
            for i in range(nloc):
                if gather:
                    for u in range(unroll):
                        g = t * unroll + u
                        elem = first_elem + g * groups
                        rows = [
                            rows_x[pl.ds(index_of(i, elem + k), 1), :] for k in range(groups)
                        ]
                        gath[pl.ds(here + i * BLOCK_ROWS + g, 1), :] = pick(masks, rows)
                values = [
                    gath[pl.ds(pl.multiple_of(there + i * BLOCK_ROWS + h, 8), 8), :] for h in halves
                ]
                for q in range(part):
                    coef = coef_ref[(t * part + q) * nloc + i]
                    for n, value in enumerate(values):
                        product = coef * value
                        totals[q][n] = product if i == 0 else totals[q][n] + product
            for n, h in enumerate(halves):
                scale = scale_ref[pl.ds(pl.multiple_of(behind * BLOCK_ROWS + h, 8), 8), :]
                for q in range(part):
                    at = first_term + (t * part + q) * BLOCK_ROWS + h
                    term_ref[pl.ds(pl.multiple_of(at, 8), 8), :] = totals[q][n] * scale
            return c

        lax.fori_loop(0, steps, step, 0)

    def send(b):
        at = pl.ds(pl.multiple_of(b * block_terms, BLOCK_ROWS), block_terms)
        return pltpu.make_async_copy(term_ref.at[at], term_hbm.at[at], term_sems.at[b])

    def face_block(b, carry):
        add_block(term_ref, accs, face_index_of, index_of, b, nloc, groups)
        return carry

    live = count_ref[0]
    blocks = (live + block_elems - 1) // block_elems
    face_blocks = jnp.minimum(blocks, face_slots // block_elems)

    def full_block(b, carry):
        block(b, True)

        @pl.when(b > 0)
        def _():
            send(b - 1).start()

        return carry

    lax.fori_loop(0, blocks, full_block, 0)
    block(blocks, False)
    send(blocks - 1).start()
    lax.fori_loop(0, face_blocks, face_block, 0)

    deep = DEEP * block_terms
    zero_block = jnp.zeros((block_terms, LANES), F32)
    chunks = (blocks + DEEP - 1) // DEEP

    def blank(b, carry):
        at = pl.ds(pl.multiple_of(b * block_terms, BLOCK_ROWS), block_terms)
        gath[at, :] = zero_block
        term_ref[at, :] = zero_block
        return carry

    lax.fori_loop(blocks, chunks * DEEP, blank, 0)

    def products(c, carry):
        at = pl.ds(pl.multiple_of(c * deep, BLOCK_ROWS), deep)
        left, left_low = split(gath[at, :])
        right, right_low = split(term_ref[at, :])
        gram_acc[...] += lax.dot_general(
            jnp.concatenate([left, left, left_low], axis=0),
            jnp.concatenate([right, right_low, right], axis=0),
            (((0,), (0,)), ((), ())),
            preferred_element_type=F32,
        )
        return carry

    lax.fori_loop(0, chunks, products, 0)
    folder = folder_of(width)
    wide = 2 * LANES

    def folded(first):
        at = pl.ds(first, wide)
        total = pick(masks, [acc[at, :] for acc in accs])
        return dot_nt(folder, jnp.concatenate(split(total), axis=1))

    def fold_face(c, carry):
        for u in range(4):
            first = pl.multiple_of((4 * c + u) * wide, wide)
            at = pl.ds(first, wide)
            total = folded(first)
            side_x_ref[:width, at] = turned(total[:width], -1.0)
            side_x_ref[width:, at] = turned(total[width:], -1.0)
            side_y_ref[:, at] = folded(pl.multiple_of(face_len + first, wide))
        return carry

    lax.fori_loop(0, face_len // (4 * wide), fold_face, 0)

    whole = gram_acc[...]
    total = whole[:width]
    for k in range(1, groups):
        part = whole[2 * width * k : 2 * width * k + width]
        total = total + pltpu.roll(part, LANES - 2 * width * k, 1)
    re_left, im_left = total[:vecs], total[vecs:]
    lane = iota((vecs, LANES), 1)
    real_here = lane // vecs % 2 == 0
    swapped = jnp.where(
        real_here, pltpu.roll(im_left, LANES - vecs, 1), -pltpu.roll(im_left, vecs, 1)
    )
    joined = re_left + swapped
    for n in range(gram_ref.shape[0]):
        gram_ref[n] = joined

    def sent(b, carry):
        send(b).wait()
        return carry

    lax.fori_loop(0, blocks, sent, 0)


def add_kernel(
    width, nloc, interior, count_ref, table_hbm, term_hbm, curl_hbm, mass_hbm, face_ref,
    dofs_ref, term_ref, images, sem, term_sems, out_sems, *accs
):
    owned_len = curl_hbm.shape[1]
    groups = LANES // (2 * width)
    capacity = term_ref.shape[0] // nloc * groups
    block_elems = groups * BLOCK_ROWS
    block_terms = nloc * BLOCK_ROWS
    load = pltpu.make_async_copy(table_hbm, dofs_ref, sem)
    load.start()
    live = count_ref[0]
    blocks = (live + block_elems - 1) // block_elems

    def fetch(b):
        at = pl.ds(pl.multiple_of(b * block_terms, BLOCK_ROWS), block_terms)
        return pltpu.make_async_copy(term_hbm.at[at], term_ref.at[at], term_sems.at[b])

    def fetch_all(b, carry):
        fetch(b).start()
        return carry

    lax.fori_loop(0, blocks, fetch_all, 0)
    many = 4
    zero_tile = jnp.zeros((many * LANES, LANES), F32)

    def clear(c, carry):
        at = pl.ds(pl.multiple_of(c * many * LANES, LANES), many * LANES)
        for acc in accs:
            acc[at, :] = zero_tile
        return carry

    lax.fori_loop(0, owned_len // (many * LANES), clear, 0)
    load.wait()

    def index_of(i, elem):
        return dofs_ref.at[pl.ds(i * capacity, capacity)][elem]

    def block(b, carry):
        fetch(b).wait()
        add_block(term_ref, accs, index_of, index_of, b, nloc, groups)
        return carry

    lax.fori_loop(0, blocks, block, 0)

    masks = lane_masks(width, groups)
    folder = folder_of(width)
    wide = 2 * LANES
    many = 4
    span = many * wide

    def fold_some(first, curl, mass):
        for u in range(many):
            at = pl.ds(pl.multiple_of(first + u * wide, wide), wide)
            total = pick(masks, [acc[at, :] for acc in accs])
            total = dot_nt(folder, jnp.concatenate(split(total), axis=1))
            to = slice(u * wide, (u + 1) * wide)
            curl[:, to] = total[:width]
            mass[:, to] = total[width:]

    moves = []
    for c in range(owned_len // span):
        at = pl.ds(c * span, span)
        if c * span < interior:
            fold_some(c * span, images.at[0, :, at], images.at[1, :, at])
            for n, image in enumerate((curl_hbm, mass_hbm)):
                moves.append(
                    pltpu.make_async_copy(
                        images.at[n, :, at], image.at[:, at], out_sems.at[2 * c + n]
                    )
                )
                moves[-1].start()
        else:
            at = pl.ds(c * span - interior, span)
            fold_some(c * span, face_ref.at[0, :, at], face_ref.at[1, :, at])
    for move in moves:
        move.wait()


def finish_kernel(
    width, scale, curl_in, mass_in, face_ref, back_x_ref, back_y_ref, gram_ref,
    curl_out, mass_out, gram_out, faces, sems,
):
    del curl_in, mass_in
    face_len = back_x_ref.shape[1]
    outer = pl.ds(curl_out.shape[1] - 2 * face_len, 2 * face_len)
    moves = []
    for n, image in enumerate((curl_out, mass_out)):
        rows = slice(n * width, (n + 1) * width)
        faces[n, :, :face_len] = face_ref[n, :, :face_len] + back_x_ref[rows, :]
        faces[n, :, face_len:] = face_ref[n, :, face_len:] + back_y_ref[rows, :]
        moves.append(pltpu.make_async_copy(faces.at[n], image.at[:, outer], sems.at[n]))
        moves[-1].start()
    total = gram_ref[0]
    for d in range(1, gram_ref.shape[0]):
        total = total + gram_ref[d]
    total = total * scale
    vecs = total.shape[0]
    for q in range(4):
        shifted = total if q == 0 else pltpu.roll(total, LANES - q * vecs, 1)
        gram_out[q * vecs : (q + 1) * vecs, :] = shifted[:, :vecs]
    for move in moves:
        move.wait()


def on_device(
    trial_block,
    stiff_coef,
    mass_coef,
    elem_count,
    elem_dofs,
    pairing,
    bloch_fraction,
    stiff_ref,
    mass_ref,
):
    own_block = trial_block[0, 0]
    vecs, owned_len = own_block.shape[1:]
    face_len = pairing.shape[0]
    interior = owned_len - 2 * face_len
    width = 2 * vecs
    groups = LANES // (2 * width)
    capacity, nloc = elem_dofs.shape[2:]
    face_slots = capacity // 8
    devices = lax.axis_size("px") * lax.axis_size("py")
    own_rows = own_block.reshape(width, owned_len)
    low_x = own_rows[:, interior : interior + face_len]
    low_y = own_rows[:, interior + face_len :]
    high_x = lax.ppermute(low_x, "px", ring_route("px", -1))
    high_y = lax.ppermute(low_y, "py", line_route("py", -1))
    live = elem_count[0]
    smem = pl.BlockSpec(memory_space=pltpu.SMEM)
    vmem = pl.BlockSpec(memory_space=pltpu.VMEM)
    left = pl.BlockSpec(memory_space=pl.ANY)

    limit = 62 * 1024 * 1024
    params = pltpu.CompilerParams(vmem_limit_bytes=limit)

    def in_hbm(*values):
        return [pltpu.with_memory_space_constraint(value, pltpu.HBM) for value in values]

    table, own_table, face_table, scale, turn, coef = pl.pallas_call(
        functools.partial(prepare_kernel, owned_len, face_len, width),
        out_shape=(
            jax.ShapeDtypeStruct((nloc + 2, 1, capacity), jnp.int32),
            jax.ShapeDtypeStruct((nloc + 2, 1, capacity), jnp.int32),
            jax.ShapeDtypeStruct((-(-nloc // 8) * 8, face_slots), jnp.int32),
            jax.ShapeDtypeStruct((capacity // groups, LANES), F32),
            jax.ShapeDtypeStruct((16, LANES), F32),
            jax.ShapeDtypeStruct((nloc * nloc, 8, LANES), F32),
        ),
        in_specs=[smem] * 4 + [vmem] * 4,
        out_specs=[vmem] * 5 + [left],
        scratch_shapes=[
            pltpu.VMEM((nloc * nloc, 8, LANES), F32),
            pltpu.SemaphoreType.DMA,
        ],
        compiler_params=params,
        name="prepare",
    )(
        live,
        bloch_fraction,
        stiff_ref,
        mass_ref,
        elem_dofs.transpose(0, 3, 1, 2).reshape(nloc, 1, capacity),
        pairing.reshape(-1, LANES),
        stiff_coef[0],
        mass_coef[0],
    )
    table = table.reshape(-1)
    own_table = own_table.reshape(-1)
    face_table = face_table.reshape(-1)

    extent = owned_len + 2 * face_len
    blocks = capacity // (groups * BLOCK_ROWS)
    term_rows = nloc * capacity // groups
    terms, side_x, side_y, gram = pl.pallas_call(
        functools.partial(term_kernel, width, nloc),
        out_shape=(
            pltpu.HBM((term_rows, LANES), F32),
            jax.ShapeDtypeStruct((2 * width, face_len), F32),
            jax.ShapeDtypeStruct((2 * width, face_len), F32),
            jax.ShapeDtypeStruct((devices, vecs, LANES), F32),
        ),
        in_specs=[smem] + [left] * 6 + [vmem] * 2,
        out_specs=[left] + [vmem] * 3,
        scratch_shapes=[
            pltpu.SMEM(table.shape, jnp.int32),
            pltpu.SMEM(face_table.shape, jnp.int32),
            pltpu.VMEM(turn.shape, F32),
            pltpu.VMEM(own_rows.shape, F32),
            pltpu.VMEM(scale.shape, F32),
            pltpu.VMEM(coef.shape, F32),
            pltpu.VMEM((term_rows, LANES), F32),
            pltpu.VMEM((extent, LANES), F32),
            pltpu.VMEM((term_rows, LANES), F32),
            pltpu.VMEM((LANES, LANES), F32),
            pltpu.SemaphoreType.DMA((6,)),
            pltpu.SemaphoreType.DMA((blocks,)),
        ]
        + [pltpu.VMEM((2 * face_len + 8, LANES), F32)] * N_ACC,
        compiler_params=pltpu.CompilerParams(vmem_limit_bytes=TERM_MIB * 1024 * 1024),
        name="terms",
    )(live, *in_hbm(table, face_table, turn, own_rows, scale, coef), high_x, high_y)

    back_x = lax.ppermute(side_x, "px", ring_route("px", 1))
    back_y = lax.ppermute(side_y, "py", line_route("py", 1))
    gathered = lax.all_to_all(gram, ("px", "py"), 0, 0)

    curl, mass, faces = pl.pallas_call(
        functools.partial(add_kernel, width, nloc, interior),
        out_shape=(
            jax.ShapeDtypeStruct((width, owned_len), F32),
            jax.ShapeDtypeStruct((width, owned_len), F32),
            jax.ShapeDtypeStruct((2, width, 2 * face_len), F32),
        ),
        in_specs=[smem, left, left],
        out_specs=[left, left, vmem],
        scratch_shapes=[
            pltpu.SMEM(own_table.shape, jnp.int32),
            pltpu.VMEM((term_rows, LANES), F32),
            pltpu.VMEM((2, width, interior), F32),
            pltpu.SemaphoreType.DMA,
            pltpu.SemaphoreType.DMA((blocks,)),
            pltpu.SemaphoreType.DMA((2 * owned_len // (8 * LANES),)),
        ]
        + [pltpu.VMEM((owned_len + 8, LANES), F32)] * N_ACC,
        compiler_params=pltpu.CompilerParams(vmem_limit_bytes=ADD_MIB * 1024 * 1024),
        cost_estimate=pl.CostEstimate(
            flops=40 * 1024 * 1024 * 1024, bytes_accessed=40 * 1024 * 1024, transcendentals=0
        ),
        name="adds",
    )(live, *in_hbm(own_table, terms))

    curl, mass, gram = pl.pallas_call(
        functools.partial(finish_kernel, width, 1.0 / float(devices * owned_len)),
        out_shape=(
            jax.ShapeDtypeStruct((width, owned_len), F32),
            jax.ShapeDtypeStruct((width, owned_len), F32),
            jax.ShapeDtypeStruct((4 * vecs, vecs), F32),
        ),
        in_specs=[left] * 2 + [vmem] * 4,
        out_specs=[left, left, vmem],
        scratch_shapes=[
            pltpu.VMEM((2, width, 2 * face_len), F32),
            pltpu.SemaphoreType.DMA((2,)),
        ],
        input_output_aliases={0: 0, 1: 1},
        compiler_params=pltpu.CompilerParams(vmem_limit_bytes=8 * 1024 * 1024),
        name="finish",
    )(curl, mass, faces, back_x, back_y, gathered)
    shape = (1, 1, 2, vecs, owned_len)
    return curl.reshape(shape), mass.reshape(shape), gram.reshape(2, 2, vecs, vecs)


def solution(mesh):
    return jax.shard_map(
        on_device,
        mesh=mesh,
        in_specs=(
            P("px", "py", None, None, None),
            P("px", "py", None),
            P("px", "py", None),
            P("px", "py"),
            P("px", "py", None, None),
            P(),
            P(),
            P(),
            P(),
        ),
        out_specs=(P("px", "py", None, None, None), P("px", "py", None, None, None), P()),
        check_vma=False,
    )
```

```python
import functools
import math

import jax
import jax.numpy as jnp
from jax import lax
from jax.experimental import pallas as pl
from jax.experimental.pallas import tpu as pltpu
from jax.sharding import PartitionSpec as P


LANES = 128
BLOCK_ROWS = 16
SUB_ROWS = 8
PAIR = 2
TERM_MIB = 32
ADD_MIB = 26
STEP = 4
DEEP = 4
N_ACC = 4
F32 = jnp.float32
BF16 = jnp.bfloat16


def ring_route(axis, steps):
    count = lax.axis_size(axis)
    return [(source, (source + steps) % count) for source in range(count)]


def line_route(axis, distance):
    devices = range(lax.axis_size(axis))
    return [(i - distance, i) for i in devices if i - distance in devices]


def iota(shape, axis):
    return lax.broadcasted_iota(jnp.int32, shape, axis)


def split(x):
    top = x.astype(BF16)
    return top, (x - top.astype(F32)).astype(BF16)


def dot_nt(left, right):
    return lax.dot_general(
        left, right, (((1,), (1,)), ((), ())), preferred_element_type=F32
    )


def gather_lanes(table_ref, index):
    high = index // LANES
    low = index % LANES
    found = jnp.zeros_like(index)
    for r in range(table_ref.shape[0]):
        line = jnp.broadcast_to(table_ref[r : r + 1, :], index.shape)
        found = jnp.where(high == r, jnp.take_along_axis(line, low, axis=1), found)
    return found


def prepare_kernel(
    owned_len, face_len, width, count_ref, bloch_ref, stiff_elem_ref, mass_elem_ref,
    dofs_ref, pair_ref, stiff_ref, mass_ref,
    table_ref, own_table_ref, face_table_ref, scale_ref, turn_ref, coef_hbm, coef_ref, coef_sem,
):
    nloc, _, capacity = dofs_ref.shape
    face_slots = face_table_ref.shape[1]
    groups = LANES // (2 * width)
    at_end = lax.axis_index("px") == lax.axis_size("px") - 1
    live = count_ref[0]

    curl_lane = iota((8, LANES), 1) // width % 2 == 0

    def build_coef(j, carry):
        for i in range(nloc):
            coef_ref[j * nloc + i] = jnp.where(curl_lane, stiff_elem_ref[j, i], mass_elem_ref[j, i])
        return carry

    lax.fori_loop(0, nloc, build_coef, 0)
    coef_move = pltpu.make_async_copy(coef_ref, coef_hbm, coef_sem)
    coef_move.start()

    index = [dofs_ref[i] for i in range(nloc)]
    flag = jnp.zeros((1, capacity), jnp.int32)
    for i in range(nloc):
        for k in range(i + 1, min(i // STEP * STEP + STEP, nloc)):
            flag = jnp.where(index[i] == index[k], 1, flag)
    reach = 1
    for row, rows in ((1, PAIR), (0, SUB_ROWS)):
        while reach < groups * rows:
            flag = jnp.maximum(flag, pltpu.roll(flag, reach, 1))
            reach *= 2
        table_ref[nloc + row] = flag
        own_table_ref[nloc + row] = flag
    for i in range(nloc):
        table_ref[i] = index[i]
        own_table_ref[i] = jnp.minimum(index[i], owned_len)

    pad = face_table_ref.shape[0] - nloc
    for c in range(0, face_slots, LANES):
        at = slice(c, c + LANES)
        first = jnp.concatenate(
            [row[:, at] for row in index] + [jnp.zeros((pad, LANES), jnp.int32)], axis=0
        )
        local = first - owned_len
        on_face = at_end & (local >= 0) & (local < face_len)
        paired = gather_lanes(pair_ref, jnp.where(on_face, local, 0))
        first = jnp.where(on_face, paired + owned_len, first)
        face_table_ref[:, at] = jnp.where(first >= owned_len, first - owned_len, 2 * face_len)
        for i in range(nloc):
            table_ref[i, :, at] = first[i : i + 1]

    per_chunk = LANES // groups
    lane_of = iota((LANES, LANES), 0)
    elem_of = iota((LANES, LANES), 1)
    mine = elem_of % groups == lane_of // (2 * width)
    is_curl = lane_of // width % 2 == 0
    chooser = (iota((per_chunk, LANES), 1) // groups == iota((per_chunk, LANES), 0)).astype(BF16)
    chooser = jnp.concatenate([chooser, chooser], axis=1)
    for c in range(capacity // LANES):
        at = slice(c * LANES, (c + 1) * LANES)
        scales = jnp.where(is_curl, stiff_ref[:, at], mass_ref[:, at])
        scales = jnp.where(mine & (c * LANES + elem_of < live), scales, 0.0)
        scale_ref[c * per_chunk : (c + 1) * per_chunk, :] = dot_nt(
            chooser, jnp.concatenate(split(scales), axis=1)
        )

    ratio = jnp.full((8, LANES), bloch_ref[0].astype(F32), F32) / bloch_ref[1].astype(F32)
    angle = (2.0 * math.pi) * jnp.where(at_end, ratio, 0.0)
    turn_ref[:8] = jnp.cos(angle)
    turn_ref[8:] = jnp.sin(angle)
    coef_move.wait()


def lane_masks(width, groups):
    lane = iota((1, LANES), 1) // (2 * width)
    return [lane == k for k in range(groups)]


def pick(masks, parts):
    out = parts[-1]
    for mask, part in zip(masks[-2::-1], parts[-2::-1]):
        out = jnp.where(mask, part, out)
    return out


def folder_of(width):
    rows = 2 * width
    folder = (iota((rows, LANES), 1) % rows == iota((rows, LANES), 0)).astype(BF16)
    return jnp.concatenate([folder, folder], axis=1)


def add_block(term_ref, accs, index_of, flag_of, b, nloc, groups):
    def part(h, carry):
        first_row = b * nloc * BLOCK_ROWS + h * SUB_ROWS
        first_elem = (b * (BLOCK_ROWS // SUB_ROWS) + h) * SUB_ROWS * groups

        def add_pair(t, step):
            for u in range(PAIR):
                g = t * PAIR + u
                elem = first_elem + g * groups
                for j in range(0, nloc, step):
                    slots = range(j, min(j + step, nloc))
                    new = [term_ref[pl.ds(first_row + s * BLOCK_ROWS + g, 1), :] for s in slots]
                    for k in range(groups):
                        places = [pl.ds(index_of(s, elem + k), 1) for s in slots]
                        sums = [accs[k][at, :] + row for at, row in zip(places, new)]
                        for at, row in zip(places, sums):
                            accs[k][at, :] = row

        def plain(t, c):
            add_pair(t, STEP)
            return c

        def careful(t, c):
            repeated = flag_of(nloc + 1, first_elem + (t + 1) * PAIR * groups - 1)

            @pl.when(repeated == 0)
            def _():
                add_pair(t, STEP)

            @pl.when(repeated != 0)
            def _():
                add_pair(t, 1)

            return c

        clash = flag_of(nloc, first_elem + SUB_ROWS * groups - 1)

        @pl.when(clash == 0)
        def _():
            lax.fori_loop(0, SUB_ROWS // PAIR, plain, 0)

        @pl.when(clash != 0)
        def _():
            lax.fori_loop(0, SUB_ROWS // PAIR, careful, 0)

        return carry

    lax.fori_loop(0, BLOCK_ROWS // SUB_ROWS, part, 0)


def term_kernel(
    width,
    nloc,
    count_ref,
    table_hbm,
    face_table_hbm,
    turn_hbm,
    own_hbm,
    scale_hbm,
    coef_hbm,
    high_x_ref,
    high_y_ref,
    term_hbm,
    side_x_ref,
    side_y_ref,
    gram_ref,
    dofs_ref,
    face_dofs_ref,
    turn_ref,
    own_ref,
    scale_ref,
    coef_ref,
    term_ref,
    rows_x,
    gath,
    gram_acc,
    sems,
    term_sems,
    *accs,
):
    owned_len = own_ref.shape[1]
    face_len = high_x_ref.shape[1]
    vecs = width // 2
    groups = LANES // (2 * width)
    capacity = scale_ref.shape[0] * groups
    face_slots = capacity // 8
    copies = LANES // width
    block_elems = groups * BLOCK_ROWS
    block_terms = nloc * BLOCK_ROWS

    own_load, turn_load, *loads = [
        pltpu.make_async_copy(source, target, sems.at[n])
        for n, (source, target) in enumerate(
            (
                (own_hbm, own_ref),
                (turn_hbm, turn_ref),
                (table_hbm, dofs_ref),
                (face_table_hbm, face_dofs_ref),
                (coef_hbm, coef_ref),
                (scale_hbm, scale_ref),
            )
        )
    ]
    for load in (own_load, turn_load, *loads):
        load.start()

    def clear(c, carry):
        at = pl.ds(pl.multiple_of(c * 4 * LANES, LANES), 4 * LANES)
        for acc in accs:
            acc[at, :] = jnp.zeros((4 * LANES, LANES), F32)
        return carry

    lax.fori_loop(0, face_len // (2 * LANES), clear, 0)
    gram_acc[...] = jnp.zeros_like(gram_acc)
    turn_load.wait()
    cos, sin = turn_ref[:vecs], turn_ref[8 : 8 + vecs]

    def turned(pair, sign):
        n = pair.shape[1] // LANES
        c = jnp.concatenate([cos] * n, axis=1)
        s = jnp.concatenate([sin] * n, axis=1) * sign
        a, b = pair[:vecs], pair[vecs:]
        return jnp.concatenate([c * a - s * b, s * a + c * b], axis=0)

    unit = (iota((LANES, LANES), 0) == iota((LANES, LANES), 1)).astype(BF16)
    unit = jnp.concatenate([unit, unit], axis=1)

    def put_rows(tile, first):
        top, low = split(tile)
        tiled = jnp.concatenate(
            [jnp.concatenate([top] * copies, axis=0), jnp.concatenate([low] * copies, axis=0)],
            axis=1,
        )
        rows_x[pl.ds(first, LANES), :] = dot_nt(unit, tiled)

    many = 8

    def build_own(c, carry):
        for u in range(many):
            first = pl.multiple_of((c * many + u) * LANES, LANES)
            put_rows(own_ref[:, pl.ds(first, LANES)], first)
        return carry


    def build_face(c, carry):
        for u in range(many // 2):
            first = pl.multiple_of((c * (many // 2) + u) * LANES, LANES)
            put_rows(
                turned(high_x_ref[:, pl.ds(first, LANES)], 1.0),
                pl.multiple_of(owned_len + first, LANES),
            )
            put_rows(
                high_y_ref[:, pl.ds(first, LANES)],
                pl.multiple_of(owned_len + face_len + first, LANES),
            )
        return carry

    lax.fori_loop(0, face_len // (many // 2 * LANES), build_face, 0)
    own_load.wait()
    lax.fori_loop(0, owned_len // (many * LANES), build_own, 0)

    for load in loads:
        load.wait()

    masks = lane_masks(width, groups)

    def index_of(i, elem):
        return dofs_ref.at[pl.ds(i * capacity, capacity)][elem]

    def face_index_of(i, elem):
        return face_dofs_ref.at[pl.ds(i * face_slots, face_slots)][elem]

    unroll = 4
    steps = BLOCK_ROWS // unroll
    halves = range(0, BLOCK_ROWS, 8)
    part = nloc // steps

    def block(b, gather):
        behind = jnp.maximum(b - 1, 0)
        here = pl.multiple_of(b * block_terms, BLOCK_ROWS)
        there = pl.multiple_of(behind * block_terms, BLOCK_ROWS)
        first_term = pl.multiple_of(behind * block_terms, BLOCK_ROWS)
        first_elem = b * block_elems

        def step(t, c):
            totals = [[None] * len(halves) for _ in range(part)]
            for i in range(nloc):
                if gather:
                    for u in range(unroll):
                        g = t * unroll + u
                        elem = first_elem + g * groups
                        rows = [
                            rows_x[pl.ds(index_of(i, elem + k), 1), :] for k in range(groups)
                        ]
                        gath[pl.ds(here + i * BLOCK_ROWS + g, 1), :] = pick(masks, rows)
                values = [
                    gath[pl.ds(pl.multiple_of(there + i * BLOCK_ROWS + h, 8), 8), :] for h in halves
                ]
                for q in range(part):
                    coef = coef_ref[(t * part + q) * nloc + i]
                    for n, value in enumerate(values):
                        product = coef * value
                        totals[q][n] = product if i == 0 else totals[q][n] + product
            for n, h in enumerate(halves):
                scale = scale_ref[pl.ds(pl.multiple_of(behind * BLOCK_ROWS + h, 8), 8), :]
                for q in range(part):
                    at = first_term + (t * part + q) * BLOCK_ROWS + h
                    term_ref[pl.ds(pl.multiple_of(at, 8), 8), :] = totals[q][n] * scale
            return c

        lax.fori_loop(0, steps, step, 0)

    def send(b):
        at = pl.ds(pl.multiple_of(b * block_terms, BLOCK_ROWS), block_terms)
        return pltpu.make_async_copy(term_ref.at[at], term_hbm.at[at], term_sems.at[b])

    def face_block(b, carry):
        add_block(term_ref, accs, face_index_of, index_of, b, nloc, groups)
        return carry

    live = count_ref[0]
    blocks = (live + block_elems - 1) // block_elems
    face_blocks = jnp.minimum(blocks, face_slots // block_elems)

    def full_block(b, carry):
        block(b, True)

        @pl.when(b > 0)
        def _():
            send(b - 1).start()

        return carry

    lax.fori_loop(0, blocks, full_block, 0)
    block(blocks, False)
    send(blocks - 1).start()
    lax.fori_loop(0, face_blocks, face_block, 0)

    deep = DEEP * block_terms
    zero_block = jnp.zeros((block_terms, LANES), F32)
    chunks = (blocks + DEEP - 1) // DEEP

    def blank(b, carry):
        at = pl.ds(pl.multiple_of(b * block_terms, BLOCK_ROWS), block_terms)
        gath[at, :] = zero_block
        term_ref[at, :] = zero_block
        return carry

    lax.fori_loop(blocks, chunks * DEEP, blank, 0)

    def products(c, carry):
        at = pl.ds(pl.multiple_of(c * deep, BLOCK_ROWS), deep)
        left, left_low = split(gath[at, :])
        right, right_low = split(term_ref[at, :])
        gram_acc[...] += lax.dot_general(
            jnp.concatenate([left, left, left_low], axis=0),
            jnp.concatenate([right, right_low, right], axis=0),
            (((0,), (0,)), ((), ())),
            preferred_element_type=F32,
        )
        return carry

    lax.fori_loop(0, chunks, products, 0)
    folder = folder_of(width)
    wide = 2 * LANES

    def folded(first):
        at = pl.ds(first, wide)
        total = pick(masks, [acc[at, :] for acc in accs])
        return dot_nt(folder, jnp.concatenate(split(total), axis=1))

    def fold_face(c, carry):
        for u in range(4):
            first = pl.multiple_of((4 * c + u) * wide, wide)
            at = pl.ds(first, wide)
            total = folded(first)
            side_x_ref[:width, at] = turned(total[:width], -1.0)
            side_x_ref[width:, at] = turned(total[width:], -1.0)
            side_y_ref[:, at] = folded(pl.multiple_of(face_len + first, wide))
        return carry

    lax.fori_loop(0, face_len // (4 * wide), fold_face, 0)

    whole = gram_acc[...]
    total = whole[:width]
    for k in range(1, groups):
        part = whole[2 * width * k : 2 * width * k + width]
        total = total + pltpu.roll(part, LANES - 2 * width * k, 1)
    re_left, im_left = total[:vecs], total[vecs:]
    lane = iota((vecs, LANES), 1)
    real_here = lane // vecs % 2 == 0
    swapped = jnp.where(
        real_here, pltpu.roll(im_left, LANES - vecs, 1), -pltpu.roll(im_left, vecs, 1)
    )
    joined = re_left + swapped
    for n in range(gram_ref.shape[0]):
        gram_ref[n] = joined

    def sent(b, carry):
        send(b).wait()
        return carry

    lax.fori_loop(0, blocks, sent, 0)


def add_kernel(
    width, nloc, interior, count_ref, table_hbm, term_hbm, curl_hbm, mass_hbm, face_ref,
    dofs_ref, term_ref, images, sem, term_sems, out_sems, *accs
):
    owned_len = curl_hbm.shape[1]
    groups = LANES // (2 * width)
    capacity = term_ref.shape[0] // nloc * groups
    block_elems = groups * BLOCK_ROWS
    block_terms = nloc * BLOCK_ROWS
    load = pltpu.make_async_copy(table_hbm, dofs_ref, sem)
    load.start()
    live = count_ref[0]
    blocks = (live + block_elems - 1) // block_elems

    def fetch(b):
        at = pl.ds(pl.multiple_of(b * block_terms, BLOCK_ROWS), block_terms)
        return pltpu.make_async_copy(term_hbm.at[at], term_ref.at[at], term_sems.at[b])

    def fetch_all(b, carry):
        fetch(b).start()
        return carry

    lax.fori_loop(0, blocks, fetch_all, 0)
    many = 4
    zero_tile = jnp.zeros((many * LANES, LANES), F32)

    def clear(c, carry):
        at = pl.ds(pl.multiple_of(c * many * LANES, LANES), many * LANES)
        for acc in accs:
            acc[at, :] = zero_tile
        return carry

    lax.fori_loop(0, owned_len // (many * LANES), clear, 0)
    load.wait()

    def index_of(i, elem):
        return dofs_ref.at[pl.ds(i * capacity, capacity)][elem]

    def block(b, carry):
        fetch(b).wait()
        add_block(term_ref, accs, index_of, index_of, b, nloc, groups)
        return carry

    lax.fori_loop(0, blocks, block, 0)

    masks = lane_masks(width, groups)
    folder = folder_of(width)
    wide = 2 * LANES
    many = 4
    span = many * wide

    def fold_some(first, curl, mass):
        for u in range(many):
            at = pl.ds(pl.multiple_of(first + u * wide, wide), wide)
            total = pick(masks, [acc[at, :] for acc in accs])
            total = dot_nt(folder, jnp.concatenate(split(total), axis=1))
            to = slice(u * wide, (u + 1) * wide)
            curl[:, to] = total[:width]
            mass[:, to] = total[width:]

    moves = []
    for c in range(owned_len // span):
        at = pl.ds(c * span, span)
        if c * span < interior:
            fold_some(c * span, images.at[0, :, at], images.at[1, :, at])
            for n, image in enumerate((curl_hbm, mass_hbm)):
                moves.append(
                    pltpu.make_async_copy(
                        images.at[n, :, at], image.at[:, at], out_sems.at[2 * c + n]
                    )
                )
                moves[-1].start()
        else:
            at = pl.ds(c * span - interior, span)
            fold_some(c * span, face_ref.at[0, :, at], face_ref.at[1, :, at])
    for move in moves:
        move.wait()


def finish_kernel(
    width, scale, curl_in, mass_in, face_ref, back_x_ref, back_y_ref, gram_ref,
    curl_out, mass_out, gram_out, faces, sems,
):
    del curl_in, mass_in
    face_len = back_x_ref.shape[1]
    outer = pl.ds(curl_out.shape[1] - 2 * face_len, 2 * face_len)
    moves = []
    at_start = lax.axis_index("py") == 0
    for n, image in enumerate((curl_out, mass_out)):
        rows = slice(n * width, (n + 1) * width)
        faces[n, :, :face_len] = face_ref[n, :, :face_len] + back_x_ref[rows, :]
        faces[n, :, face_len:] = face_ref[n, :, face_len:] + jnp.where(
            at_start, 0.0, back_y_ref[rows, :]
        )
        moves.append(pltpu.make_async_copy(faces.at[n], image.at[:, outer], sems.at[n]))
        moves[-1].start()
    total = gram_ref[0]
    for d in range(1, gram_ref.shape[0]):
        total = total + gram_ref[d]
    total = total * scale
    vecs = total.shape[0]
    for q in range(4):
        shifted = total if q == 0 else pltpu.roll(total, LANES - q * vecs, 1)
        gram_out[q * vecs : (q + 1) * vecs, :] = shifted[:, :vecs]
    for move in moves:
        move.wait()


def on_device(
    trial_block,
    stiff_coef,
    mass_coef,
    elem_count,
    elem_dofs,
    pairing,
    bloch_fraction,
    stiff_ref,
    mass_ref,
):
    own_block = trial_block[0, 0]
    vecs, owned_len = own_block.shape[1:]
    face_len = pairing.shape[0]
    interior = owned_len - 2 * face_len
    width = 2 * vecs
    groups = LANES // (2 * width)
    capacity, nloc = elem_dofs.shape[2:]
    face_slots = capacity // 8
    devices = lax.axis_size("px") * lax.axis_size("py")
    own_rows = own_block.reshape(width, owned_len)
    low_x = own_rows[:, interior : interior + face_len]
    low_y = own_rows[:, interior + face_len :]
    high_x = lax.ppermute(low_x, "px", ring_route("px", -1))
    high_y = lax.ppermute(low_y, "py", line_route("py", -1))
    live = elem_count[0]
    smem = pl.BlockSpec(memory_space=pltpu.SMEM)
    vmem = pl.BlockSpec(memory_space=pltpu.VMEM)
    left = pl.BlockSpec(memory_space=pl.ANY)

    limit = 62 * 1024 * 1024
    params = pltpu.CompilerParams(vmem_limit_bytes=limit)

    def in_hbm(*values):
        return [pltpu.with_memory_space_constraint(value, pltpu.HBM) for value in values]

    table, own_table, face_table, scale, turn, coef = pl.pallas_call(
        functools.partial(prepare_kernel, owned_len, face_len, width),
        out_shape=(
            jax.ShapeDtypeStruct((nloc + 2, 1, capacity), jnp.int32),
            jax.ShapeDtypeStruct((nloc + 2, 1, capacity), jnp.int32),
            jax.ShapeDtypeStruct((-(-nloc // 8) * 8, face_slots), jnp.int32),
            jax.ShapeDtypeStruct((capacity // groups, LANES), F32),
            jax.ShapeDtypeStruct((16, LANES), F32),
            jax.ShapeDtypeStruct((nloc * nloc, 8, LANES), F32),
        ),
        in_specs=[smem] * 4 + [vmem] * 4,
        out_specs=[vmem] * 5 + [left],
        scratch_shapes=[
            pltpu.VMEM((nloc * nloc, 8, LANES), F32),
            pltpu.SemaphoreType.DMA,
        ],
        compiler_params=params,
        name="prepare",
    )(
        live,
        bloch_fraction,
        stiff_ref,
        mass_ref,
        elem_dofs.transpose(0, 3, 1, 2).reshape(nloc, 1, capacity),
        pairing.reshape(-1, LANES),
        stiff_coef[0],
        mass_coef[0],
    )
    table = table.reshape(-1)
    own_table = own_table.reshape(-1)
    face_table = face_table.reshape(-1)

    extent = owned_len + 2 * face_len
    blocks = capacity // (groups * BLOCK_ROWS)
    term_rows = nloc * capacity // groups
    terms, side_x, side_y, gram = pl.pallas_call(
        functools.partial(term_kernel, width, nloc),
        out_shape=(
            pltpu.HBM((term_rows, LANES), F32),
            jax.ShapeDtypeStruct((2 * width, face_len), F32),
            jax.ShapeDtypeStruct((2 * width, face_len), F32),
            jax.ShapeDtypeStruct((devices, vecs, LANES), F32),
        ),
        in_specs=[smem] + [left] * 6 + [vmem] * 2,
        out_specs=[left] + [vmem] * 3,
        scratch_shapes=[
            pltpu.SMEM(table.shape, jnp.int32),
            pltpu.SMEM(face_table.shape, jnp.int32),
            pltpu.VMEM(turn.shape, F32),
            pltpu.VMEM(own_rows.shape, F32),
            pltpu.VMEM(scale.shape, F32),
            pltpu.VMEM(coef.shape, F32),
            pltpu.VMEM((term_rows, LANES), F32),
            pltpu.VMEM((extent, LANES), F32),
            pltpu.VMEM((term_rows, LANES), F32),
            pltpu.VMEM((LANES, LANES), F32),
            pltpu.SemaphoreType.DMA((6,)),
            pltpu.SemaphoreType.DMA((blocks,)),
        ]
        + [pltpu.VMEM((2 * face_len + 8, LANES), F32)] * N_ACC,
        compiler_params=pltpu.CompilerParams(vmem_limit_bytes=TERM_MIB * 1024 * 1024),
        name="terms",
    )(live, *in_hbm(table, face_table, turn, own_rows, scale, coef), high_x, high_y)

    back_x = lax.ppermute(side_x, "px", ring_route("px", 1))
    back_y = lax.ppermute(side_y, "py", ring_route("py", 1))
    gathered = lax.all_to_all(gram, ("px", "py"), 0, 0)

    curl, mass, faces = pl.pallas_call(
        functools.partial(add_kernel, width, nloc, interior),
        out_shape=(
            jax.ShapeDtypeStruct((width, owned_len), F32),
            jax.ShapeDtypeStruct((width, owned_len), F32),
            jax.ShapeDtypeStruct((2, width, 2 * face_len), F32),
        ),
        in_specs=[smem, left, left],
        out_specs=[left, left, vmem],
        scratch_shapes=[
            pltpu.SMEM(own_table.shape, jnp.int32),
            pltpu.VMEM((term_rows, LANES), F32),
            pltpu.VMEM((2, width, interior), F32),
            pltpu.SemaphoreType.DMA,
            pltpu.SemaphoreType.DMA((blocks,)),
            pltpu.SemaphoreType.DMA((2 * owned_len // (8 * LANES),)),
        ]
        + [pltpu.VMEM((owned_len + 8, LANES), F32)] * N_ACC,
        compiler_params=pltpu.CompilerParams(vmem_limit_bytes=ADD_MIB * 1024 * 1024),
        cost_estimate=pl.CostEstimate(
            flops=40 * 1024 * 1024 * 1024, bytes_accessed=40 * 1024 * 1024, transcendentals=0
        ),
        name="adds",
    )(live, *in_hbm(own_table, terms))

    curl, mass, gram = pl.pallas_call(
        functools.partial(finish_kernel, width, 1.0 / float(devices * owned_len)),
        out_shape=(
            jax.ShapeDtypeStruct((width, owned_len), F32),
            jax.ShapeDtypeStruct((width, owned_len), F32),
            jax.ShapeDtypeStruct((4 * vecs, vecs), F32),
        ),
        in_specs=[left] * 2 + [vmem] * 4,
        out_specs=[left, left, vmem],
        scratch_shapes=[
            pltpu.VMEM((2, width, 2 * face_len), F32),
            pltpu.SemaphoreType.DMA((2,)),
        ],
        input_output_aliases={0: 0, 1: 1},
        compiler_params=pltpu.CompilerParams(vmem_limit_bytes=8 * 1024 * 1024),
        name="finish",
    )(curl, mass, faces, back_x, back_y, gathered)
    shape = (1, 1, 2, vecs, owned_len)
    return curl.reshape(shape), mass.reshape(shape), gram.reshape(2, 2, vecs, vecs)


def solution(mesh):
    return jax.shard_map(
        on_device,
        mesh=mesh,
        in_specs=(
            P("px", "py", None, None, None),
            P("px", "py", None),
            P("px", "py", None),
            P("px", "py"),
            P("px", "py", None, None),
            P(),
            P(),
            P(),
            P(),
        ),
        out_specs=(P("px", "py", None, None, None), P("px", "py", None, None, None), P()),
        check_vma=False,
    )
```

```python
import functools
import math

import jax
import jax.numpy as jnp
from jax import lax
from jax.experimental import pallas as pl
from jax.experimental.pallas import tpu as pltpu
from jax.sharding import PartitionSpec as P


LANES = 128
BLOCK_ROWS = 16
SUB_ROWS = 8
PAIR = 2
TERM_MIB = 32
ADD_MIB = 26
STEP = 4
DEEP = 4
N_ACC = 4
F32 = jnp.float32
BF16 = jnp.bfloat16


def ring_route(axis, steps):
    count = lax.axis_size(axis)
    return [(source, (source + steps) % count) for source in range(count)]


def iota(shape, axis):
    return lax.broadcasted_iota(jnp.int32, shape, axis)


def split(x):
    top = x.astype(BF16)
    return top, (x - top.astype(F32)).astype(BF16)


def dot_nt(left, right):
    return lax.dot_general(
        left, right, (((1,), (1,)), ((), ())), preferred_element_type=F32
    )


def gather_lanes(table_ref, index):
    high = index // LANES
    low = index % LANES
    found = jnp.zeros_like(index)
    for r in range(table_ref.shape[0]):
        line = jnp.broadcast_to(table_ref[r : r + 1, :], index.shape)
        found = jnp.where(high == r, jnp.take_along_axis(line, low, axis=1), found)
    return found


def prepare_kernel(
    owned_len, face_len, width, count_ref, bloch_ref, stiff_elem_ref, mass_elem_ref,
    dofs_ref, pair_ref, stiff_ref, mass_ref,
    table_ref, own_table_ref, face_table_ref, scale_ref, turn_ref, coef_hbm, coef_ref, coef_sem,
):
    nloc, _, capacity = dofs_ref.shape
    face_slots = face_table_ref.shape[1]
    groups = LANES // (2 * width)
    at_end = lax.axis_index("px") == lax.axis_size("px") - 1
    live = count_ref[0]

    curl_lane = iota((8, LANES), 1) // width % 2 == 0

    def build_coef(j, carry):
        for i in range(nloc):
            coef_ref[j * nloc + i] = jnp.where(curl_lane, stiff_elem_ref[j, i], mass_elem_ref[j, i])
        return carry

    lax.fori_loop(0, nloc, build_coef, 0)
    coef_move = pltpu.make_async_copy(coef_ref, coef_hbm, coef_sem)
    coef_move.start()

    index = [dofs_ref[i] for i in range(nloc)]
    flag = jnp.zeros((1, capacity), jnp.int32)
    for i in range(nloc):
        for k in range(i + 1, min(i // STEP * STEP + STEP, nloc)):
            flag = jnp.where(index[i] == index[k], 1, flag)
    reach = 1
    for row, rows in ((1, PAIR), (0, SUB_ROWS)):
        while reach < groups * rows:
            flag = jnp.maximum(flag, pltpu.roll(flag, reach, 1))
            reach *= 2
        table_ref[nloc + row] = flag
        own_table_ref[nloc + row] = flag
    for i in range(nloc):
        table_ref[i] = index[i]
        own_table_ref[i] = jnp.minimum(index[i], owned_len)

    pad = face_table_ref.shape[0] - nloc
    for c in range(0, face_slots, LANES):
        at = slice(c, c + LANES)
        first = jnp.concatenate(
            [row[:, at] for row in index] + [jnp.zeros((pad, LANES), jnp.int32)], axis=0
        )
        local = first - owned_len
        on_face = at_end & (local >= 0) & (local < face_len)
        paired = gather_lanes(pair_ref, jnp.where(on_face, local, 0))
        first = jnp.where(on_face, paired + owned_len, first)
        face_table_ref[:, at] = jnp.where(first >= owned_len, first - owned_len, 2 * face_len)
        for i in range(nloc):
            table_ref[i, :, at] = first[i : i + 1]

    per_chunk = LANES // groups
    lane_of = iota((LANES, LANES), 0)
    elem_of = iota((LANES, LANES), 1)
    mine = elem_of % groups == lane_of // (2 * width)
    is_curl = lane_of // width % 2 == 0
    chooser = (iota((per_chunk, LANES), 1) // groups == iota((per_chunk, LANES), 0)).astype(BF16)
    chooser = jnp.concatenate([chooser, chooser], axis=1)
    for c in range(capacity // LANES):
        at = slice(c * LANES, (c + 1) * LANES)
        scales = jnp.where(is_curl, stiff_ref[:, at], mass_ref[:, at])
        scales = jnp.where(mine & (c * LANES + elem_of < live), scales, 0.0)
        scale_ref[c * per_chunk : (c + 1) * per_chunk, :] = dot_nt(
            chooser, jnp.concatenate(split(scales), axis=1)
        )

    ratio = jnp.full((8, LANES), bloch_ref[0].astype(F32), F32) / bloch_ref[1].astype(F32)
    angle = (2.0 * math.pi) * jnp.where(at_end, ratio, 0.0)
    turn_ref[:8] = jnp.cos(angle)
    turn_ref[8:] = jnp.sin(angle)
    coef_move.wait()


def lane_masks(width, groups):
    lane = iota((1, LANES), 1) // (2 * width)
    return [lane == k for k in range(groups)]


def pick(masks, parts):
    out = parts[-1]
    for mask, part in zip(masks[-2::-1], parts[-2::-1]):
        out = jnp.where(mask, part, out)
    return out


def folder_of(width):
    rows = 2 * width
    folder = (iota((rows, LANES), 1) % rows == iota((rows, LANES), 0)).astype(BF16)
    return jnp.concatenate([folder, folder], axis=1)


def add_block(term_ref, accs, index_of, flag_of, b, nloc, groups):
    def part(h, carry):
        first_row = b * nloc * BLOCK_ROWS + h * SUB_ROWS
        first_elem = (b * (BLOCK_ROWS // SUB_ROWS) + h) * SUB_ROWS * groups

        def add_pair(t, step):
            for u in range(PAIR):
                g = t * PAIR + u
                elem = first_elem + g * groups
                for j in range(0, nloc, step):
                    slots = range(j, min(j + step, nloc))
                    new = [term_ref[pl.ds(first_row + s * BLOCK_ROWS + g, 1), :] for s in slots]
                    for k in range(groups):
                        places = [pl.ds(index_of(s, elem + k), 1) for s in slots]
                        sums = [accs[k][at, :] + row for at, row in zip(places, new)]
                        for at, row in zip(places, sums):
                            accs[k][at, :] = row

        def plain(t, c):
            add_pair(t, STEP)
            return c

        def careful(t, c):
            repeated = flag_of(nloc + 1, first_elem + (t + 1) * PAIR * groups - 1)

            @pl.when(repeated == 0)
            def _():
                add_pair(t, STEP)

            @pl.when(repeated != 0)
            def _():
                add_pair(t, 1)

            return c

        clash = flag_of(nloc, first_elem + SUB_ROWS * groups - 1)

        @pl.when(clash == 0)
        def _():
            lax.fori_loop(0, SUB_ROWS // PAIR, plain, 0)

        @pl.when(clash != 0)
        def _():
            lax.fori_loop(0, SUB_ROWS // PAIR, careful, 0)

        return carry

    lax.fori_loop(0, BLOCK_ROWS // SUB_ROWS, part, 0)


def term_kernel(
    width,
    nloc,
    count_ref,
    table_hbm,
    face_table_hbm,
    turn_hbm,
    own_hbm,
    scale_hbm,
    coef_hbm,
    high_x_ref,
    high_y_ref,
    term_hbm,
    side_x_ref,
    side_y_ref,
    gram_ref,
    dofs_ref,
    face_dofs_ref,
    turn_ref,
    own_ref,
    scale_ref,
    coef_ref,
    term_ref,
    rows_x,
    gath,
    gram_acc,
    sems,
    term_sems,
    *accs,
):
    owned_len = own_ref.shape[1]
    face_len = high_x_ref.shape[1]
    vecs = width // 2
    groups = LANES // (2 * width)
    capacity = scale_ref.shape[0] * groups
    face_slots = capacity // 8
    copies = LANES // width
    block_elems = groups * BLOCK_ROWS
    block_terms = nloc * BLOCK_ROWS

    own_load, turn_load, *loads = [
        pltpu.make_async_copy(source, target, sems.at[n])
        for n, (source, target) in enumerate(
            (
                (own_hbm, own_ref),
                (turn_hbm, turn_ref),
                (table_hbm, dofs_ref),
                (face_table_hbm, face_dofs_ref),
                (coef_hbm, coef_ref),
                (scale_hbm, scale_ref),
            )
        )
    ]
    for load in (own_load, turn_load, *loads):
        load.start()

    def clear(c, carry):
        at = pl.ds(pl.multiple_of(c * 4 * LANES, LANES), 4 * LANES)
        for acc in accs:
            acc[at, :] = jnp.zeros((4 * LANES, LANES), F32)
        return carry

    lax.fori_loop(0, face_len // (2 * LANES), clear, 0)
    gram_acc[...] = jnp.zeros_like(gram_acc)
    turn_load.wait()
    cos, sin = turn_ref[:vecs], turn_ref[8 : 8 + vecs]

    def turned(pair, sign):
        n = pair.shape[1] // LANES
        c = jnp.concatenate([cos] * n, axis=1)
        s = jnp.concatenate([sin] * n, axis=1) * sign
        a, b = pair[:vecs], pair[vecs:]
        return jnp.concatenate([c * a - s * b, s * a + c * b], axis=0)

    unit = (iota((LANES, LANES), 0) == iota((LANES, LANES), 1)).astype(BF16)
    unit = jnp.concatenate([unit, unit], axis=1)

    def put_rows(tile, first):
        top, low = split(tile)
        tiled = jnp.concatenate(
            [jnp.concatenate([top] * copies, axis=0), jnp.concatenate([low] * copies, axis=0)],
            axis=1,
        )
        rows_x[pl.ds(first, LANES), :] = dot_nt(unit, tiled)

    many = 8
    at_last = lax.axis_index("py") == lax.axis_size("py") - 1

    def build_own(c, carry):
        for u in range(many):
            first = pl.multiple_of((c * many + u) * LANES, LANES)
            put_rows(own_ref[:, pl.ds(first, LANES)], first)
        return carry


    def build_face(c, carry):
        for u in range(many // 2):
            first = pl.multiple_of((c * (many // 2) + u) * LANES, LANES)
            put_rows(
                turned(high_x_ref[:, pl.ds(first, LANES)], 1.0),
                pl.multiple_of(owned_len + first, LANES),
            )
            put_rows(
                jnp.where(at_last, 0.0, high_y_ref[:, pl.ds(first, LANES)]),
                pl.multiple_of(owned_len + face_len + first, LANES),
            )
        return carry

    lax.fori_loop(0, face_len // (many // 2 * LANES), build_face, 0)
    own_load.wait()
    lax.fori_loop(0, owned_len // (many * LANES), build_own, 0)

    for load in loads:
        load.wait()

    masks = lane_masks(width, groups)

    def index_of(i, elem):
        return dofs_ref.at[pl.ds(i * capacity, capacity)][elem]

    def face_index_of(i, elem):
        return face_dofs_ref.at[pl.ds(i * face_slots, face_slots)][elem]

    unroll = 4
    steps = BLOCK_ROWS // unroll
    halves = range(0, BLOCK_ROWS, 8)
    part = nloc // steps

    def block(b, gather):
        behind = jnp.maximum(b - 1, 0)
        here = pl.multiple_of(b * block_terms, BLOCK_ROWS)
        there = pl.multiple_of(behind * block_terms, BLOCK_ROWS)
        first_term = pl.multiple_of(behind * block_terms, BLOCK_ROWS)
        first_elem = b * block_elems

        def step(t, c):
            totals = [[None] * len(halves) for _ in range(part)]
            for i in range(nloc):
                if gather:
                    for u in range(unroll):
                        g = t * unroll + u
                        elem = first_elem + g * groups
                        rows = [
                            rows_x[pl.ds(index_of(i, elem + k), 1), :] for k in range(groups)
                        ]
                        gath[pl.ds(here + i * BLOCK_ROWS + g, 1), :] = pick(masks, rows)
                values = [
                    gath[pl.ds(pl.multiple_of(there + i * BLOCK_ROWS + h, 8), 8), :] for h in halves
                ]
                for q in range(part):
                    coef = coef_ref[(t * part + q) * nloc + i]
                    for n, value in enumerate(values):
                        product = coef * value
                        totals[q][n] = product if i == 0 else totals[q][n] + product
            for n, h in enumerate(halves):
                scale = scale_ref[pl.ds(pl.multiple_of(behind * BLOCK_ROWS + h, 8), 8), :]
                for q in range(part):
                    at = first_term + (t * part + q) * BLOCK_ROWS + h
                    term_ref[pl.ds(pl.multiple_of(at, 8), 8), :] = totals[q][n] * scale
            return c

        lax.fori_loop(0, steps, step, 0)

    def send(b):
        at = pl.ds(pl.multiple_of(b * block_terms, BLOCK_ROWS), block_terms)
        return pltpu.make_async_copy(term_ref.at[at], term_hbm.at[at], term_sems.at[b])

    def face_block(b, carry):
        add_block(term_ref, accs, face_index_of, index_of, b, nloc, groups)
        return carry

    live = count_ref[0]
    blocks = (live + block_elems - 1) // block_elems
    face_blocks = jnp.minimum(blocks, face_slots // block_elems)

    def full_block(b, carry):
        block(b, True)

        @pl.when(b > 0)
        def _():
            send(b - 1).start()

        return carry

    lax.fori_loop(0, blocks, full_block, 0)
    block(blocks, False)
    send(blocks - 1).start()
    lax.fori_loop(0, face_blocks, face_block, 0)

    deep = DEEP * block_terms
    zero_block = jnp.zeros((block_terms, LANES), F32)
    chunks = (blocks + DEEP - 1) // DEEP

    def blank(b, carry):
        at = pl.ds(pl.multiple_of(b * block_terms, BLOCK_ROWS), block_terms)
        gath[at, :] = zero_block
        term_ref[at, :] = zero_block
        return carry

    lax.fori_loop(blocks, chunks * DEEP, blank, 0)

    def products(c, carry):
        at = pl.ds(pl.multiple_of(c * deep, BLOCK_ROWS), deep)
        left, left_low = split(gath[at, :])
        right, right_low = split(term_ref[at, :])
        gram_acc[...] += lax.dot_general(
            jnp.concatenate([left, left, left_low], axis=0),
            jnp.concatenate([right, right_low, right], axis=0),
            (((0,), (0,)), ((), ())),
            preferred_element_type=F32,
        )
        return carry

    lax.fori_loop(0, chunks, products, 0)
    folder = folder_of(width)
    wide = 2 * LANES

    def folded(first):
        at = pl.ds(first, wide)
        total = pick(masks, [acc[at, :] for acc in accs])
        return dot_nt(folder, jnp.concatenate(split(total), axis=1))

    def fold_face(c, carry):
        for u in range(4):
            first = pl.multiple_of((4 * c + u) * wide, wide)
            at = pl.ds(first, wide)
            total = folded(first)
            side_x_ref[:width, at] = turned(total[:width], -1.0)
            side_x_ref[width:, at] = turned(total[width:], -1.0)
            side_y_ref[:, at] = folded(pl.multiple_of(face_len + first, wide))
        return carry

    lax.fori_loop(0, face_len // (4 * wide), fold_face, 0)

    whole = gram_acc[...]
    total = whole[:width]
    for k in range(1, groups):
        part = whole[2 * width * k : 2 * width * k + width]
        total = total + pltpu.roll(part, LANES - 2 * width * k, 1)
    re_left, im_left = total[:vecs], total[vecs:]
    lane = iota((vecs, LANES), 1)
    real_here = lane // vecs % 2 == 0
    swapped = jnp.where(
        real_here, pltpu.roll(im_left, LANES - vecs, 1), -pltpu.roll(im_left, vecs, 1)
    )
    joined = re_left + swapped
    for n in range(gram_ref.shape[0]):
        gram_ref[n] = joined

    def sent(b, carry):
        send(b).wait()
        return carry

    lax.fori_loop(0, blocks, sent, 0)


def add_kernel(
    width, nloc, interior, count_ref, table_hbm, term_hbm, curl_hbm, mass_hbm, face_ref,
    dofs_ref, term_ref, images, sem, term_sems, out_sems, *accs
):
    owned_len = curl_hbm.shape[1]
    groups = LANES // (2 * width)
    capacity = term_ref.shape[0] // nloc * groups
    block_elems = groups * BLOCK_ROWS
    block_terms = nloc * BLOCK_ROWS
    load = pltpu.make_async_copy(table_hbm, dofs_ref, sem)
    load.start()
    live = count_ref[0]
    blocks = (live + block_elems - 1) // block_elems

    def fetch(b):
        at = pl.ds(pl.multiple_of(b * block_terms, BLOCK_ROWS), block_terms)
        return pltpu.make_async_copy(term_hbm.at[at], term_ref.at[at], term_sems.at[b])

    def fetch_all(b, carry):
        fetch(b).start()
        return carry

    lax.fori_loop(0, blocks, fetch_all, 0)
    many = 4
    zero_tile = jnp.zeros((many * LANES, LANES), F32)

    def clear(c, carry):
        at = pl.ds(pl.multiple_of(c * many * LANES, LANES), many * LANES)
        for acc in accs:
            acc[at, :] = zero_tile
        return carry

    lax.fori_loop(0, owned_len // (many * LANES), clear, 0)
    load.wait()

    def index_of(i, elem):
        return dofs_ref.at[pl.ds(i * capacity, capacity)][elem]

    def block(b, carry):
        fetch(b).wait()
        add_block(term_ref, accs, index_of, index_of, b, nloc, groups)
        return carry

    lax.fori_loop(0, blocks, block, 0)

    masks = lane_masks(width, groups)
    folder = folder_of(width)
    wide = 2 * LANES
    many = 4
    span = many * wide

    def fold_some(first, curl, mass):
        for u in range(many):
            at = pl.ds(pl.multiple_of(first + u * wide, wide), wide)
            total = pick(masks, [acc[at, :] for acc in accs])
            total = dot_nt(folder, jnp.concatenate(split(total), axis=1))
            to = slice(u * wide, (u + 1) * wide)
            curl[:, to] = total[:width]
            mass[:, to] = total[width:]

    moves = []
    for c in range(owned_len // span):
        at = pl.ds(c * span, span)
        if c * span < interior:
            fold_some(c * span, images.at[0, :, at], images.at[1, :, at])
            for n, image in enumerate((curl_hbm, mass_hbm)):
                moves.append(
                    pltpu.make_async_copy(
                        images.at[n, :, at], image.at[:, at], out_sems.at[2 * c + n]
                    )
                )
                moves[-1].start()
        else:
            at = pl.ds(c * span - interior, span)
            fold_some(c * span, face_ref.at[0, :, at], face_ref.at[1, :, at])
    for move in moves:
        move.wait()


def finish_kernel(
    width, scale, curl_in, mass_in, face_ref, back_x_ref, back_y_ref, gram_ref,
    curl_out, mass_out, gram_out, faces, sems,
):
    del curl_in, mass_in
    face_len = back_x_ref.shape[1]
    outer = pl.ds(curl_out.shape[1] - 2 * face_len, 2 * face_len)
    moves = []
    at_start = lax.axis_index("py") == 0
    for n, image in enumerate((curl_out, mass_out)):
        rows = slice(n * width, (n + 1) * width)
        faces[n, :, :face_len] = face_ref[n, :, :face_len] + back_x_ref[rows, :]
        faces[n, :, face_len:] = face_ref[n, :, face_len:] + jnp.where(
            at_start, 0.0, back_y_ref[rows, :]
        )
        moves.append(pltpu.make_async_copy(faces.at[n], image.at[:, outer], sems.at[n]))
        moves[-1].start()
    total = gram_ref[0]
    for d in range(1, gram_ref.shape[0]):
        total = total + gram_ref[d]
    total = total * scale
    vecs = total.shape[0]
    for q in range(4):
        shifted = total if q == 0 else pltpu.roll(total, LANES - q * vecs, 1)
        gram_out[q * vecs : (q + 1) * vecs, :] = shifted[:, :vecs]
    for move in moves:
        move.wait()


def on_device(
    trial_block,
    stiff_coef,
    mass_coef,
    elem_count,
    elem_dofs,
    pairing,
    bloch_fraction,
    stiff_ref,
    mass_ref,
):
    own_block = trial_block[0, 0]
    vecs, owned_len = own_block.shape[1:]
    face_len = pairing.shape[0]
    interior = owned_len - 2 * face_len
    width = 2 * vecs
    groups = LANES // (2 * width)
    capacity, nloc = elem_dofs.shape[2:]
    face_slots = capacity // 8
    devices = lax.axis_size("px") * lax.axis_size("py")
    own_rows = own_block.reshape(width, owned_len)
    low_x = own_rows[:, interior : interior + face_len]
    low_y = own_rows[:, interior + face_len :]
    high_x = lax.ppermute(low_x, "px", ring_route("px", -1))
    high_y = lax.ppermute(low_y, "py", ring_route("py", -1))
    live = elem_count[0]
    smem = pl.BlockSpec(memory_space=pltpu.SMEM)
    vmem = pl.BlockSpec(memory_space=pltpu.VMEM)
    left = pl.BlockSpec(memory_space=pl.ANY)

    limit = 62 * 1024 * 1024
    params = pltpu.CompilerParams(vmem_limit_bytes=limit)

    def in_hbm(*values):
        return [pltpu.with_memory_space_constraint(value, pltpu.HBM) for value in values]

    table, own_table, face_table, scale, turn, coef = pl.pallas_call(
        functools.partial(prepare_kernel, owned_len, face_len, width),
        out_shape=(
            jax.ShapeDtypeStruct((nloc + 2, 1, capacity), jnp.int32),
            jax.ShapeDtypeStruct((nloc + 2, 1, capacity), jnp.int32),
            jax.ShapeDtypeStruct((-(-nloc // 8) * 8, face_slots), jnp.int32),
            jax.ShapeDtypeStruct((capacity // groups, LANES), F32),
            jax.ShapeDtypeStruct((16, LANES), F32),
            jax.ShapeDtypeStruct((nloc * nloc, 8, LANES), F32),
        ),
        in_specs=[smem] * 4 + [vmem] * 4,
        out_specs=[vmem] * 5 + [left],
        scratch_shapes=[
            pltpu.VMEM((nloc * nloc, 8, LANES), F32),
            pltpu.SemaphoreType.DMA,
        ],
        compiler_params=params,
        name="prepare",
    )(
        live,
        bloch_fraction,
        stiff_ref,
        mass_ref,
        elem_dofs.transpose(0, 3, 1, 2).reshape(nloc, 1, capacity),
        pairing.reshape(-1, LANES),
        stiff_coef[0],
        mass_coef[0],
    )
    table = table.reshape(-1)
    own_table = own_table.reshape(-1)
    face_table = face_table.reshape(-1)

    extent = owned_len + 2 * face_len
    blocks = capacity // (groups * BLOCK_ROWS)
    term_rows = nloc * capacity // groups
    terms, side_x, side_y, gram = pl.pallas_call(
        functools.partial(term_kernel, width, nloc),
        out_shape=(
            pltpu.HBM((term_rows, LANES), F32),
            jax.ShapeDtypeStruct((2 * width, face_len), F32),
            jax.ShapeDtypeStruct((2 * width, face_len), F32),
            jax.ShapeDtypeStruct((devices, vecs, LANES), F32),
        ),
        in_specs=[smem] + [left] * 6 + [vmem] * 2,
        out_specs=[left] + [vmem] * 3,
        scratch_shapes=[
            pltpu.SMEM(table.shape, jnp.int32),
            pltpu.SMEM(face_table.shape, jnp.int32),
            pltpu.VMEM(turn.shape, F32),
            pltpu.VMEM(own_rows.shape, F32),
            pltpu.VMEM(scale.shape, F32),
            pltpu.VMEM(coef.shape, F32),
            pltpu.VMEM((term_rows, LANES), F32),
            pltpu.VMEM((extent, LANES), F32),
            pltpu.VMEM((term_rows, LANES), F32),
            pltpu.VMEM((LANES, LANES), F32),
            pltpu.SemaphoreType.DMA((6,)),
            pltpu.SemaphoreType.DMA((blocks,)),
        ]
        + [pltpu.VMEM((2 * face_len + 8, LANES), F32)] * N_ACC,
        compiler_params=pltpu.CompilerParams(vmem_limit_bytes=TERM_MIB * 1024 * 1024),
        name="terms",
    )(live, *in_hbm(table, face_table, turn, own_rows, scale, coef), high_x, high_y)

    back_x = lax.ppermute(side_x, "px", ring_route("px", 1))
    back_y = lax.ppermute(side_y, "py", ring_route("py", 1))
    gathered = lax.all_to_all(gram, ("px", "py"), 0, 0)

    curl, mass, faces = pl.pallas_call(
        functools.partial(add_kernel, width, nloc, interior),
        out_shape=(
            jax.ShapeDtypeStruct((width, owned_len), F32),
            jax.ShapeDtypeStruct((width, owned_len), F32),
            jax.ShapeDtypeStruct((2, width, 2 * face_len), F32),
        ),
        in_specs=[smem, left, left],
        out_specs=[left, left, vmem],
        scratch_shapes=[
            pltpu.SMEM(own_table.shape, jnp.int32),
            pltpu.VMEM((term_rows, LANES), F32),
            pltpu.VMEM((2, width, interior), F32),
            pltpu.SemaphoreType.DMA,
            pltpu.SemaphoreType.DMA((blocks,)),
            pltpu.SemaphoreType.DMA((2 * owned_len // (8 * LANES),)),
        ]
        + [pltpu.VMEM((owned_len + 8, LANES), F32)] * N_ACC,
        compiler_params=pltpu.CompilerParams(vmem_limit_bytes=ADD_MIB * 1024 * 1024),
        cost_estimate=pl.CostEstimate(
            flops=40 * 1024 * 1024 * 1024, bytes_accessed=40 * 1024 * 1024, transcendentals=0
        ),
        name="adds",
    )(live, *in_hbm(own_table, terms))

    curl, mass, gram = pl.pallas_call(
        functools.partial(finish_kernel, width, 1.0 / float(devices * owned_len)),
        out_shape=(
            jax.ShapeDtypeStruct((width, owned_len), F32),
            jax.ShapeDtypeStruct((width, owned_len), F32),
            jax.ShapeDtypeStruct((4 * vecs, vecs), F32),
        ),
        in_specs=[left] * 2 + [vmem] * 4,
        out_specs=[left, left, vmem],
        scratch_shapes=[
            pltpu.VMEM((2, width, 2 * face_len), F32),
            pltpu.SemaphoreType.DMA((2,)),
        ],
        input_output_aliases={0: 0, 1: 1},
        compiler_params=pltpu.CompilerParams(vmem_limit_bytes=8 * 1024 * 1024),
        name="finish",
    )(curl, mass, faces, back_x, back_y, gathered)
    shape = (1, 1, 2, vecs, owned_len)
    return curl.reshape(shape), mass.reshape(shape), gram.reshape(2, 2, vecs, vecs)


def solution(mesh):
    return jax.shard_map(
        on_device,
        mesh=mesh,
        in_specs=(
            P("px", "py", None, None, None),
            P("px", "py", None),
            P("px", "py", None),
            P("px", "py"),
            P("px", "py", None, None),
            P(),
            P(),
            P(),
            P(),
        ),
        out_specs=(P("px", "py", None, None, None), P("px", "py", None, None, None), P()),
        check_vma=False,
    )
```

```python
import functools
import math

import jax
import jax.numpy as jnp
from jax import lax
from jax.experimental import pallas as pl
from jax.experimental.pallas import tpu as pltpu
from jax.sharding import PartitionSpec as P


LANES = 128
BLOCK_ROWS = 16
SUB_ROWS = 8
PAIR = 2
TERM_MIB = 32
ADD_MIB = 26
STEP = 4
DEEP = 4
N_ACC = 4
F32 = jnp.float32
BF16 = jnp.bfloat16


def ring_route(axis, steps):
    count = lax.axis_size(axis)
    return [(source, (source + steps) % count) for source in range(count)]


def iota(shape, axis):
    return lax.broadcasted_iota(jnp.int32, shape, axis)


def split(x):
    top = x.astype(BF16)
    return top, (x - top.astype(F32)).astype(BF16)


def dot_nt(left, right):
    return lax.dot_general(
        left, right, (((1,), (1,)), ((), ())), preferred_element_type=F32
    )


def gather_lanes(table_ref, index):
    high = index // LANES
    low = index % LANES
    found = jnp.zeros_like(index)
    for r in range(table_ref.shape[0]):
        line = jnp.broadcast_to(table_ref[r : r + 1, :], index.shape)
        found = jnp.where(high == r, jnp.take_along_axis(line, low, axis=1), found)
    return found


def prepare_kernel(
    owned_len, face_len, width, count_ref, bloch_ref, stiff_elem_ref, mass_elem_ref,
    dofs_ref, pair_ref, stiff_ref, mass_ref,
    table_ref, own_table_ref, face_table_ref, scale_ref, turn_ref, coef_hbm, coef_ref, coef_sem,
):
    nloc, _, capacity = dofs_ref.shape
    face_slots = face_table_ref.shape[1]
    groups = LANES // (2 * width)
    at_end = lax.axis_index("px") == lax.axis_size("px") - 1
    live = count_ref[0]

    curl_lane = iota((1, LANES), 1) // width % 2 == 0

    def build_coef(j, carry):
        for i in range(nloc):
            coef_ref[pl.ds(j * nloc + i, 1), :] = jnp.where(curl_lane, stiff_elem_ref[j, i], mass_elem_ref[j, i])
        return carry

    lax.fori_loop(0, nloc, build_coef, 0)
    coef_move = pltpu.make_async_copy(coef_ref, coef_hbm, coef_sem)
    coef_move.start()

    index = [dofs_ref[i] for i in range(nloc)]
    flag = jnp.zeros((1, capacity), jnp.int32)
    for i in range(nloc):
        for k in range(i + 1, min(i // STEP * STEP + STEP, nloc)):
            flag = jnp.where(index[i] == index[k], 1, flag)
    reach = 1
    for row, rows in ((1, PAIR), (0, SUB_ROWS)):
        while reach < groups * rows:
            flag = jnp.maximum(flag, pltpu.roll(flag, reach, 1))
            reach *= 2
        table_ref[nloc + row] = flag
        own_table_ref[nloc + row] = flag
    for i in range(nloc):
        table_ref[i] = index[i]
        own_table_ref[i] = jnp.minimum(index[i], owned_len)

    pad = face_table_ref.shape[0] - nloc
    for c in range(0, face_slots, LANES):
        at = slice(c, c + LANES)
        first = jnp.concatenate(
            [row[:, at] for row in index] + [jnp.zeros((pad, LANES), jnp.int32)], axis=0
        )
        local = first - owned_len
        on_face = at_end & (local >= 0) & (local < face_len)
        paired = gather_lanes(pair_ref, jnp.where(on_face, local, 0))
        first = jnp.where(on_face, paired + owned_len, first)
        face_table_ref[:, at] = jnp.where(first >= owned_len, first - owned_len, 2 * face_len)
        for i in range(nloc):
            table_ref[i, :, at] = first[i : i + 1]

    per_chunk = LANES // groups
    lane_of = iota((LANES, LANES), 0)
    elem_of = iota((LANES, LANES), 1)
    mine = elem_of % groups == lane_of // (2 * width)
    is_curl = lane_of // width % 2 == 0
    chooser = (iota((per_chunk, LANES), 1) // groups == iota((per_chunk, LANES), 0)).astype(BF16)
    chooser = jnp.concatenate([chooser, chooser], axis=1)
    for c in range(capacity // LANES):
        at = slice(c * LANES, (c + 1) * LANES)
        scales = jnp.where(is_curl, stiff_ref[:, at], mass_ref[:, at])
        scales = jnp.where(mine & (c * LANES + elem_of < live), scales, 0.0)
        scale_ref[c * per_chunk : (c + 1) * per_chunk, :] = dot_nt(
            chooser, jnp.concatenate(split(scales), axis=1)
        )

    ratio = jnp.full((8, LANES), bloch_ref[0].astype(F32), F32) / bloch_ref[1].astype(F32)
    angle = (2.0 * math.pi) * jnp.where(at_end, ratio, 0.0)
    turn_ref[:8] = jnp.cos(angle)
    turn_ref[8:] = jnp.sin(angle)
    coef_move.wait()


def lane_masks(width, groups):
    lane = iota((1, LANES), 1) // (2 * width)
    return [lane == k for k in range(groups)]


def pick(masks, parts):
    out = parts[-1]
    for mask, part in zip(masks[-2::-1], parts[-2::-1]):
        out = jnp.where(mask, part, out)
    return out


def folder_of(width):
    rows = 2 * width
    folder = (iota((rows, LANES), 1) % rows == iota((rows, LANES), 0)).astype(BF16)
    return jnp.concatenate([folder, folder], axis=1)


def add_block(term_ref, accs, index_of, flag_of, b, nloc, groups):
    def part(h, carry):
        first_row = b * nloc * BLOCK_ROWS + h * SUB_ROWS
        first_elem = (b * (BLOCK_ROWS // SUB_ROWS) + h) * SUB_ROWS * groups

        def add_pair(t, step):
            for u in range(PAIR):
                g = t * PAIR + u
                elem = first_elem + g * groups
                for j in range(0, nloc, step):
                    slots = range(j, min(j + step, nloc))
                    new = [term_ref[pl.ds(first_row + s * BLOCK_ROWS + g, 1), :] for s in slots]
                    for k in range(groups):
                        places = [pl.ds(index_of(s, elem + k), 1) for s in slots]
                        sums = [accs[k][at, :] + row for at, row in zip(places, new)]
                        for at, row in zip(places, sums):
                            accs[k][at, :] = row

        def plain(t, c):
            add_pair(t, STEP)
            return c

        def careful(t, c):
            repeated = flag_of(nloc + 1, first_elem + (t + 1) * PAIR * groups - 1)

            @pl.when(repeated == 0)
            def _():
                add_pair(t, STEP)

            @pl.when(repeated != 0)
            def _():
                add_pair(t, 1)

            return c

        clash = flag_of(nloc, first_elem + SUB_ROWS * groups - 1)

        @pl.when(clash == 0)
        def _():
            lax.fori_loop(0, SUB_ROWS // PAIR, plain, 0)

        @pl.when(clash != 0)
        def _():
            lax.fori_loop(0, SUB_ROWS // PAIR, careful, 0)

        return carry

    lax.fori_loop(0, BLOCK_ROWS // SUB_ROWS, part, 0)


def term_kernel(
    width,
    nloc,
    count_ref,
    table_hbm,
    face_table_hbm,
    turn_hbm,
    own_hbm,
    scale_hbm,
    coef_hbm,
    high_x_ref,
    high_y_ref,
    term_hbm,
    side_x_ref,
    side_y_ref,
    gram_ref,
    dofs_ref,
    face_dofs_ref,
    turn_ref,
    own_ref,
    scale_ref,
    coef_ref,
    term_ref,
    rows_x,
    gath,
    gram_acc,
    sems,
    term_sems,
    *accs,
):
    owned_len = own_ref.shape[1]
    face_len = high_x_ref.shape[1]
    vecs = width // 2
    groups = LANES // (2 * width)
    capacity = scale_ref.shape[0] * groups
    face_slots = capacity // 8
    copies = LANES // width
    block_elems = groups * BLOCK_ROWS
    block_terms = nloc * BLOCK_ROWS

    own_load, turn_load, *loads = [
        pltpu.make_async_copy(source, target, sems.at[n])
        for n, (source, target) in enumerate(
            (
                (own_hbm, own_ref),
                (turn_hbm, turn_ref),
                (table_hbm, dofs_ref),
                (face_table_hbm, face_dofs_ref),
                (coef_hbm, coef_ref),
                (scale_hbm, scale_ref),
            )
        )
    ]
    for load in (own_load, turn_load, *loads):
        load.start()

    def clear(c, carry):
        at = pl.ds(pl.multiple_of(c * 4 * LANES, LANES), 4 * LANES)
        for acc in accs:
            acc[at, :] = jnp.zeros((4 * LANES, LANES), F32)
        return carry

    lax.fori_loop(0, face_len // (2 * LANES), clear, 0)
    gram_acc[...] = jnp.zeros_like(gram_acc)
    turn_load.wait()
    cos, sin = turn_ref[:vecs], turn_ref[8 : 8 + vecs]

    def turned(pair, sign):
        n = pair.shape[1] // LANES
        c = jnp.concatenate([cos] * n, axis=1)
        s = jnp.concatenate([sin] * n, axis=1) * sign
        a, b = pair[:vecs], pair[vecs:]
        return jnp.concatenate([c * a - s * b, s * a + c * b], axis=0)

    unit = (iota((LANES, LANES), 0) == iota((LANES, LANES), 1)).astype(BF16)
    unit = jnp.concatenate([unit, unit], axis=1)

    def put_rows(tile, first):
        top, low = split(tile)
        tiled = jnp.concatenate(
            [jnp.concatenate([top] * copies, axis=0), jnp.concatenate([low] * copies, axis=0)],
            axis=1,
        )
        rows_x[pl.ds(first, LANES), :] = dot_nt(unit, tiled)

    many = 8
    at_last = lax.axis_index("py") == lax.axis_size("py") - 1

    def build_own(c, carry):
        for u in range(many):
            first = pl.multiple_of((c * many + u) * LANES, LANES)
            put_rows(own_ref[:, pl.ds(first, LANES)], first)
        return carry


    def build_face(c, carry):
        for u in range(many // 2):
            first = pl.multiple_of((c * (many // 2) + u) * LANES, LANES)
            put_rows(
                turned(high_x_ref[:, pl.ds(first, LANES)], 1.0),
                pl.multiple_of(owned_len + first, LANES),
            )
            put_rows(
                jnp.where(at_last, 0.0, high_y_ref[:, pl.ds(first, LANES)]),
                pl.multiple_of(owned_len + face_len + first, LANES),
            )
        return carry

    lax.fori_loop(0, face_len // (many // 2 * LANES), build_face, 0)
    own_load.wait()
    lax.fori_loop(0, owned_len // (many * LANES), build_own, 0)

    for load in loads:
        load.wait()

    masks = lane_masks(width, groups)

    def index_of(i, elem):
        return dofs_ref.at[pl.ds(i * capacity, capacity)][elem]

    def face_index_of(i, elem):
        return face_dofs_ref.at[pl.ds(i * face_slots, face_slots)][elem]

    unroll = 4
    steps = BLOCK_ROWS // unroll
    halves = range(0, BLOCK_ROWS, 8)
    part = nloc // steps

    def block(b, gather):
        behind = jnp.maximum(b - 1, 0)
        here = pl.multiple_of(b * block_terms, BLOCK_ROWS)
        there = pl.multiple_of(behind * block_terms, BLOCK_ROWS)
        first_term = pl.multiple_of(behind * block_terms, BLOCK_ROWS)
        first_elem = b * block_elems

        def step(t, c):
            totals = [[None] * len(halves) for _ in range(part)]
            for i in range(nloc):
                if gather:
                    for u in range(unroll):
                        g = t * unroll + u
                        elem = first_elem + g * groups
                        rows = [
                            rows_x[pl.ds(index_of(i, elem + k), 1), :] for k in range(groups)
                        ]
                        gath[pl.ds(here + i * BLOCK_ROWS + g, 1), :] = pick(masks, rows)
                values = [
                    gath[pl.ds(pl.multiple_of(there + i * BLOCK_ROWS + h, 8), 8), :] for h in halves
                ]
                for q in range(part):
                    coef = jnp.broadcast_to(
                        coef_ref[pl.ds((t * part + q) * nloc + i, 1), :], (8, LANES)
                    )
                    for n, value in enumerate(values):
                        product = coef * value
                        totals[q][n] = product if i == 0 else totals[q][n] + product
            for n, h in enumerate(halves):
                scale = scale_ref[pl.ds(pl.multiple_of(behind * BLOCK_ROWS + h, 8), 8), :]
                for q in range(part):
                    at = first_term + (t * part + q) * BLOCK_ROWS + h
                    term_ref[pl.ds(pl.multiple_of(at, 8), 8), :] = totals[q][n] * scale
            return c

        lax.fori_loop(0, steps, step, 0)

    def send(b):
        at = pl.ds(pl.multiple_of(b * block_terms, BLOCK_ROWS), block_terms)
        return pltpu.make_async_copy(term_ref.at[at], term_hbm.at[at], term_sems.at[b])

    def face_block(b, carry):
        add_block(term_ref, accs, face_index_of, index_of, b, nloc, groups)
        return carry

    live = count_ref[0]
    blocks = (live + block_elems - 1) // block_elems
    face_blocks = jnp.minimum(blocks, face_slots // block_elems)

    def full_block(b, carry):
        block(b, True)

        @pl.when(b > 0)
        def _():
            send(b - 1).start()

        return carry

    lax.fori_loop(0, blocks, full_block, 0)
    block(blocks, False)
    send(blocks - 1).start()
    lax.fori_loop(0, face_blocks, face_block, 0)

    deep = DEEP * block_terms
    zero_block = jnp.zeros((block_terms, LANES), F32)
    chunks = (blocks + DEEP - 1) // DEEP

    def blank(b, carry):
        at = pl.ds(pl.multiple_of(b * block_terms, BLOCK_ROWS), block_terms)
        gath[at, :] = zero_block
        term_ref[at, :] = zero_block
        return carry

    lax.fori_loop(blocks, chunks * DEEP, blank, 0)

    def products(c, carry):
        at = pl.ds(pl.multiple_of(c * deep, BLOCK_ROWS), deep)
        left, left_low = split(gath[at, :])
        right, right_low = split(term_ref[at, :])
        over_rows = (((0,), (0,)), ((), ()))
        gram_acc[:, : 2 * LANES] += lax.dot_general(
            left,
            jnp.concatenate([right, right_low], axis=1),
            over_rows,
            preferred_element_type=F32,
        )
        gram_acc[:, 2 * LANES :] += lax.dot_general(
            left_low, right, over_rows, preferred_element_type=F32
        )
        return carry

    lax.fori_loop(0, chunks, products, 0)
    folder = folder_of(width)
    wide = 2 * LANES

    def folded(first):
        at = pl.ds(first, wide)
        total = pick(masks, [acc[at, :] for acc in accs])
        return dot_nt(folder, jnp.concatenate(split(total), axis=1))

    def fold_face(c, carry):
        for u in range(4):
            first = pl.multiple_of((4 * c + u) * wide, wide)
            at = pl.ds(first, wide)
            total = folded(first)
            side_x_ref[:width, at] = turned(total[:width], -1.0)
            side_x_ref[width:, at] = turned(total[width:], -1.0)
            side_y_ref[:, at] = folded(pl.multiple_of(face_len + first, wide))
        return carry

    lax.fori_loop(0, face_len // (4 * wide), fold_face, 0)

    whole = gram_acc[:, :LANES] + gram_acc[:, LANES : 2 * LANES] + gram_acc[:, 2 * LANES :]
    total = whole[:width]
    for k in range(1, groups):
        part = whole[2 * width * k : 2 * width * k + width]
        total = total + pltpu.roll(part, LANES - 2 * width * k, 1)
    re_left, im_left = total[:vecs], total[vecs:]
    lane = iota((vecs, LANES), 1)
    real_here = lane // vecs % 2 == 0
    swapped = jnp.where(
        real_here, pltpu.roll(im_left, LANES - vecs, 1), -pltpu.roll(im_left, vecs, 1)
    )
    joined = re_left + swapped
    for n in range(gram_ref.shape[0]):
        gram_ref[n] = joined

    def sent(b, carry):
        send(b).wait()
        return carry

    lax.fori_loop(0, blocks, sent, 0)


def add_kernel(
    width, nloc, interior, count_ref, table_hbm, term_hbm, curl_hbm, mass_hbm, face_ref,
    dofs_ref, term_ref, images, sem, term_sems, out_sems, *accs
):
    owned_len = curl_hbm.shape[1]
    groups = LANES // (2 * width)
    capacity = term_ref.shape[0] // nloc * groups
    block_elems = groups * BLOCK_ROWS
    block_terms = nloc * BLOCK_ROWS
    load = pltpu.make_async_copy(table_hbm, dofs_ref, sem)
    load.start()
    live = count_ref[0]
    blocks = (live + block_elems - 1) // block_elems

    def fetch(b):
        at = pl.ds(pl.multiple_of(b * block_terms, BLOCK_ROWS), block_terms)
        return pltpu.make_async_copy(term_hbm.at[at], term_ref.at[at], term_sems.at[b])

    def fetch_all(b, carry):
        fetch(b).start()
        return carry

    lax.fori_loop(0, blocks, fetch_all, 0)
    many = 4
    zero_tile = jnp.zeros((many * LANES, LANES), F32)

    def clear(c, carry):
        at = pl.ds(pl.multiple_of(c * many * LANES, LANES), many * LANES)
        for acc in accs:
            acc[at, :] = zero_tile
        return carry

    lax.fori_loop(0, owned_len // (many * LANES), clear, 0)
    load.wait()

    def index_of(i, elem):
        return dofs_ref.at[pl.ds(i * capacity, capacity)][elem]

    def block(b, carry):
        fetch(b).wait()
        add_block(term_ref, accs, index_of, index_of, b, nloc, groups)
        return carry

    lax.fori_loop(0, blocks, block, 0)

    masks = lane_masks(width, groups)
    folder = folder_of(width)
    wide = 2 * LANES
    many = 4
    span = many * wide

    def fold_some(first, curl, mass):
        for u in range(many):
            at = pl.ds(pl.multiple_of(first + u * wide, wide), wide)
            total = pick(masks, [acc[at, :] for acc in accs])
            total = dot_nt(folder, jnp.concatenate(split(total), axis=1))
            to = slice(u * wide, (u + 1) * wide)
            curl[:, to] = total[:width]
            mass[:, to] = total[width:]

    moves = []
    for c in range(owned_len // span):
        at = pl.ds(c * span, span)
        if c * span < interior:
            fold_some(c * span, images.at[0, :, at], images.at[1, :, at])
            for n, image in enumerate((curl_hbm, mass_hbm)):
                moves.append(
                    pltpu.make_async_copy(
                        images.at[n, :, at], image.at[:, at], out_sems.at[2 * c + n]
                    )
                )
                moves[-1].start()
        else:
            at = pl.ds(c * span - interior, span)
            fold_some(c * span, face_ref.at[0, :, at], face_ref.at[1, :, at])
    for move in moves:
        move.wait()


def finish_kernel(
    width, scale, curl_in, mass_in, face_ref, back_x_ref, back_y_ref, gram_ref,
    curl_out, mass_out, gram_out, faces, sems,
):
    del curl_in, mass_in
    face_len = back_x_ref.shape[1]
    outer = pl.ds(curl_out.shape[1] - 2 * face_len, 2 * face_len)
    moves = []
    at_start = lax.axis_index("py") == 0
    for n, image in enumerate((curl_out, mass_out)):
        rows = slice(n * width, (n + 1) * width)
        faces[n, :, :face_len] = face_ref[n, :, :face_len] + back_x_ref[rows, :]
        faces[n, :, face_len:] = face_ref[n, :, face_len:] + jnp.where(
            at_start, 0.0, back_y_ref[rows, :]
        )
        moves.append(pltpu.make_async_copy(faces.at[n], image.at[:, outer], sems.at[n]))
        moves[-1].start()
    total = gram_ref[0]
    for d in range(1, gram_ref.shape[0]):
        total = total + gram_ref[d]
    total = total * scale
    vecs = total.shape[0]
    for q in range(4):
        shifted = total if q == 0 else pltpu.roll(total, LANES - q * vecs, 1)
        gram_out[q * vecs : (q + 1) * vecs, :] = shifted[:, :vecs]
    for move in moves:
        move.wait()


def on_device(
    trial_block,
    stiff_coef,
    mass_coef,
    elem_count,
    elem_dofs,
    pairing,
    bloch_fraction,
    stiff_ref,
    mass_ref,
):
    own_block = trial_block[0, 0]
    vecs, owned_len = own_block.shape[1:]
    face_len = pairing.shape[0]
    interior = owned_len - 2 * face_len
    width = 2 * vecs
    groups = LANES // (2 * width)
    capacity, nloc = elem_dofs.shape[2:]
    face_slots = capacity // 8
    devices = lax.axis_size("px") * lax.axis_size("py")
    own_rows = own_block.reshape(width, owned_len)
    low_x = own_rows[:, interior : interior + face_len]
    low_y = own_rows[:, interior + face_len :]
    high_x = lax.ppermute(low_x, "px", ring_route("px", -1))
    high_y = lax.ppermute(low_y, "py", ring_route("py", -1))
    live = elem_count[0]
    smem = pl.BlockSpec(memory_space=pltpu.SMEM)
    vmem = pl.BlockSpec(memory_space=pltpu.VMEM)
    left = pl.BlockSpec(memory_space=pl.ANY)

    limit = 62 * 1024 * 1024
    params = pltpu.CompilerParams(vmem_limit_bytes=limit)

    def in_hbm(*values):
        return [pltpu.with_memory_space_constraint(value, pltpu.HBM) for value in values]

    table, own_table, face_table, scale, turn, coef = pl.pallas_call(
        functools.partial(prepare_kernel, owned_len, face_len, width),
        out_shape=(
            jax.ShapeDtypeStruct((nloc + 2, 1, capacity), jnp.int32),
            jax.ShapeDtypeStruct((nloc + 2, 1, capacity), jnp.int32),
            jax.ShapeDtypeStruct((-(-nloc // 8) * 8, face_slots), jnp.int32),
            jax.ShapeDtypeStruct((capacity // groups, LANES), F32),
            jax.ShapeDtypeStruct((16, LANES), F32),
            jax.ShapeDtypeStruct((nloc * nloc, LANES), F32),
        ),
        in_specs=[smem] * 4 + [vmem] * 4,
        out_specs=[vmem] * 5 + [left],
        scratch_shapes=[
            pltpu.VMEM((nloc * nloc, LANES), F32),
            pltpu.SemaphoreType.DMA,
        ],
        compiler_params=params,
        name="prepare",
    )(
        live,
        bloch_fraction,
        stiff_ref,
        mass_ref,
        elem_dofs.transpose(0, 3, 1, 2).reshape(nloc, 1, capacity),
        pairing.reshape(-1, LANES),
        stiff_coef[0],
        mass_coef[0],
    )
    table = table.reshape(-1)
    own_table = own_table.reshape(-1)
    face_table = face_table.reshape(-1)

    extent = owned_len + 2 * face_len
    blocks = capacity // (groups * BLOCK_ROWS)
    term_rows = nloc * capacity // groups
    terms, side_x, side_y, gram = pl.pallas_call(
        functools.partial(term_kernel, width, nloc),
        out_shape=(
            pltpu.HBM((term_rows, LANES), F32),
            jax.ShapeDtypeStruct((2 * width, face_len), F32),
            jax.ShapeDtypeStruct((2 * width, face_len), F32),
            jax.ShapeDtypeStruct((devices, vecs, LANES), F32),
        ),
        in_specs=[smem] + [left] * 6 + [vmem] * 2,
        out_specs=[left] + [vmem] * 3,
        scratch_shapes=[
            pltpu.SMEM(table.shape, jnp.int32),
            pltpu.SMEM(face_table.shape, jnp.int32),
            pltpu.VMEM(turn.shape, F32),
            pltpu.VMEM(own_rows.shape, F32),
            pltpu.VMEM(scale.shape, F32),
            pltpu.VMEM(coef.shape, F32),
            pltpu.VMEM((term_rows, LANES), F32),
            pltpu.VMEM((extent, LANES), F32),
            pltpu.VMEM((term_rows, LANES), F32),
            pltpu.VMEM((LANES, 3 * LANES), F32),
            pltpu.SemaphoreType.DMA((6,)),
            pltpu.SemaphoreType.DMA((blocks,)),
        ]
        + [pltpu.VMEM((2 * face_len + 8, LANES), F32)] * N_ACC,
        compiler_params=pltpu.CompilerParams(vmem_limit_bytes=TERM_MIB * 1024 * 1024),
        name="terms",
    )(live, *in_hbm(table, face_table, turn, own_rows, scale, coef), high_x, high_y)

    back_x = lax.ppermute(side_x, "px", ring_route("px", 1))
    back_y = lax.ppermute(side_y, "py", ring_route("py", 1))
    gathered = lax.all_to_all(gram, ("px", "py"), 0, 0)

    curl, mass, faces = pl.pallas_call(
        functools.partial(add_kernel, width, nloc, interior),
        out_shape=(
            jax.ShapeDtypeStruct((width, owned_len), F32),
            jax.ShapeDtypeStruct((width, owned_len), F32),
            jax.ShapeDtypeStruct((2, width, 2 * face_len), F32),
        ),
        in_specs=[smem, left, left],
        out_specs=[left, left, vmem],
        scratch_shapes=[
            pltpu.SMEM(own_table.shape, jnp.int32),
            pltpu.VMEM((term_rows, LANES), F32),
            pltpu.VMEM((2, width, interior), F32),
            pltpu.SemaphoreType.DMA,
            pltpu.SemaphoreType.DMA((blocks,)),
            pltpu.SemaphoreType.DMA((2 * owned_len // (8 * LANES),)),
        ]
        + [pltpu.VMEM((owned_len + 8, LANES), F32)] * N_ACC,
        compiler_params=pltpu.CompilerParams(vmem_limit_bytes=ADD_MIB * 1024 * 1024),
        cost_estimate=pl.CostEstimate(
            flops=40 * 1024 * 1024 * 1024, bytes_accessed=40 * 1024 * 1024, transcendentals=0
        ),
        name="adds",
    )(live, *in_hbm(own_table, terms))

    curl, mass, gram = pl.pallas_call(
        functools.partial(finish_kernel, width, 1.0 / float(devices * owned_len)),
        out_shape=(
            jax.ShapeDtypeStruct((width, owned_len), F32),
            jax.ShapeDtypeStruct((width, owned_len), F32),
            jax.ShapeDtypeStruct((4 * vecs, vecs), F32),
        ),
        in_specs=[left] * 2 + [vmem] * 4,
        out_specs=[left, left, vmem],
        scratch_shapes=[
            pltpu.VMEM((2, width, 2 * face_len), F32),
            pltpu.SemaphoreType.DMA((2,)),
        ],
        input_output_aliases={0: 0, 1: 1},
        compiler_params=pltpu.CompilerParams(vmem_limit_bytes=8 * 1024 * 1024),
        name="finish",
    )(curl, mass, faces, back_x, back_y, gathered)
    shape = (1, 1, 2, vecs, owned_len)
    return curl.reshape(shape), mass.reshape(shape), gram.reshape(2, 2, vecs, vecs)


def solution(mesh):
    return jax.shard_map(
        on_device,
        mesh=mesh,
        in_specs=(
            P("px", "py", None, None, None),
            P("px", "py", None),
            P("px", "py", None),
            P("px", "py"),
            P("px", "py", None, None),
            P(),
            P(),
            P(),
            P(),
        ),
        out_specs=(P("px", "py", None, None, None), P("px", "py", None, None, None), P()),
        check_vma=False,
    )
```

```python
import functools
import math

import jax
import jax.numpy as jnp
from jax import lax
from jax.experimental import pallas as pl
from jax.experimental.pallas import tpu as pltpu
from jax.sharding import PartitionSpec as P


LANES = 128
BLOCK_ROWS = 16
SUB_ROWS = 8
PAIR = 2
TERM_MIB = 32
ADD_MIB = 26
STEP = 4
DEEP = 4
N_ACC = 4
F32 = jnp.float32
BF16 = jnp.bfloat16


def ring_route(axis, steps):
    count = lax.axis_size(axis)
    return [(source, (source + steps) % count) for source in range(count)]


def iota(shape, axis):
    return lax.broadcasted_iota(jnp.int32, shape, axis)


def split(x):
    top = x.astype(BF16)
    return top, (x - top.astype(F32)).astype(BF16)


def dot_nt(left, right):
    return lax.dot_general(
        left, right, (((1,), (1,)), ((), ())), preferred_element_type=F32
    )


def gather_lanes(table_ref, index):
    high = index // LANES
    low = index % LANES
    found = jnp.zeros_like(index)
    for r in range(table_ref.shape[0]):
        line = jnp.broadcast_to(table_ref[r : r + 1, :], index.shape)
        found = jnp.where(high == r, jnp.take_along_axis(line, low, axis=1), found)
    return found


def prepare_kernel(
    owned_len, face_len, width, count_ref, bloch_ref, stiff_elem_ref, mass_elem_ref,
    dofs_ref, pair_ref, stiff_ref, mass_ref,
    table_ref, own_table_ref, face_table_ref, scale_ref, turn_ref, coef_hbm, coef_ref, coef_sem,
):
    nloc, _, capacity = dofs_ref.shape
    face_slots = face_table_ref.shape[1]
    groups = LANES // (2 * width)
    at_end = lax.axis_index("px") == lax.axis_size("px") - 1
    live = count_ref[0, 0]

    curl_lane = iota((1, LANES), 1) // width % 2 == 0

    def build_coef(j, carry):
        for i in range(nloc):
            coef_ref[pl.ds(j * nloc + i, 1), :] = jnp.where(curl_lane, stiff_elem_ref[j, i], mass_elem_ref[j, i])
        return carry

    lax.fori_loop(0, nloc, build_coef, 0)
    coef_move = pltpu.make_async_copy(coef_ref, coef_hbm, coef_sem)
    coef_move.start()

    index = [dofs_ref[i] for i in range(nloc)]
    flag = jnp.zeros((1, capacity), jnp.int32)
    for i in range(nloc):
        for k in range(i + 1, min(i // STEP * STEP + STEP, nloc)):
            flag = jnp.where(index[i] == index[k], 1, flag)
    reach = 1
    for row, rows in ((1, PAIR), (0, SUB_ROWS)):
        while reach < groups * rows:
            flag = jnp.maximum(flag, pltpu.roll(flag, reach, 1))
            reach *= 2
        table_ref[nloc + row] = flag
        own_table_ref[nloc + row] = flag
    for i in range(nloc):
        table_ref[i] = index[i]
        own_table_ref[i] = jnp.minimum(index[i], owned_len)

    pad = face_table_ref.shape[0] - nloc
    for c in range(0, face_slots, LANES):
        at = slice(c, c + LANES)
        first = jnp.concatenate(
            [row[:, at] for row in index] + [jnp.zeros((pad, LANES), jnp.int32)], axis=0
        )
        local = first - owned_len
        on_face = at_end & (local >= 0) & (local < face_len)
        paired = gather_lanes(pair_ref, jnp.where(on_face, local, 0))
        first = jnp.where(on_face, paired + owned_len, first)
        face_table_ref[:, at] = jnp.where(first >= owned_len, first - owned_len, 2 * face_len)
        for i in range(nloc):
            table_ref[i, :, at] = first[i : i + 1]

    per_chunk = LANES // groups
    lane_of = iota((LANES, LANES), 0)
    elem_of = iota((LANES, LANES), 1)
    mine = elem_of % groups == lane_of // (2 * width)
    is_curl = lane_of // width % 2 == 0
    chooser = (iota((per_chunk, LANES), 1) // groups == iota((per_chunk, LANES), 0)).astype(BF16)
    chooser = jnp.concatenate([chooser, chooser], axis=1)
    for c in range(capacity // LANES):
        at = slice(c * LANES, (c + 1) * LANES)
        scales = jnp.where(is_curl, stiff_ref[:, at], mass_ref[:, at])
        scales = jnp.where(mine & (c * LANES + elem_of < live), scales, 0.0)
        scale_ref[c * per_chunk : (c + 1) * per_chunk, :] = dot_nt(
            chooser, jnp.concatenate(split(scales), axis=1)
        )

    ratio = jnp.full((8, LANES), bloch_ref[0].astype(F32), F32) / bloch_ref[1].astype(F32)
    angle = (2.0 * math.pi) * jnp.where(at_end, ratio, 0.0)
    turn_ref[:8] = jnp.cos(angle)
    turn_ref[8:] = jnp.sin(angle)
    coef_move.wait()


def lane_masks(width, groups):
    lane = iota((1, LANES), 1) // (2 * width)
    return [lane == k for k in range(groups)]


def pick(masks, parts):
    out = parts[-1]
    for mask, part in zip(masks[-2::-1], parts[-2::-1]):
        out = jnp.where(mask, part, out)
    return out


def folder_of(width):
    rows = 2 * width
    folder = (iota((rows, LANES), 1) % rows == iota((rows, LANES), 0)).astype(BF16)
    return jnp.concatenate([folder, folder], axis=1)


def add_block(term_ref, accs, index_of, flag_of, b, nloc, groups):
    def part(h, carry):
        first_row = b * nloc * BLOCK_ROWS + h * SUB_ROWS
        first_elem = (b * (BLOCK_ROWS // SUB_ROWS) + h) * SUB_ROWS * groups

        def add_pair(t, step):
            for u in range(PAIR):
                g = t * PAIR + u
                elem = first_elem + g * groups
                for j in range(0, nloc, step):
                    slots = range(j, min(j + step, nloc))
                    new = [term_ref[pl.ds(first_row + s * BLOCK_ROWS + g, 1), :] for s in slots]
                    for k in range(groups):
                        places = [pl.ds(index_of(s, elem + k), 1) for s in slots]
                        sums = [accs[k][at, :] + row for at, row in zip(places, new)]
                        for at, row in zip(places, sums):
                            accs[k][at, :] = row

        def plain(t, c):
            add_pair(t, STEP)
            return c

        def careful(t, c):
            repeated = flag_of(nloc + 1, first_elem + (t + 1) * PAIR * groups - 1)

            @pl.when(repeated == 0)
            def _():
                add_pair(t, STEP)

            @pl.when(repeated != 0)
            def _():
                add_pair(t, 1)

            return c

        clash = flag_of(nloc, first_elem + SUB_ROWS * groups - 1)

        @pl.when(clash == 0)
        def _():
            lax.fori_loop(0, SUB_ROWS // PAIR, plain, 0)

        @pl.when(clash != 0)
        def _():
            lax.fori_loop(0, SUB_ROWS // PAIR, careful, 0)

        return carry

    lax.fori_loop(0, BLOCK_ROWS // SUB_ROWS, part, 0)


def term_kernel(
    width,
    nloc,
    count_ref,
    table_hbm,
    face_table_hbm,
    turn_hbm,
    own_hbm,
    scale_hbm,
    coef_hbm,
    high_x_ref,
    high_y_ref,
    term_hbm,
    side_x_ref,
    side_y_ref,
    gram_ref,
    dofs_ref,
    face_dofs_ref,
    turn_ref,
    own_ref,
    scale_ref,
    coef_ref,
    term_ref,
    rows_x,
    gath,
    gram_acc,
    sems,
    term_sems,
    *accs,
):
    owned_len = own_ref.shape[1]
    face_len = high_x_ref.shape[1]
    vecs = width // 2
    groups = LANES // (2 * width)
    capacity = scale_ref.shape[0] * groups
    face_slots = capacity // 8
    copies = LANES // width
    block_elems = groups * BLOCK_ROWS
    block_terms = nloc * BLOCK_ROWS

    own_load, turn_load, *loads = [
        pltpu.make_async_copy(source, target, sems.at[n])
        for n, (source, target) in enumerate(
            (
                (own_hbm, own_ref),
                (turn_hbm, turn_ref),
                (table_hbm, dofs_ref),
                (face_table_hbm, face_dofs_ref),
                (coef_hbm, coef_ref),
                (scale_hbm, scale_ref),
            )
        )
    ]
    for load in (own_load, turn_load, *loads):
        load.start()

    def clear(c, carry):
        at = pl.ds(pl.multiple_of(c * 4 * LANES, LANES), 4 * LANES)
        for acc in accs:
            acc[at, :] = jnp.zeros((4 * LANES, LANES), F32)
        return carry

    lax.fori_loop(0, face_len // (2 * LANES), clear, 0)
    gram_acc[...] = jnp.zeros_like(gram_acc)
    turn_load.wait()
    cos, sin = turn_ref[:vecs], turn_ref[8 : 8 + vecs]

    def turned(pair, sign):
        n = pair.shape[1] // LANES
        c = jnp.concatenate([cos] * n, axis=1)
        s = jnp.concatenate([sin] * n, axis=1) * sign
        a, b = pair[:vecs], pair[vecs:]
        return jnp.concatenate([c * a - s * b, s * a + c * b], axis=0)

    unit = (iota((LANES, LANES), 0) == iota((LANES, LANES), 1)).astype(BF16)
    unit = jnp.concatenate([unit, unit], axis=1)

    def put_rows(tile, first):
        top, low = split(tile)
        tiled = jnp.concatenate(
            [jnp.concatenate([top] * copies, axis=0), jnp.concatenate([low] * copies, axis=0)],
            axis=1,
        )
        rows_x[pl.ds(first, LANES), :] = dot_nt(unit, tiled)

    many = 8
    at_last = lax.axis_index("py") == lax.axis_size("py") - 1

    def build_own(c, carry):
        for u in range(many):
            first = pl.multiple_of((c * many + u) * LANES, LANES)
            put_rows(own_ref[:, pl.ds(first, LANES)], first)
        return carry


    def build_face(c, carry):
        for u in range(many // 2):
            first = pl.multiple_of((c * (many // 2) + u) * LANES, LANES)
            put_rows(
                turned(high_x_ref[:, pl.ds(first, LANES)], 1.0),
                pl.multiple_of(owned_len + first, LANES),
            )
            put_rows(
                jnp.where(at_last, 0.0, high_y_ref[:, pl.ds(first, LANES)]),
                pl.multiple_of(owned_len + face_len + first, LANES),
            )
        return carry

    lax.fori_loop(0, face_len // (many // 2 * LANES), build_face, 0)
    own_load.wait()
    lax.fori_loop(0, owned_len // (many * LANES), build_own, 0)

    for load in loads:
        load.wait()

    masks = lane_masks(width, groups)

    def index_of(i, elem):
        return dofs_ref.at[pl.ds(i * capacity, capacity)][elem]

    def face_index_of(i, elem):
        return face_dofs_ref.at[pl.ds(i * face_slots, face_slots)][elem]

    unroll = 4
    steps = BLOCK_ROWS // unroll
    halves = range(0, BLOCK_ROWS, 8)
    part = nloc // steps

    def block(b, gather):
        behind = jnp.maximum(b - 1, 0)
        here = pl.multiple_of(b * block_terms, BLOCK_ROWS)
        there = pl.multiple_of(behind * block_terms, BLOCK_ROWS)
        first_term = pl.multiple_of(behind * block_terms, BLOCK_ROWS)
        first_elem = b * block_elems

        def step(t, c):
            totals = [[None] * len(halves) for _ in range(part)]
            for i in range(nloc):
                if gather:
                    for u in range(unroll):
                        g = t * unroll + u
                        elem = first_elem + g * groups
                        rows = [
                            rows_x[pl.ds(index_of(i, elem + k), 1), :] for k in range(groups)
                        ]
                        gath[pl.ds(here + i * BLOCK_ROWS + g, 1), :] = pick(masks, rows)
                values = [
                    gath[pl.ds(pl.multiple_of(there + i * BLOCK_ROWS + h, 8), 8), :] for h in halves
                ]
                for q in range(part):
                    coef = jnp.broadcast_to(
                        coef_ref[pl.ds((t * part + q) * nloc + i, 1), :], (8, LANES)
                    )
                    for n, value in enumerate(values):
                        product = coef * value
                        totals[q][n] = product if i == 0 else totals[q][n] + product
            for n, h in enumerate(halves):
                scale = scale_ref[pl.ds(pl.multiple_of(behind * BLOCK_ROWS + h, 8), 8), :]
                for q in range(part):
                    at = first_term + (t * part + q) * BLOCK_ROWS + h
                    term_ref[pl.ds(pl.multiple_of(at, 8), 8), :] = totals[q][n] * scale
            return c

        lax.fori_loop(0, steps, step, 0)

    def send(b):
        at = pl.ds(pl.multiple_of(b * block_terms, BLOCK_ROWS), block_terms)
        return pltpu.make_async_copy(term_ref.at[at], term_hbm.at[at], term_sems.at[b])

    def face_block(b, carry):
        add_block(term_ref, accs, face_index_of, index_of, b, nloc, groups)
        return carry

    live = count_ref[0, 0]
    blocks = (live + block_elems - 1) // block_elems
    face_blocks = jnp.minimum(blocks, face_slots // block_elems)

    def full_block(b, carry):
        block(b, True)

        @pl.when(b > 0)
        def _():
            send(b - 1).start()

        return carry

    lax.fori_loop(0, blocks, full_block, 0)
    block(blocks, False)
    send(blocks - 1).start()
    lax.fori_loop(0, face_blocks, face_block, 0)

    deep = DEEP * block_terms
    zero_block = jnp.zeros((block_terms, LANES), F32)
    chunks = (blocks + DEEP - 1) // DEEP

    def blank(b, carry):
        at = pl.ds(pl.multiple_of(b * block_terms, BLOCK_ROWS), block_terms)
        gath[at, :] = zero_block
        term_ref[at, :] = zero_block
        return carry

    lax.fori_loop(blocks, chunks * DEEP, blank, 0)

    def products(c, carry):
        at = pl.ds(pl.multiple_of(c * deep, BLOCK_ROWS), deep)
        left, left_low = split(gath[at, :])
        right, right_low = split(term_ref[at, :])
        over_rows = (((0,), (0,)), ((), ()))
        gram_acc[:, : 2 * LANES] += lax.dot_general(
            left,
            jnp.concatenate([right, right_low], axis=1),
            over_rows,
            preferred_element_type=F32,
        )
        gram_acc[:, 2 * LANES :] += lax.dot_general(
            left_low, right, over_rows, preferred_element_type=F32
        )
        return carry

    lax.fori_loop(0, chunks, products, 0)
    folder = folder_of(width)
    wide = 2 * LANES

    def folded(first):
        at = pl.ds(first, wide)
        total = pick(masks, [acc[at, :] for acc in accs])
        return dot_nt(folder, jnp.concatenate(split(total), axis=1))

    def fold_face(c, carry):
        for u in range(4):
            first = pl.multiple_of((4 * c + u) * wide, wide)
            at = pl.ds(first, wide)
            total = folded(first)
            side_x_ref[:width, at] = turned(total[:width], -1.0)
            side_x_ref[width:, at] = turned(total[width:], -1.0)
            side_y_ref[:, at] = folded(pl.multiple_of(face_len + first, wide))
        return carry

    lax.fori_loop(0, face_len // (4 * wide), fold_face, 0)

    whole = gram_acc[:, :LANES] + gram_acc[:, LANES : 2 * LANES] + gram_acc[:, 2 * LANES :]
    total = whole[:width]
    for k in range(1, groups):
        part = whole[2 * width * k : 2 * width * k + width]
        total = total + pltpu.roll(part, LANES - 2 * width * k, 1)
    re_left, im_left = total[:vecs], total[vecs:]
    lane = iota((vecs, LANES), 1)
    real_here = lane // vecs % 2 == 0
    swapped = jnp.where(
        real_here, pltpu.roll(im_left, LANES - vecs, 1), -pltpu.roll(im_left, vecs, 1)
    )
    joined = re_left + swapped
    for n in range(gram_ref.shape[0]):
        gram_ref[n] = joined

    def sent(b, carry):
        send(b).wait()
        return carry

    lax.fori_loop(0, blocks, sent, 0)


def add_kernel(
    width, nloc, interior, count_ref, table_hbm, term_hbm, curl_hbm, mass_hbm, face_ref,
    dofs_ref, term_ref, images, sem, term_sems, out_sems, *accs
):
    owned_len = curl_hbm.shape[1]
    groups = LANES // (2 * width)
    capacity = term_ref.shape[0] // nloc * groups
    block_elems = groups * BLOCK_ROWS
    block_terms = nloc * BLOCK_ROWS
    load = pltpu.make_async_copy(table_hbm, dofs_ref, sem)
    load.start()
    live = count_ref[0, 0]
    blocks = (live + block_elems - 1) // block_elems

    def fetch(b):
        at = pl.ds(pl.multiple_of(b * block_terms, BLOCK_ROWS), block_terms)
        return pltpu.make_async_copy(term_hbm.at[at], term_ref.at[at], term_sems.at[b])

    def fetch_all(b, carry):
        fetch(b).start()
        return carry

    lax.fori_loop(0, blocks, fetch_all, 0)
    many = 4
    zero_tile = jnp.zeros((many * LANES, LANES), F32)

    def clear(c, carry):
        at = pl.ds(pl.multiple_of(c * many * LANES, LANES), many * LANES)
        for acc in accs:
            acc[at, :] = zero_tile
        return carry

    lax.fori_loop(0, owned_len // (many * LANES), clear, 0)
    load.wait()

    def index_of(i, elem):
        return dofs_ref.at[pl.ds(i * capacity, capacity)][elem]

    def block(b, carry):
        fetch(b).wait()
        add_block(term_ref, accs, index_of, index_of, b, nloc, groups)
        return carry

    lax.fori_loop(0, blocks, block, 0)

    masks = lane_masks(width, groups)
    folder = folder_of(width)
    wide = 2 * LANES
    many = 4
    span = many * wide

    def fold_some(first, curl, mass):
        for u in range(many):
            at = pl.ds(pl.multiple_of(first + u * wide, wide), wide)
            total = pick(masks, [acc[at, :] for acc in accs])
            total = dot_nt(folder, jnp.concatenate(split(total), axis=1))
            to = slice(u * wide, (u + 1) * wide)
            curl[:, to] = total[:width]
            mass[:, to] = total[width:]

    moves = []
    for c in range(owned_len // span):
        at = pl.ds(c * span, span)
        if c * span < interior:
            fold_some(c * span, images.at[0, :, at], images.at[1, :, at])
            for n, image in enumerate((curl_hbm, mass_hbm)):
                moves.append(
                    pltpu.make_async_copy(
                        images.at[n, :, at], image.at[:, at], out_sems.at[2 * c + n]
                    )
                )
                moves[-1].start()
        else:
            at = pl.ds(c * span - interior, span)
            fold_some(c * span, face_ref.at[0, :, at], face_ref.at[1, :, at])
    for move in moves:
        move.wait()


def finish_kernel(
    width, scale, curl_in, mass_in, face_ref, back_x_ref, back_y_ref, gram_ref,
    curl_out, mass_out, gram_out, faces, sems,
):
    del curl_in, mass_in
    face_len = back_x_ref.shape[1]
    outer = pl.ds(curl_out.shape[1] - 2 * face_len, 2 * face_len)
    moves = []
    at_start = lax.axis_index("py") == 0
    for n, image in enumerate((curl_out, mass_out)):
        rows = slice(n * width, (n + 1) * width)
        faces[n, :, :face_len] = face_ref[n, :, :face_len] + back_x_ref[rows, :]
        faces[n, :, face_len:] = face_ref[n, :, face_len:] + jnp.where(
            at_start, 0.0, back_y_ref[rows, :]
        )
        moves.append(pltpu.make_async_copy(faces.at[n], image.at[:, outer], sems.at[n]))
        moves[-1].start()
    total = gram_ref[0]
    for d in range(1, gram_ref.shape[0]):
        total = total + gram_ref[d]
    total = total * scale
    vecs = total.shape[0]
    for q in range(4):
        shifted = total if q == 0 else pltpu.roll(total, LANES - q * vecs, 1)
        gram_out[q * vecs : (q + 1) * vecs, :] = shifted[:, :vecs]
    for move in moves:
        move.wait()


def on_device(
    trial_block,
    stiff_coef,
    mass_coef,
    elem_count,
    elem_dofs,
    pairing,
    bloch_fraction,
    stiff_ref,
    mass_ref,
):
    own_block = trial_block[0, 0]
    vecs, owned_len = own_block.shape[1:]
    face_len = pairing.shape[0]
    interior = owned_len - 2 * face_len
    width = 2 * vecs
    groups = LANES // (2 * width)
    capacity, nloc = elem_dofs.shape[2:]
    face_slots = capacity // 8
    devices = lax.axis_size("px") * lax.axis_size("py")
    own_rows = own_block.reshape(width, owned_len)
    low_x = own_rows[:, interior : interior + face_len]
    low_y = own_rows[:, interior + face_len :]
    high_x = lax.ppermute(low_x, "px", ring_route("px", -1))
    high_y = lax.ppermute(low_y, "py", ring_route("py", -1))
    live = elem_count
    smem = pl.BlockSpec(memory_space=pltpu.SMEM)
    vmem = pl.BlockSpec(memory_space=pltpu.VMEM)
    left = pl.BlockSpec(memory_space=pl.ANY)

    limit = 62 * 1024 * 1024
    params = pltpu.CompilerParams(vmem_limit_bytes=limit)

    def in_hbm(*values):
        return [pltpu.with_memory_space_constraint(value, pltpu.HBM) for value in values]

    table, own_table, face_table, scale, turn, coef = pl.pallas_call(
        functools.partial(prepare_kernel, owned_len, face_len, width),
        out_shape=(
            jax.ShapeDtypeStruct((nloc + 2, 1, capacity), jnp.int32),
            jax.ShapeDtypeStruct((nloc + 2, 1, capacity), jnp.int32),
            jax.ShapeDtypeStruct((-(-nloc // 8) * 8, face_slots), jnp.int32),
            jax.ShapeDtypeStruct((capacity // groups, LANES), F32),
            jax.ShapeDtypeStruct((16, LANES), F32),
            jax.ShapeDtypeStruct((nloc * nloc, LANES), F32),
        ),
        in_specs=[smem] * 4 + [vmem] * 4,
        out_specs=[vmem] * 5 + [left],
        scratch_shapes=[
            pltpu.VMEM((nloc * nloc, LANES), F32),
            pltpu.SemaphoreType.DMA,
        ],
        compiler_params=params,
        name="prepare",
    )(
        live,
        bloch_fraction,
        stiff_ref,
        mass_ref,
        elem_dofs.transpose(0, 3, 1, 2).reshape(nloc, 1, capacity),
        pairing.reshape(-1, LANES),
        stiff_coef[0],
        mass_coef[0],
    )
    table = table.reshape(-1)
    own_table = own_table.reshape(-1)
    face_table = face_table.reshape(-1)

    extent = owned_len + 2 * face_len
    blocks = capacity // (groups * BLOCK_ROWS)
    term_rows = nloc * capacity // groups
    terms, side_x, side_y, gram = pl.pallas_call(
        functools.partial(term_kernel, width, nloc),
        out_shape=(
            pltpu.HBM((term_rows, LANES), F32),
            jax.ShapeDtypeStruct((2 * width, face_len), F32),
            jax.ShapeDtypeStruct((2 * width, face_len), F32),
            jax.ShapeDtypeStruct((devices, vecs, LANES), F32),
        ),
        in_specs=[smem] + [left] * 6 + [vmem] * 2,
        out_specs=[left] + [vmem] * 3,
        scratch_shapes=[
            pltpu.SMEM(table.shape, jnp.int32),
            pltpu.SMEM(face_table.shape, jnp.int32),
            pltpu.VMEM(turn.shape, F32),
            pltpu.VMEM(own_rows.shape, F32),
            pltpu.VMEM(scale.shape, F32),
            pltpu.VMEM(coef.shape, F32),
            pltpu.VMEM((term_rows, LANES), F32),
            pltpu.VMEM((extent, LANES), F32),
            pltpu.VMEM((term_rows, LANES), F32),
            pltpu.VMEM((LANES, 3 * LANES), F32),
            pltpu.SemaphoreType.DMA((6,)),
            pltpu.SemaphoreType.DMA((blocks,)),
        ]
        + [pltpu.VMEM((2 * face_len + 8, LANES), F32)] * N_ACC,
        compiler_params=pltpu.CompilerParams(vmem_limit_bytes=TERM_MIB * 1024 * 1024),
        name="terms",
    )(live, *in_hbm(table, face_table, turn, own_rows, scale, coef), high_x, high_y)

    back_x = lax.ppermute(side_x, "px", ring_route("px", 1))
    back_y = lax.ppermute(side_y, "py", ring_route("py", 1))
    gathered = lax.all_to_all(gram, ("px", "py"), 0, 0)

    curl, mass, faces = pl.pallas_call(
        functools.partial(add_kernel, width, nloc, interior),
        out_shape=(
            jax.ShapeDtypeStruct((width, owned_len), F32),
            jax.ShapeDtypeStruct((width, owned_len), F32),
            jax.ShapeDtypeStruct((2, width, 2 * face_len), F32),
        ),
        in_specs=[smem, left, left],
        out_specs=[left, left, vmem],
        scratch_shapes=[
            pltpu.SMEM(own_table.shape, jnp.int32),
            pltpu.VMEM((term_rows, LANES), F32),
            pltpu.VMEM((2, width, interior), F32),
            pltpu.SemaphoreType.DMA,
            pltpu.SemaphoreType.DMA((blocks,)),
            pltpu.SemaphoreType.DMA((2 * owned_len // (8 * LANES),)),
        ]
        + [pltpu.VMEM((owned_len + 8, LANES), F32)] * N_ACC,
        compiler_params=pltpu.CompilerParams(vmem_limit_bytes=ADD_MIB * 1024 * 1024),
        cost_estimate=pl.CostEstimate(
            flops=40 * 1024 * 1024 * 1024, bytes_accessed=40 * 1024 * 1024, transcendentals=0
        ),
        name="adds",
    )(live, *in_hbm(own_table, terms))

    curl, mass, gram = pl.pallas_call(
        functools.partial(finish_kernel, width, 1.0 / float(devices * owned_len)),
        out_shape=(
            jax.ShapeDtypeStruct((width, owned_len), F32),
            jax.ShapeDtypeStruct((width, owned_len), F32),
            jax.ShapeDtypeStruct((4 * vecs, vecs), F32),
        ),
        in_specs=[left] * 2 + [vmem] * 4,
        out_specs=[left, left, vmem],
        scratch_shapes=[
            pltpu.VMEM((2, width, 2 * face_len), F32),
            pltpu.SemaphoreType.DMA((2,)),
        ],
        input_output_aliases={0: 0, 1: 1},
        compiler_params=pltpu.CompilerParams(vmem_limit_bytes=8 * 1024 * 1024),
        name="finish",
    )(curl, mass, faces, back_x, back_y, gathered)
    shape = (1, 1, 2, vecs, owned_len)
    return curl.reshape(shape), mass.reshape(shape), gram.reshape(2, 2, vecs, vecs)


def solution(mesh):
    return jax.shard_map(
        on_device,
        mesh=mesh,
        in_specs=(
            P("px", "py", None, None, None),
            P("px", "py", None),
            P("px", "py", None),
            P("px", "py"),
            P("px", "py", None, None),
            P(),
            P(),
            P(),
            P(),
        ),
        out_specs=(P("px", "py", None, None, None), P("px", "py", None, None, None), P()),
        check_vma=False,
    )
```

```python
import functools
import math

import jax
import jax.numpy as jnp
from jax import lax
from jax.experimental import pallas as pl
from jax.experimental.pallas import tpu as pltpu
from jax.sharding import PartitionSpec as P


LANES = 128
BLOCK_ROWS = 16
SUB_ROWS = 8
PAIR = 2
CHUNKS = 4
TERM_MIB = 32
ADD_MIB = 26
STEP = 4
DEEP = 8
N_ACC = 4
F32 = jnp.float32
BF16 = jnp.bfloat16


def ring_route(axis, steps):
    count = lax.axis_size(axis)
    return [(source, (source + steps) % count) for source in range(count)]


def iota(shape, axis):
    return lax.broadcasted_iota(jnp.int32, shape, axis)


def split(x):
    top = x.astype(BF16)
    return top, (x - top.astype(F32)).astype(BF16)


def dot_nt(left, right):
    return lax.dot_general(
        left, right, (((1,), (1,)), ((), ())), preferred_element_type=F32
    )


def gather_lanes(table_ref, index):
    high = index // LANES
    low = index % LANES
    found = jnp.zeros_like(index)
    for r in range(table_ref.shape[0]):
        line = jnp.broadcast_to(table_ref[r : r + 1, :], index.shape)
        found = jnp.where(high == r, jnp.take_along_axis(line, low, axis=1), found)
    return found


def prepare_kernel(
    owned_len, face_len, width, count_ref, bloch_ref, stiff_elem_ref, mass_elem_ref,
    dofs_ref, pair_ref, stiff_ref, mass_ref,
    table_ref, own_table_ref, face_table_ref, scale_ref, turn_ref, coef_hbm, coef_ref, coef_sem,
):
    nloc, _, capacity = dofs_ref.shape
    face_slots = face_table_ref.shape[1]
    groups = LANES // (2 * width)
    at_end = lax.axis_index("px") == lax.axis_size("px") - 1
    live = count_ref[0, 0]

    curl_lane = iota((1, LANES), 1) // width % 2 == 0

    def build_coef(j, carry):
        for i in range(nloc):
            coef_ref[pl.ds(j * nloc + i, 1), :] = jnp.where(curl_lane, stiff_elem_ref[j, i], mass_elem_ref[j, i])
        return carry

    lax.fori_loop(0, nloc, build_coef, 0)
    coef_move = pltpu.make_async_copy(coef_ref, coef_hbm, coef_sem)
    coef_move.start()

    index = [dofs_ref[i] for i in range(nloc)]
    chunk = capacity // CHUNKS
    flag = jnp.zeros((1, capacity), jnp.int32)
    for i in range(nloc):
        for k in range(i + 1, min(i // STEP * STEP + STEP, nloc)):
            flag = jnp.where(index[i] == index[k], 1, flag)
    reach = 1
    for row, rows in ((1, PAIR), (0, SUB_ROWS)):
        while reach < groups * rows:
            flag = jnp.maximum(flag, pltpu.roll(flag, reach, 1))
            reach *= 2
        table_ref[nloc + row] = flag
        for c in range(CHUNKS):
            own_table_ref[c * (nloc + 2) + nloc + row] = flag[:, c * chunk : (c + 1) * chunk]
    for i in range(nloc):
        table_ref[i] = index[i]
        owned = jnp.minimum(index[i], owned_len)
        for c in range(CHUNKS):
            own_table_ref[c * (nloc + 2) + i] = owned[:, c * chunk : (c + 1) * chunk]

    pad = face_table_ref.shape[0] - nloc
    for c in range(0, face_slots, LANES):
        at = slice(c, c + LANES)
        first = jnp.concatenate(
            [row[:, at] for row in index] + [jnp.zeros((pad, LANES), jnp.int32)], axis=0
        )
        local = first - owned_len
        on_face = at_end & (local >= 0) & (local < face_len)
        paired = gather_lanes(pair_ref, jnp.where(on_face, local, 0))
        first = jnp.where(on_face, paired + owned_len, first)
        face_table_ref[:, at] = jnp.where(first >= owned_len, first - owned_len, 2 * face_len)
        for i in range(nloc):
            table_ref[i, :, at] = first[i : i + 1]

    per_chunk = LANES // groups
    lane_of = iota((LANES, LANES), 0)
    elem_of = iota((LANES, LANES), 1)
    mine = elem_of % groups == lane_of // (2 * width)
    is_curl = lane_of // width % 2 == 0
    chooser = (iota((per_chunk, LANES), 1) // groups == iota((per_chunk, LANES), 0)).astype(BF16)
    chooser = jnp.concatenate([chooser, chooser], axis=1)
    for c in range(capacity // LANES):
        at = slice(c * LANES, (c + 1) * LANES)
        scales = jnp.where(is_curl, stiff_ref[:, at], mass_ref[:, at])
        scales = jnp.where(mine & (c * LANES + elem_of < live), scales, 0.0)
        scale_ref[c * per_chunk : (c + 1) * per_chunk, :] = dot_nt(
            chooser, jnp.concatenate(split(scales), axis=1)
        )

    ratio = jnp.full((8, LANES), bloch_ref[0].astype(F32), F32) / bloch_ref[1].astype(F32)
    angle = (2.0 * math.pi) * jnp.where(at_end, ratio, 0.0)
    turn_ref[:8] = jnp.cos(angle)
    turn_ref[8:] = jnp.sin(angle)
    coef_move.wait()


def lane_masks(width, groups):
    lane = iota((1, LANES), 1) // (2 * width)
    return [lane == k for k in range(groups)]


def pick(masks, parts):
    out = parts[-1]
    for mask, part in zip(masks[-2::-1], parts[-2::-1]):
        out = jnp.where(mask, part, out)
    return out


def folder_of(width):
    rows = 2 * width
    folder = (iota((rows, LANES), 1) % rows == iota((rows, LANES), 0)).astype(BF16)
    return jnp.concatenate([folder, folder], axis=1)


def add_block(term_ref, accs, index_of, flag_of, b, shift, nloc, groups):
    def part(h, carry):
        first_row = b * nloc * BLOCK_ROWS + h * SUB_ROWS
        first_elem = (b * (BLOCK_ROWS // SUB_ROWS) + h) * SUB_ROWS * groups + shift

        def add_pair(t, step):
            for u in range(PAIR):
                g = t * PAIR + u
                elem = first_elem + g * groups
                for j in range(0, nloc, step):
                    slots = range(j, min(j + step, nloc))
                    new = [term_ref[pl.ds(first_row + s * BLOCK_ROWS + g, 1), :] for s in slots]
                    for k in range(groups):
                        places = [pl.ds(index_of(s, elem + k), 1) for s in slots]
                        sums = [accs[k][at, :] + row for at, row in zip(places, new)]
                        for at, row in zip(places, sums):
                            accs[k][at, :] = row

        def plain(t, c):
            add_pair(t, STEP)
            return c

        def careful(t, c):
            repeated = flag_of(nloc + 1, first_elem + (t + 1) * PAIR * groups - 1)

            @pl.when(repeated == 0)
            def _():
                add_pair(t, STEP)

            @pl.when(repeated != 0)
            def _():
                add_pair(t, 1)

            return c

        clash = flag_of(nloc, first_elem + SUB_ROWS * groups - 1)

        @pl.when(clash == 0)
        def _():
            lax.fori_loop(0, SUB_ROWS // PAIR, plain, 0)

        @pl.when(clash != 0)
        def _():
            lax.fori_loop(0, SUB_ROWS // PAIR, careful, 0)

        return carry

    lax.fori_loop(0, BLOCK_ROWS // SUB_ROWS, part, 0)


def term_kernel(
    width,
    nloc,
    count_ref,
    table_hbm,
    face_table_hbm,
    turn_hbm,
    own_hbm,
    scale_hbm,
    coef_hbm,
    high_x_ref,
    high_y_ref,
    term_hbm,
    side_x_ref,
    side_y_ref,
    gram_ref,
    dofs_ref,
    face_dofs_ref,
    turn_ref,
    own_ref,
    scale_ref,
    coef_ref,
    term_ref,
    rows_x,
    gath,
    gram_acc,
    sems,
    term_sems,
    *accs,
):
    owned_len = own_ref.shape[1]
    face_len = high_x_ref.shape[1]
    vecs = width // 2
    groups = LANES // (2 * width)
    capacity = scale_ref.shape[0] * groups
    face_slots = capacity // 8
    copies = LANES // width
    block_elems = groups * BLOCK_ROWS
    block_terms = nloc * BLOCK_ROWS

    own_load, turn_load, *loads = [
        pltpu.make_async_copy(source, target, sems.at[n])
        for n, (source, target) in enumerate(
            (
                (own_hbm, own_ref),
                (turn_hbm, turn_ref),
                (table_hbm, dofs_ref),
                (face_table_hbm, face_dofs_ref),
                (coef_hbm, coef_ref),
                (scale_hbm, scale_ref),
            )
        )
    ]
    for load in (own_load, turn_load, *loads):
        load.start()

    def clear(c, carry):
        at = pl.ds(pl.multiple_of(c * 4 * LANES, LANES), 4 * LANES)
        for acc in accs:
            acc[at, :] = jnp.zeros((4 * LANES, LANES), F32)
        return carry

    lax.fori_loop(0, face_len // (2 * LANES), clear, 0)
    gram_acc[...] = jnp.zeros_like(gram_acc)
    turn_load.wait()
    cos, sin = turn_ref[:vecs], turn_ref[8 : 8 + vecs]

    def turned(pair, sign):
        n = pair.shape[1] // LANES
        c = jnp.concatenate([cos] * n, axis=1)
        s = jnp.concatenate([sin] * n, axis=1) * sign
        a, b = pair[:vecs], pair[vecs:]
        return jnp.concatenate([c * a - s * b, s * a + c * b], axis=0)

    unit = (iota((LANES, LANES), 0) == iota((LANES, LANES), 1)).astype(BF16)
    unit = jnp.concatenate([unit, unit], axis=1)

    def put_rows(tile, first):
        top, low = split(tile)
        tiled = jnp.concatenate(
            [jnp.concatenate([top] * copies, axis=0), jnp.concatenate([low] * copies, axis=0)],
            axis=1,
        )
        rows_x[pl.ds(first, LANES), :] = dot_nt(unit, tiled)

    many = 8
    at_last = lax.axis_index("py") == lax.axis_size("py") - 1

    def build_own(c, carry):
        for u in range(many):
            first = pl.multiple_of((c * many + u) * LANES, LANES)
            put_rows(own_ref[:, pl.ds(first, LANES)], first)
        return carry


    def build_face(c, carry):
        for u in range(many // 2):
            first = pl.multiple_of((c * (many // 2) + u) * LANES, LANES)
            put_rows(
                turned(high_x_ref[:, pl.ds(first, LANES)], 1.0),
                pl.multiple_of(owned_len + first, LANES),
            )
            put_rows(
                jnp.where(at_last, 0.0, high_y_ref[:, pl.ds(first, LANES)]),
                pl.multiple_of(owned_len + face_len + first, LANES),
            )
        return carry

    lax.fori_loop(0, face_len // (many // 2 * LANES), build_face, 0)
    own_load.wait()
    lax.fori_loop(0, owned_len // (many * LANES), build_own, 0)

    for load in loads:
        load.wait()

    masks = lane_masks(width, groups)

    def index_of(i, elem):
        return dofs_ref.at[pl.ds(i * capacity, capacity)][elem]

    def face_index_of(i, elem):
        return face_dofs_ref.at[pl.ds(i * face_slots, face_slots)][elem]

    unroll = 4
    steps = BLOCK_ROWS // unroll
    halves = range(0, BLOCK_ROWS, 8)
    part = nloc // steps

    def block(b, gather):
        behind = jnp.maximum(b - 1, 0)
        here = pl.multiple_of(b * block_terms, BLOCK_ROWS)
        there = pl.multiple_of(behind * block_terms, BLOCK_ROWS)
        first_term = pl.multiple_of(behind * block_terms, BLOCK_ROWS)
        first_elem = b * block_elems

        def step(t, c):
            totals = [[None] * len(halves) for _ in range(part)]
            for i in range(nloc):
                if gather:
                    for u in range(unroll):
                        g = t * unroll + u
                        elem = first_elem + g * groups
                        rows = [
                            rows_x[pl.ds(index_of(i, elem + k), 1), :] for k in range(groups)
                        ]
                        gath[pl.ds(here + i * BLOCK_ROWS + g, 1), :] = pick(masks, rows)
                values = [
                    gath[pl.ds(pl.multiple_of(there + i * BLOCK_ROWS + h, 8), 8), :] for h in halves
                ]
                for q in range(part):
                    coef = jnp.broadcast_to(
                        coef_ref[pl.ds((t * part + q) * nloc + i, 1), :], (8, LANES)
                    )
                    for n, value in enumerate(values):
                        product = coef * value
                        totals[q][n] = product if i == 0 else totals[q][n] + product
            for n, h in enumerate(halves):
                scale = scale_ref[pl.ds(pl.multiple_of(behind * BLOCK_ROWS + h, 8), 8), :]
                for q in range(part):
                    at = first_term + (t * part + q) * BLOCK_ROWS + h
                    term_ref[pl.ds(pl.multiple_of(at, 8), 8), :] = totals[q][n] * scale
            return c

        lax.fori_loop(0, steps, step, 0)

    def send(b):
        at = pl.ds(pl.multiple_of(b * block_terms, BLOCK_ROWS), block_terms)
        return pltpu.make_async_copy(term_ref.at[at], term_hbm.at[at], term_sems.at[b])

    def face_block(b, carry):
        add_block(term_ref, accs, face_index_of, index_of, b, 0, nloc, groups)
        return carry

    live = count_ref[0, 0]
    blocks = (live + block_elems - 1) // block_elems
    face_blocks = jnp.minimum(blocks, face_slots // block_elems)

    def full_block(b, carry):
        block(b, True)

        @pl.when(b > 0)
        def _():
            send(b - 1).start()

        return carry

    lax.fori_loop(0, blocks, full_block, 0)
    block(blocks, False)
    send(blocks - 1).start()
    lax.fori_loop(0, face_blocks, face_block, 0)

    deep = DEEP * block_terms
    zero_block = jnp.zeros((block_terms, LANES), F32)
    chunks = (blocks + DEEP - 1) // DEEP

    def blank(b, carry):
        at = pl.ds(pl.multiple_of(b * block_terms, BLOCK_ROWS), block_terms)
        gath[at, :] = zero_block
        term_ref[at, :] = zero_block
        return carry

    lax.fori_loop(blocks, chunks * DEEP, blank, 0)

    def products(c, carry):
        at = pl.ds(pl.multiple_of(c * deep, BLOCK_ROWS), deep)
        left, left_low = split(gath[at, :])
        right, right_low = split(term_ref[at, :])
        over_rows = (((0,), (0,)), ((), ()))
        gram_acc[:, : 2 * LANES] += lax.dot_general(
            left,
            jnp.concatenate([right, right_low], axis=1),
            over_rows,
            preferred_element_type=F32,
        )
        gram_acc[:, 2 * LANES :] += lax.dot_general(
            left_low, right, over_rows, preferred_element_type=F32
        )
        return carry

    lax.fori_loop(0, chunks, products, 0)
    folder = folder_of(width)
    wide = 2 * LANES

    def folded(first):
        at = pl.ds(first, wide)
        total = pick(masks, [acc[at, :] for acc in accs])
        return dot_nt(folder, jnp.concatenate(split(total), axis=1))

    def fold_face(c, carry):
        for u in range(4):
            first = pl.multiple_of((4 * c + u) * wide, wide)
            at = pl.ds(first, wide)
            total = folded(first)
            side_x_ref[:width, at] = turned(total[:width], -1.0)
            side_x_ref[width:, at] = turned(total[width:], -1.0)
            side_y_ref[:, at] = folded(pl.multiple_of(face_len + first, wide))
        return carry

    lax.fori_loop(0, face_len // (4 * wide), fold_face, 0)

    whole = gram_acc[:, :LANES] + gram_acc[:, LANES : 2 * LANES] + gram_acc[:, 2 * LANES :]
    total = whole[:width]
    for k in range(1, groups):
        part = whole[2 * width * k : 2 * width * k + width]
        total = total + pltpu.roll(part, LANES - 2 * width * k, 1)
    re_left, im_left = total[:vecs], total[vecs:]
    lane = iota((vecs, LANES), 1)
    real_here = lane // vecs % 2 == 0
    swapped = jnp.where(
        real_here, pltpu.roll(im_left, LANES - vecs, 1), -pltpu.roll(im_left, vecs, 1)
    )
    joined = re_left + swapped
    for n in range(gram_ref.shape[0]):
        gram_ref[n] = joined

    def sent(b, carry):
        send(b).wait()
        return carry

    lax.fori_loop(0, blocks, sent, 0)


def add_kernel(
    width, nloc, interior, count_ref, table_hbm, term_hbm, curl_hbm, mass_hbm, face_ref,
    dofs_ref, term_ref, images, table_sems, term_sems, out_sems, *accs
):
    owned_len = curl_hbm.shape[1]
    groups = LANES // (2 * width)
    capacity = term_ref.shape[0] // nloc * groups
    block_elems = groups * BLOCK_ROWS
    block_terms = nloc * BLOCK_ROWS
    chunk = capacity // CHUNKS
    size = (nloc + 2) * chunk

    def load(c):
        at = pl.ds(c * size, size)
        return pltpu.make_async_copy(table_hbm.at[at], dofs_ref.at[at], table_sems.at[c])

    for c in range(CHUNKS):
        load(c).start()
    live = count_ref[0, 0]
    blocks = (live + block_elems - 1) // block_elems

    def fetch(b):
        at = pl.ds(pl.multiple_of(b * block_terms, BLOCK_ROWS), block_terms)
        return pltpu.make_async_copy(term_hbm.at[at], term_ref.at[at], term_sems.at[b])

    def fetch_all(b, carry):
        fetch(b).start()
        return carry

    lax.fori_loop(0, blocks, fetch_all, 0)
    many = 4
    zero_tile = jnp.zeros((many * LANES, LANES), F32)

    def clear(c, carry):
        at = pl.ds(pl.multiple_of(c * many * LANES, LANES), many * LANES)
        for acc in accs:
            acc[at, :] = zero_tile
        return carry

    lax.fori_loop(0, owned_len // (many * LANES), clear, 0)

    def index_of(i, elem):
        return dofs_ref.at[pl.ds(i * chunk, CHUNKS * size - i * chunk)][elem]

    def block(c, b):
        fetch(b).wait()
        shift = c * (size - chunk)
        add_block(term_ref, accs, index_of, index_of, b, shift, nloc, groups)

    per_chunk = chunk // block_elems

    def some_blocks(c, carry):
        load(c).wait()

        def one(b, inner):
            block(c, b)
            return inner

        lax.fori_loop(c * per_chunk, jnp.minimum((c + 1) * per_chunk, blocks), one, 0)
        return carry

    lax.fori_loop(0, CHUNKS, some_blocks, 0)

    masks = lane_masks(width, groups)
    folder = folder_of(width)
    wide = 2 * LANES
    many = 4
    span = many * wide

    def fold_some(first, curl, mass):
        for u in range(many):
            at = pl.ds(pl.multiple_of(first + u * wide, wide), wide)
            total = pick(masks, [acc[at, :] for acc in accs])
            total = dot_nt(folder, jnp.concatenate(split(total), axis=1))
            to = slice(u * wide, (u + 1) * wide)
            curl[:, to] = total[:width]
            mass[:, to] = total[width:]

    moves = []
    for c in range(owned_len // span):
        at = pl.ds(c * span, span)
        if c * span < interior:
            fold_some(c * span, images.at[0, :, at], images.at[1, :, at])
            for n, image in enumerate((curl_hbm, mass_hbm)):
                moves.append(
                    pltpu.make_async_copy(
                        images.at[n, :, at], image.at[:, at], out_sems.at[2 * c + n]
                    )
                )
                moves[-1].start()
        else:
            at = pl.ds(c * span - interior, span)
            fold_some(c * span, face_ref.at[0, :, at], face_ref.at[1, :, at])
    for move in moves:
        move.wait()


def finish_kernel(
    width, scale, curl_in, mass_in, face_ref, back_x_ref, back_y_ref, gram_ref,
    curl_out, mass_out, gram_out, faces, sems,
):
    del curl_in, mass_in
    face_len = back_x_ref.shape[1]
    outer = pl.ds(curl_out.shape[1] - 2 * face_len, 2 * face_len)
    moves = []
    at_start = lax.axis_index("py") == 0
    for n, image in enumerate((curl_out, mass_out)):
        rows = slice(n * width, (n + 1) * width)
        faces[n, :, :face_len] = face_ref[n, :, :face_len] + back_x_ref[rows, :]
        faces[n, :, face_len:] = face_ref[n, :, face_len:] + jnp.where(
            at_start, 0.0, back_y_ref[rows, :]
        )
        moves.append(pltpu.make_async_copy(faces.at[n], image.at[:, outer], sems.at[n]))
        moves[-1].start()
    total = gram_ref[0]
    for d in range(1, gram_ref.shape[0]):
        total = total + gram_ref[d]
    total = total * scale
    vecs = total.shape[0]
    for q in range(4):
        shifted = total if q == 0 else pltpu.roll(total, LANES - q * vecs, 1)
        gram_out[q * vecs : (q + 1) * vecs, :] = shifted[:, :vecs]
    for move in moves:
        move.wait()


def on_device(
    trial_block,
    stiff_coef,
    mass_coef,
    elem_count,
    elem_dofs,
    pairing,
    bloch_fraction,
    stiff_ref,
    mass_ref,
):
    own_block = trial_block[0, 0]
    vecs, owned_len = own_block.shape[1:]
    face_len = pairing.shape[0]
    interior = owned_len - 2 * face_len
    width = 2 * vecs
    groups = LANES // (2 * width)
    capacity, nloc = elem_dofs.shape[2:]
    face_slots = capacity // 8
    devices = lax.axis_size("px") * lax.axis_size("py")
    own_rows = own_block.reshape(width, owned_len)
    low_x = own_rows[:, interior : interior + face_len]
    low_y = own_rows[:, interior + face_len :]
    high_x = lax.ppermute(low_x, "px", ring_route("px", -1))
    high_y = lax.ppermute(low_y, "py", ring_route("py", -1))
    live = elem_count
    smem = pl.BlockSpec(memory_space=pltpu.SMEM)
    vmem = pl.BlockSpec(memory_space=pltpu.VMEM)
    left = pl.BlockSpec(memory_space=pl.ANY)

    limit = 62 * 1024 * 1024
    params = pltpu.CompilerParams(vmem_limit_bytes=limit)

    def in_hbm(*values):
        return [pltpu.with_memory_space_constraint(value, pltpu.HBM) for value in values]

    table, own_table, face_table, scale, turn, coef = pl.pallas_call(
        functools.partial(prepare_kernel, owned_len, face_len, width),
        out_shape=(
            jax.ShapeDtypeStruct((nloc + 2, 1, capacity), jnp.int32),
            jax.ShapeDtypeStruct((CHUNKS * (nloc + 2), 1, capacity // CHUNKS), jnp.int32),
            jax.ShapeDtypeStruct((-(-nloc // 8) * 8, face_slots), jnp.int32),
            jax.ShapeDtypeStruct((capacity // groups, LANES), F32),
            jax.ShapeDtypeStruct((16, LANES), F32),
            jax.ShapeDtypeStruct((nloc * nloc, LANES), F32),
        ),
        in_specs=[smem] * 4 + [vmem] * 4,
        out_specs=[vmem] * 5 + [left],
        scratch_shapes=[
            pltpu.VMEM((nloc * nloc, LANES), F32),
            pltpu.SemaphoreType.DMA,
        ],
        compiler_params=params,
        name="prepare",
    )(
        live,
        bloch_fraction,
        stiff_ref,
        mass_ref,
        elem_dofs.transpose(0, 3, 1, 2).reshape(nloc, 1, capacity),
        pairing.reshape(-1, LANES),
        stiff_coef[0],
        mass_coef[0],
    )
    table = table.reshape(-1)
    own_table = own_table.reshape(-1)
    face_table = face_table.reshape(-1)

    extent = owned_len + 2 * face_len
    blocks = capacity // (groups * BLOCK_ROWS)
    term_rows = nloc * capacity // groups
    terms, side_x, side_y, gram = pl.pallas_call(
        functools.partial(term_kernel, width, nloc),
        out_shape=(
            pltpu.HBM((term_rows, LANES), F32),
            jax.ShapeDtypeStruct((2 * width, face_len), F32),
            jax.ShapeDtypeStruct((2 * width, face_len), F32),
            jax.ShapeDtypeStruct((devices, vecs, LANES), F32),
        ),
        in_specs=[smem] + [left] * 6 + [vmem] * 2,
        out_specs=[left] + [vmem] * 3,
        scratch_shapes=[
            pltpu.SMEM(table.shape, jnp.int32),
            pltpu.SMEM(face_table.shape, jnp.int32),
            pltpu.VMEM(turn.shape, F32),
            pltpu.VMEM(own_rows.shape, F32),
            pltpu.VMEM(scale.shape, F32),
            pltpu.VMEM(coef.shape, F32),
            pltpu.VMEM((term_rows, LANES), F32),
            pltpu.VMEM((extent, LANES), F32),
            pltpu.VMEM((term_rows, LANES), F32),
            pltpu.VMEM((LANES, 3 * LANES), F32),
            pltpu.SemaphoreType.DMA((6,)),
            pltpu.SemaphoreType.DMA((blocks,)),
        ]
        + [pltpu.VMEM((2 * face_len + 8, LANES), F32)] * N_ACC,
        compiler_params=pltpu.CompilerParams(vmem_limit_bytes=TERM_MIB * 1024 * 1024),
        name="terms",
    )(live, *in_hbm(table, face_table, turn, own_rows, scale, coef), high_x, high_y)

    back_x = lax.ppermute(side_x, "px", ring_route("px", 1))
    back_y = lax.ppermute(side_y, "py", ring_route("py", 1))
    gathered = lax.all_to_all(gram, ("px", "py"), 0, 0)

    curl, mass, faces = pl.pallas_call(
        functools.partial(add_kernel, width, nloc, interior),
        out_shape=(
            jax.ShapeDtypeStruct((width, owned_len), F32),
            jax.ShapeDtypeStruct((width, owned_len), F32),
            jax.ShapeDtypeStruct((2, width, 2 * face_len), F32),
        ),
        in_specs=[smem, left, left],
        out_specs=[left, left, vmem],
        scratch_shapes=[
            pltpu.SMEM(own_table.shape, jnp.int32),
            pltpu.VMEM((term_rows, LANES), F32),
            pltpu.VMEM((2, width, interior), F32),
            pltpu.SemaphoreType.DMA((CHUNKS,)),
            pltpu.SemaphoreType.DMA((blocks,)),
            pltpu.SemaphoreType.DMA((2 * owned_len // (8 * LANES),)),
        ]
        + [pltpu.VMEM((owned_len + 8, LANES), F32)] * N_ACC,
        compiler_params=pltpu.CompilerParams(vmem_limit_bytes=ADD_MIB * 1024 * 1024),
        cost_estimate=pl.CostEstimate(
            flops=40 * 1024 * 1024 * 1024, bytes_accessed=40 * 1024 * 1024, transcendentals=0
        ),
        name="adds",
    )(live, *in_hbm(own_table, terms))

    curl, mass, gram = pl.pallas_call(
        functools.partial(finish_kernel, width, 1.0 / float(devices * owned_len)),
        out_shape=(
            jax.ShapeDtypeStruct((width, owned_len), F32),
            jax.ShapeDtypeStruct((width, owned_len), F32),
            jax.ShapeDtypeStruct((4 * vecs, vecs), F32),
        ),
        in_specs=[left] * 2 + [vmem] * 4,
        out_specs=[left, left, vmem],
        scratch_shapes=[
            pltpu.VMEM((2, width, 2 * face_len), F32),
            pltpu.SemaphoreType.DMA((2,)),
        ],
        input_output_aliases={0: 0, 1: 1},
        compiler_params=pltpu.CompilerParams(vmem_limit_bytes=8 * 1024 * 1024),
        name="finish",
    )(curl, mass, faces, back_x, back_y, gathered)
    shape = (1, 1, 2, vecs, owned_len)
    return curl.reshape(shape), mass.reshape(shape), gram.reshape(2, 2, vecs, vecs)


def solution(mesh):
    return jax.shard_map(
        on_device,
        mesh=mesh,
        in_specs=(
            P("px", "py", None, None, None),
            P("px", "py", None),
            P("px", "py", None),
            P("px", "py"),
            P("px", "py", None, None),
            P(),
            P(),
            P(),
            P(),
        ),
        out_specs=(P("px", "py", None, None, None), P("px", "py", None, None, None), P()),
        check_vma=False,
    )
```
